32 devices in a mesh: grp: 2 (over x), tmpl: 16 (over z, y, core).
Axes of the slice: x: 2, y: 2, z: 4, core: 2. Of those that a mesh axis runs over, the one named last changes fastest.
Arguments:
- strain: float32 [16, 512, 1024], P('grp', None, 'tmpl'), parts along dimension 0, may hold values from -6 to 6
- analysis: float32 [1024, 1024], P('grp', 'tmpl'), parts along dimension 0, may hold values from -6 to 6
- bank: bfloat16 [2, 16, 512, 512], P(None, None, 'tmpl'), may hold values from -6 to 6
- cutoff: int32 [16], replicated, may hold values from 65536 to 262144
- order: int32 [16], replicated, may hold values from 0 to 15, each once
Outputs:
- snr: bfloat16 [32, 512, 1024], P(('grp', 'tmpl')), parts along dimension 0
The draws below stay inside these ranges and needn't reach their ends.
There are 2 independent parts, one for each index of `grp`. The reference program is written for one: setup_inputs(seed, part) draws one part's arguments, and reference() takes and returns one part's arrays. A program takes and returns all parts, laid end to end along the dimension named above; an argument that names none is the same for every part. Nothing has to cross between parts.
Inputs may be any that keep to these rules, and one draw needn't show every extreme that they name: `order`: a permutation of the bank's templates.
All inputs are finite; a program needn't handle non-finite values.
Results may differ from the reference program's by a relative error of at most 0.013.
Values may be sent and summed in bfloat16 or wider, within the bound.
No kernel may reach another device: no remote copies, remote signals or barrier semaphores. Data moves between devices by JAX's collectives and lax.ppermute only.
A program may use at most 64 MiB of HBM per device.

```python
import math
import jax
import jax.numpy as jnp
from jax import lax

N1 = 512
N2 = 1024
SEGS = 8
SAMPLES = 524288
TEMPLATES = 16


def plant(result, own_key, least, top_value):
    spot = [jax.random.randint(jax.random.fold_in(own_key, axis), (), 0, length) for axis, length in enumerate(result.shape)]
    longest = result.shape.index(max(result.shape))
    next_to = spot[:longest] + [(spot[longest] + 1) % result.shape[longest]] + spot[longest + 1:]
    return result.at[tuple(spot)].set(least).at[tuple(next_to)].set(top_value)


def steps_of(key, dims, cuts, least, high):
    level, own = 1.0, jax.random.fold_in(key, 6)
    for axis_at, blocks in cuts:
        steps = jnp.exp(jax.random.uniform(jax.random.fold_in(own, axis_at), (blocks,), jnp.float32, least / len(cuts), high / len(cuts)))
        level = level * jnp.repeat(steps, dims[axis_at] // blocks).reshape([-1 if axis == axis_at else 1 for axis in range(len(dims))])
    return level


def normal_values(stream_key, shape, scale, limit, shards=(), kind=jnp.bfloat16):
    loudness = steps_of(stream_key, shape, shards, -0.22, 0.18) if shards else 1.0
    drawn = jax.random.normal(stream_key, shape, jnp.float32) * scale * loudness
    return jnp.minimum(jnp.maximum(drawn, -limit), limit).astype(kind)


def setup_inputs(seed: int = 0, part: int = 0) -> dict:
    streams_of = jax.random.split(jax.random.key(seed), 6)
    part_splits = jax.random.split(jax.random.fold_in(streams_of[5], part), 6)
    return {
        "strain": normal_values(part_splits[0], (SEGS, N1, N2), 1.0, 6.0, ((2, 16),), jnp.float32),
        "analysis": normal_values(part_splits[1], (N1, N2), 1.0, 6.0, ((1, 16),), jnp.float32),
        "bank": normal_values(streams_of[2], (2, TEMPLATES, N1, N2 // 2), 1.0, 6.0, ((2, 16),)),
        "cutoff": plant(jax.random.randint(streams_of[3], (TEMPLATES,), SAMPLES // 8, SAMPLES // 2 + 1), jax.random.fold_in(streams_of[3], 1), SAMPLES // 8, (SAMPLES // 2 + 1) - 1).astype(jnp.int32),
        "order": jax.random.permutation(streams_of[4], TEMPLATES).astype(jnp.int32),
    }


def angles(left_idx, right_idx, period):
    product = left_idx[:, None] * right_idx[None, :] % period
    phase_angle = product.astype(jnp.float32) * (2.0 * math.pi / period)
    return (jnp.cos(phase_angle), jnp.sin(phase_angle))

def round_trip(values):
    narrow = lax.optimization_barrier(values.astype(jnp.bfloat16))
    return narrow.astype(jnp.float32)

def reference(strain, analysis, bank, cutoff, order):
    length = N1 * N2
    half_len = N2 // 2
    sample_idx = jnp.arange(length, dtype=jnp.int32)
    window = math.sqrt(8.0 / 3.0) * jnp.sin(sample_idx.astype(jnp.float32) * (math.pi / length)) ** 2
    series = jnp.concatenate([strain.reshape(SEGS, length) * window, analysis.reshape(1, length)], 0)
    spectra = jnp.fft.fft(series, axis=1).reshape(SEGS + 1, N2, N1)[:, :half_len, :].transpose(0, 2, 1)
    spec_real = jnp.real(spectra).astype(jnp.float32)
    spec_imag = jnp.imag(spectra).astype(jnp.float32)
    power_spec = jnp.maximum(lax.optimization_barrier(jnp.mean(spec_real[:SEGS] ** 2 + spec_imag[:SEGS] ** 2, axis=0)), 0.2 * length)
    white_real = round_trip(spec_real[SEGS] / power_spec)
    white_imag = round_trip(spec_imag[SEGS] / power_spec)
    freq_bin = jnp.arange(N1, dtype=jnp.int32)[:, None] + N1 * jnp.arange(half_len, dtype=jnp.int32)[None, :]
    chosen = jnp.take(bank, order, axis=1).transpose(1, 0, 2, 3)
    cuts = jnp.take(cutoff, order)
    cos_twist, sin_twist = angles(jnp.arange(N1, dtype=jnp.int32), jnp.arange(N2, dtype=jnp.int32), length)

    def one_template(item):
        pair, cut_bin = item
        tmpl_real = pair[0].astype(jnp.float32)
        tmpl_imag = pair[1].astype(jnp.float32)
        in_band = freq_bin < cut_bin
        norm_sq = jnp.sum(jnp.where(in_band, (tmpl_real ** 2 + tmpl_imag ** 2) / power_spec, 0.0))
        filt_real = round_trip(jnp.where(in_band, white_real * tmpl_real + white_imag * tmpl_imag, 0.0))
        filt_imag = round_trip(jnp.where(in_band, white_imag * tmpl_real - white_real * tmpl_imag, 0.0))
        padded = jnp.pad(filt_real + 1j * filt_imag, ((0, 0), (0, N2 - half_len)))
        spread = N2 * jnp.fft.ifft(padded, axis=1)
        spread_real = jnp.real(spread)
        spread_imag = jnp.imag(spread)
        lift_real = round_trip(spread_real * cos_twist - spread_imag * sin_twist)
        lift_imag = round_trip(spread_real * sin_twist + spread_imag * cos_twist)
        field = N1 * jnp.fft.ifft(lift_real + 1j * lift_imag, axis=0)
        return (jnp.abs(field) / jnp.sqrt(norm_sq)).astype(jnp.bfloat16)
    return lax.map(one_template, (chosen, cuts))
```

```python
import functools
import math

import jax
import jax.numpy as jnp
import numpy as np
from jax import lax
from jax.experimental import pallas as pl
from jax.experimental.pallas import tpu as pltpu
from jax.sharding import PartitionSpec as P

BF16 = jnp.bfloat16
F32 = jnp.float32
STEP = 16


def turns(product, period):
    angle = (product % period) * (2.0 * math.pi / period)
    return np.cos(angle).astype(np.float32), np.sin(angle).astype(np.float32)


def matmul(left, right):
    return jnp.dot(left, right, preferred_element_type=F32)


def vmem(shape, dtype):
    return pltpu.VMEM(shape, dtype)


def whole():
    return pl.BlockSpec(memory_space=pltpu.VMEM)


def stage_one_kernel(segs, cols, lanes, strain, analysis, window, cos, sin, out, packed):
    tail = segs * cols
    for seg in range(segs):
        packed[:, seg * cols : (seg + 1) * cols] = (strain[seg] * window[...]).astype(BF16)
    last = analysis[...].astype(BF16)
    packed[:, tail : tail + cols] = last
    packed[:, tail + cols :] = jnp.zeros_like(packed[:, tail + cols :])
    first_len = cos.shape[0]
    block = first_len // 4

    def rows(step, carry):
        at = pl.ds(pl.multiple_of(step * block, block), block)
        real = matmul(cos[at, :], packed[...])
        imag = -matmul(sin[at, :], packed[...])
        out[at, 0:tail] = real[:, :tail].astype(BF16)
        out[at, tail : 2 * tail] = imag[:, :tail].astype(BF16)
        joined = jnp.concatenate([real[:, tail : tail + cols], imag[:, tail : tail + cols]], 1)
        out[at, 2 * tail :] = joined.astype(BF16)
        return carry

    lax.fori_loop(0, 4, rows, 0)


def tables_kernel(
    place, full_c, full_s, full_rc, full_rs, col_c, col_s, col_rc, col_rs,
    lift_c, lift_s, lift_rc, lift_rs, base_c, base_s,
    forward, rows_out, cols_out, lift_out_c, lift_out_s, near_c, near_s,
):
    second_len = full_c.shape[1]
    half_len = second_len // 2
    first_len = col_c.shape[1]

    def turn(cos, sin, by_cos, by_sin):
        return cos * by_cos - sin * by_sin, sin * by_cos + cos * by_sin

    def at(step):
        return pl.ds(pl.multiple_of(step * STEP, STEP), STEP)

    def store_forward(step, cos, sin):
        forward[at(step), 0:half_len] = cos[:, :half_len].astype(BF16)
        forward[at(step), half_len:] = sin[:, :half_len].astype(BF16)

    def upper(step, carry):
        cos, sin = carry
        store_forward(step, cos, sin)
        rows_out[at(step), 0:second_len] = cos.astype(BF16)
        rows_out[at(step), second_len:] = sin.astype(BF16)
        return turn(cos, sin, full_rc[...], full_rs[...])

    cos, sin = lax.fori_loop(0, half_len // STEP, upper, (full_c[...], full_s[...]))

    def lower(step, carry):
        cos, sin = carry
        store_forward(step, cos, sin)
        return turn(cos, sin, full_rc[:, :half_len], full_rs[:, :half_len])

    lax.fori_loop(
        half_len // STEP, second_len // STEP, lower, (cos[:, :half_len], sin[:, :half_len])
    )

    def columns(step, carry):
        cos, sin = carry
        cols_out[at(step), 0:first_len] = cos.astype(BF16)
        cols_out[at(step), first_len:] = sin.astype(BF16)
        return turn(cos, sin, col_rc[...], col_rs[...])

    lax.fori_loop(0, first_len // STEP, columns, (col_c[...], col_s[...]))

    def lifts(step, carry):
        cos, sin = carry
        lift_out_c[at(step), :] = cos.astype(BF16)
        lift_out_s[at(step), :] = sin.astype(BF16)
        return turn(cos, sin, lift_rc[...], lift_rs[...])

    lax.fori_loop(0, first_len // STEP, lifts, (lift_c[...], lift_s[...]))

    mine = pl.ds(place[0], 1)
    by_cos, by_sin = base_c[mine, :], base_s[mine, :]
    cos, sin = lift_c[...], lift_s[...]
    for step in range(near_c.shape[0] // STEP):
        near = pl.ds(step * STEP, STEP)
        near_c[near, :], near_s[near, :] = turn(cos, sin, by_cos, by_sin)
        cos, sin = turn(cos, sin, lift_rc[...], lift_rs[...])


def choose_kernel(first_len, order, cuts, place, bank, chosen, power):
    template = order[pl.program_id(0)]
    shape = bank.shape[2:]
    row = place[0] * shape[0] + lax.broadcasted_iota(jnp.int32, shape, 0)
    freq_bin = row + first_len * lax.broadcasted_iota(jnp.int32, shape, 1)
    in_band = freq_bin < cuts[template]
    real = jnp.where(in_band, bank[0, 0].astype(F32), 0.0)
    imag = jnp.where(in_band, bank[1, 0].astype(F32), 0.0)
    chosen[0, 0] = real.astype(BF16)
    chosen[0, 1] = imag.astype(BF16)
    power[0] = real * real + imag * imag


def stage_two_kernel(
    segs, moved, near_c, near_s, forward_hbm, chosen_hbm, power_hbm, out,
    forward, chosen, power, stacked, sems,
):
    copies = [
        pltpu.make_async_copy(forward_hbm, forward, sems.at[0]),
        pltpu.make_async_copy(chosen_hbm, chosen, sems.at[1]),
        pltpu.make_async_copy(power_hbm, power, sems.at[2]),
    ]
    for copy in copies:
        copy.start()
    sources, rows, _ = moved.shape
    second_len = forward.shape[0]
    half_len = second_len // 2
    cols = second_len // sources
    tail = segs * cols
    all_rows = (segs + 1) * rows
    low = lax.broadcasted_iota(jnp.int32, (rows, 2 * cols), 1) < cols

    def pair(left, right):
        return (
            jnp.where(low, left, pltpu.roll(right, cols, 1)),
            jnp.where(low, pltpu.roll(left, cols, 1), right),
        )

    for tile in range(sources // 2):
        lane = slice(tile * 2 * cols, (tile + 1) * 2 * cols)
        cos, sin = near_c[:, lane], near_s[:, lane]

        def piece(lo, tile=tile):
            hi = lo + 2 * cols
            return pair(
                moved[2 * tile, :, lo:hi].astype(F32), moved[2 * tile + 1, :, lo:hi].astype(F32)
            )

        def put(seg, real, imag, lane=lane, cos=cos, sin=sin):
            at = seg * rows
            stacked[at : at + rows, lane] = (real * cos + imag * sin).astype(BF16)
            at += all_rows
            stacked[at : at + rows, lane] = (imag * cos - real * sin).astype(BF16)

        for twin in range(segs // 2):
            real_one, real_two = piece(twin * 2 * cols)
            imag_one, imag_two = piece(tail + twin * 2 * cols)
            put(2 * twin, real_one, imag_one)
            put(2 * twin + 1, real_two, imag_two)
        real, imag = piece(2 * tail)
        put(segs, real, imag)

    copies[0].wait()
    real_part, imag_part = slice(0, half_len), slice(half_len, 2 * half_len)

    def spectrum(seg):
        upper = matmul(stacked[pl.ds(seg * rows, rows), :], forward[...])
        lower = matmul(stacked[pl.ds(all_rows + seg * rows, rows), :], forward[...])
        return (
            upper[:, real_part] + lower[:, imag_part],
            lower[:, real_part] - upper[:, imag_part],
        )

    level = jnp.zeros((rows, half_len), F32)
    for seg in range(segs):
        real, imag = spectrum(seg)
        level = level + (real * real + imag * imag)
    length = second_len * sources * rows
    level = jnp.maximum(level * (1.0 / segs), 0.2 * length)
    weight = 1.0 / level
    real, imag = spectrum(segs)
    white_real = (real / level).astype(BF16).astype(F32)
    white_imag = (imag / level).astype(BF16).astype(F32)
    copies[1].wait()
    copies[2].wait()
    blocks = half_len // 128

    def one_template(row, carry):
        tmpl_real = chosen[row, 0].astype(F32)
        tmpl_imag = chosen[row, 1].astype(F32)
        filt_real = (white_real * tmpl_real + white_imag * tmpl_imag).astype(BF16)
        filt_imag = (white_imag * tmpl_real - white_real * tmpl_imag).astype(BF16)
        for block in range(blocks):
            lane = slice(block * 128, (block + 1) * 128)
            out[row, block * rows : (block + 1) * rows, :] = filt_real[:, lane]
            out[row, (blocks + block) * rows : (blocks + block + 1) * rows, :] = filt_imag[:, lane]
        norm = jnp.sum(power[row] * weight, keepdims=True)
        high = norm.astype(BF16).astype(F32)
        middle = (norm - high).astype(BF16).astype(F32)
        lowest = norm - high - middle
        line = lax.broadcasted_iota(jnp.int32, (16, 128), 1)
        terms = jnp.where(line == 0, high, jnp.where(line == 1, middle, lowest))
        out[row, 2 * blocks * rows :, :] = terms.astype(BF16)
        return carry

    lax.fori_loop(0, chosen.shape[0], one_template, 0)


def inverse_kernel(
    moved, rows_hbm, cols_hbm, lift_c_hbm, lift_s_hbm, out,
    rows_table, cols_table, lift_c, lift_s, spread, lifted, sems,
):
    copies = [
        pltpu.make_async_copy(rows_hbm, rows_table, sems.at[0]),
        pltpu.make_async_copy(lift_c_hbm, lift_c, sems.at[1]),
        pltpu.make_async_copy(lift_s_hbm, lift_s, sems.at[2]),
        pltpu.make_async_copy(cols_hbm, cols_table, sems.at[3]),
    ]
    for copy in copies:
        copy.start()
    half_len, second_len = rows_table.shape[0], lift_c.shape[1]
    first_len = cols_table.shape[0]
    sources = moved.shape[0]
    rows = first_len // sources
    blocks = half_len // 128
    for source in range(sources):
        for block in range(2 * blocks):
            lane = slice(block * 128, (block + 1) * 128)
            spread[source * rows : (source + 1) * rows, lane] = moved[
                source, block * rows : (block + 1) * rows, :
            ]
    terms = moved[:, 2 * blocks * rows, :].astype(F32)
    line = lax.broadcasted_iota(jnp.int32, terms.shape, 1)
    norm = jnp.sum(jnp.where(line < 3, terms, 0.0), keepdims=True)
    scale = lax.rsqrt(norm)
    for copy in copies[:3]:
        copy.wait()
    deep = 128

    def lift(step, carry):
        at = pl.ds(pl.multiple_of(step * deep, deep), deep)
        real, imag = spread[at, :half_len], spread[at, half_len:]
        wide = 512
        for lane in range(0, second_len, wide):
            cos_at, sin_at = slice(lane, lane + wide), slice(second_len + lane, second_len + lane + wide)
            cos, sin = rows_table[:, cos_at], rows_table[:, sin_at]
            spread_real = matmul(real, cos) - matmul(imag, sin)
            spread_imag = matmul(real, sin) + matmul(imag, cos)
            turn_c, turn_s = lift_c[at, cos_at].astype(F32), lift_s[at, cos_at].astype(F32)
            lifted[at, cos_at] = (spread_real * turn_c - spread_imag * turn_s).astype(BF16)
            lifted[at, sin_at] = (spread_real * turn_s + spread_imag * turn_c).astype(BF16)
        return carry

    lax.fori_loop(0, first_len // deep, lift, 0)
    copies[3].wait()

    def field(step, carry):
        at = pl.ds(pl.multiple_of(step * deep, deep), deep)
        cos, sin = cols_table[at, :first_len], cols_table[at, first_len:]
        wide = 512
        for lane in range(0, second_len, wide):
            real, imag = lifted[:, lane : lane + wide], lifted[:, second_len + lane : second_len + lane + wide]
            field_real = matmul(cos, real) - matmul(sin, imag)
            field_imag = matmul(sin, real) + matmul(cos, imag)
            power = field_real * field_real + field_imag * field_imag
            out[0, at, lane : lane + wide] = (jnp.sqrt(power) * scale).astype(BF16)
        return carry

    lax.fori_loop(0, first_len // deep, field, 0)


def tiled_local(strain, analysis, bank, cutoff, order):
    dev_count = lax.axis_size("tmpl")
    my_index = lax.axis_index("tmpl")
    segs, first_len, cols = strain.shape
    second_len = cols * dev_count
    length = first_len * second_len
    half_len = second_len // 2
    rows = first_len // dev_count
    templates = order.shape[0]
    lanes = 2 * (segs + 1) * cols
    place = jnp.reshape(my_index, (1,)).astype(jnp.int32)

    first = np.arange(first_len)
    second = np.arange(second_len)
    step = np.arange(STEP)
    row_c, row_s = turns(first[:, None] * second_len, length)
    col_c, col_s = turns(np.arange(second_len).reshape(dev_count, cols), length)
    mine_c = lax.dynamic_slice_in_dim(jnp.asarray(col_c), my_index, 1)
    mine_s = lax.dynamic_slice_in_dim(jnp.asarray(col_s), my_index, 1)
    window = (0.5 * math.sqrt(8.0 / 3.0)) * (1.0 - (row_c * mine_c - row_s * mine_s))
    one_c, one_s = turns(first[:, None] * first[None, :], first_len)

    packed_lanes = -(-(segs + 1) * cols // 128) * 128
    send = pl.pallas_call(
        functools.partial(stage_one_kernel, segs, cols, lanes),
        out_shape=jax.ShapeDtypeStruct((first_len, lanes), BF16),
        in_specs=[whole()] * 5,
        out_specs=whole(),
        scratch_shapes=[vmem((first_len, packed_lanes), BF16)],
        name="stage_one",
    )(strain, analysis, window, jnp.asarray(one_c, BF16), jnp.asarray(one_s, BF16))
    moved = lax.all_to_all(
        send.reshape(dev_count, rows, lanes), "tmpl", split_axis=0, concat_axis=0, tiled=True
    )

    consts = [
        *turns(step[:, None] * second[None, :], second_len),
        *turns(STEP * second[None, :], second_len),
        *turns(step[:, None] * first[None, :], first_len),
        *turns(STEP * first[None, :], first_len),
        *turns(step[:, None] * second[None, :], length),
        *turns(STEP * second[None, :], length),
        *turns((rows * np.arange(dev_count))[:, None] * second[None, :], length),
    ]
    shapes = [
        ((second_len, second_len), BF16),
        ((half_len, 2 * second_len), BF16),
        ((first_len, 2 * first_len), BF16),
        ((first_len, second_len), BF16),
        ((first_len, second_len), BF16),
        ((rows, second_len), F32),
        ((rows, second_len), F32),
    ]
    forward, rows_table, cols_table, lift_c, lift_s, near_c, near_s = pl.pallas_call(
        tables_kernel,
        out_shape=[jax.ShapeDtypeStruct(*shape) for shape in shapes],
        in_specs=[pl.BlockSpec(memory_space=pltpu.SMEM)] + [whole()] * len(consts),
        out_specs=[whole()] * len(shapes),
        cost_estimate=pl.CostEstimate(flops=10**7, bytes_accessed=2 * 10**7, transcendentals=0),
        name="tables",
    )(place, *[jnp.asarray(table) for table in consts])

    chosen, power = pl.pallas_call(
        functools.partial(choose_kernel, first_len),
        grid_spec=pltpu.PrefetchScalarGridSpec(
            num_scalar_prefetch=3,
            grid=(templates,),
            in_specs=[
                pl.BlockSpec((2, 1, rows, half_len), lambda at, order, cuts, place: (0, order[at], 0, 0))
            ],
            out_specs=[
                pl.BlockSpec((1, 2, rows, half_len), lambda at, *_: (at, 0, 0, 0)),
                pl.BlockSpec((1, rows, half_len), lambda at, *_: (at, 0, 0)),
            ],
        ),
        out_shape=[
            jax.ShapeDtypeStruct((templates, 2, rows, half_len), BF16),
            jax.ShapeDtypeStruct((templates, rows, half_len), F32),
        ],
        cost_estimate=pl.CostEstimate(flops=10**7, bytes_accessed=5 * 10**6, transcendentals=0),
        name="choose",
    )(order, cutoff, place, bank)

    any_space = pl.BlockSpec(memory_space=pl.ANY)
    sent_rows = 2 * half_len // 128 * rows + 16
    filtered_rows = pl.pallas_call(
        functools.partial(stage_two_kernel, segs),
        out_shape=jax.ShapeDtypeStruct((templates, sent_rows, 128), BF16),
        in_specs=[whole()] * 3 + [any_space] * 3,
        out_specs=whole(),
        scratch_shapes=[
            vmem(forward.shape, BF16),
            vmem(chosen.shape, BF16),
            vmem(power.shape, F32),
            vmem((2 * (segs + 1) * rows, second_len), BF16),
            pltpu.SemaphoreType.DMA((3,)),
        ],
        name="stage_two",
    )(moved, near_c, near_s, forward, chosen, power)
    gathered = lax.all_to_all(filtered_rows, "tmpl", split_axis=0, concat_axis=0, tiled=True)
    return pl.pallas_call(
        inverse_kernel,
        out_shape=jax.ShapeDtypeStruct((1, first_len, second_len), BF16),
        in_specs=[whole()] + [any_space] * 4,
        out_specs=whole(),
        scratch_shapes=[
            vmem(rows_table.shape, BF16),
            vmem(cols_table.shape, BF16),
            vmem(lift_c.shape, BF16),
            vmem(lift_s.shape, BF16),
            vmem((first_len, 2 * half_len), BF16),
            vmem((first_len, 2 * second_len), BF16),
            pltpu.SemaphoreType.DMA((4,)),
        ],
        name="inverse",
    )(gathered, rows_table, cols_table, lift_c, lift_s)


def angles(left_idx, right_idx, period):
    product = left_idx[:, None] * right_idx[None, :] % period
    phase_angle = product.astype(jnp.float32) * (2.0 * math.pi / period)
    return (jnp.cos(phase_angle), jnp.sin(phase_angle))


def filtered(white_pair, tmpl_pair, cut_bins, freq_bin):
    white_real = white_pair[0].astype(jnp.float32)
    white_imag = white_pair[1].astype(jnp.float32)
    tmpl_real = tmpl_pair[0].astype(jnp.float32)
    tmpl_imag = tmpl_pair[1].astype(jnp.float32)
    in_band = freq_bin[None] < cut_bins[:, None, None]
    filt_real = jnp.where(in_band, white_real * tmpl_real + white_imag * tmpl_imag, 0.0)
    filt_imag = jnp.where(in_band, white_imag * tmpl_real - white_real * tmpl_imag, 0.0)
    return jnp.concatenate([filt_real, filt_imag], -1).astype(jnp.bfloat16)


def inverse_rows(stacked, row_bins, second_len, length):
    half_len = second_len // 2
    cosine, sine = angles(
        jnp.arange(half_len, dtype=jnp.int32), jnp.arange(second_len, dtype=jnp.int32), second_len
    )
    dft_table = jnp.concatenate(
        [jnp.concatenate([cosine, sine], 1), jnp.concatenate([-sine, cosine], 1)], 0
    ).astype(jnp.bfloat16)
    spread = jnp.einsum("tkf,fg->tkg", stacked, dft_table, preferred_element_type=jnp.float32)
    spread_real = spread[..., :second_len]
    spread_imag = spread[..., second_len:]
    cos_twist, sin_twist = angles(row_bins, jnp.arange(second_len, dtype=jnp.int32), length)
    lift_real = spread_real * cos_twist - spread_imag * sin_twist
    lift_imag = spread_real * sin_twist + spread_imag * cos_twist
    return jnp.concatenate([lift_real, lift_imag], -1).astype(jnp.bfloat16)


def inverse_cols(lifted, first_len, second_len):
    row_idx = jnp.arange(first_len, dtype=jnp.int32)
    cosine, sine = angles(row_idx, row_idx, first_len)
    cosine = cosine.astype(jnp.bfloat16)
    sine = sine.astype(jnp.bfloat16)
    lift_real = lifted[..., :second_len]
    lift_imag = lifted[..., second_len:]
    field_real = jnp.einsum(
        "ak,tkb->tab", cosine, lift_real, preferred_element_type=jnp.float32
    ) - jnp.einsum("ak,tkb->tab", sine, lift_imag, preferred_element_type=jnp.float32)
    field_imag = jnp.einsum(
        "ak,tkb->tab", sine, lift_real, preferred_element_type=jnp.float32
    ) + jnp.einsum("ak,tkb->tab", cosine, lift_imag, preferred_element_type=jnp.float32)
    return (field_real, field_imag)


def plain_local(strain, analysis, bank, cutoff, order):
    highest = lax.Precision.HIGHEST
    dev_count = lax.axis_size("tmpl")
    my_index = lax.axis_index("tmpl")
    seg_count = strain.shape[0]
    first_len = strain.shape[1]
    col_count = strain.shape[2]
    second_len = col_count * dev_count
    length = first_len * second_len
    half_len = second_len // 2
    row_count = first_len // dev_count
    row_idx = jnp.arange(first_len, dtype=jnp.int32)
    col_index = my_index * col_count + jnp.arange(col_count, dtype=jnp.int32)
    sample_idx = row_idx[:, None] * second_len + col_index[None, :]
    window = (
        math.sqrt(8.0 / 3.0) * jnp.sin(sample_idx.astype(jnp.float32) * (math.pi / length)) ** 2
    )
    series = jnp.concatenate([strain * window, analysis[None]], 0)
    cos_one, sin_one = angles(row_idx, row_idx, first_len)
    part_real = jnp.einsum("ka,sab->skb", cos_one, series, precision=highest)
    part_imag = -jnp.einsum("ka,sab->skb", sin_one, series, precision=highest)
    cos_twist, sin_twist = angles(row_idx, col_index, length)
    twist_real = part_real * cos_twist + part_imag * sin_twist
    twist_imag = part_imag * cos_twist - part_real * sin_twist
    moved = lax.all_to_all(
        jnp.stack([twist_real, twist_imag]).astype(jnp.bfloat16),
        "tmpl",
        split_axis=2,
        concat_axis=3,
        tiled=True,
    ).astype(jnp.float32)
    cos_two, sin_two = angles(
        jnp.arange(second_len, dtype=jnp.int32), jnp.arange(half_len, dtype=jnp.int32), second_len
    )
    spec_real = jnp.einsum("skb,bf->skf", moved[0], cos_two, precision=highest) + jnp.einsum(
        "skb,bf->skf", moved[1], sin_two, precision=highest
    )
    spec_imag = jnp.einsum("skb,bf->skf", moved[1], cos_two, precision=highest) - jnp.einsum(
        "skb,bf->skf", moved[0], sin_two, precision=highest
    )
    power_spec = jnp.maximum(
        jnp.mean(spec_real[:seg_count] ** 2 + spec_imag[:seg_count] ** 2, axis=0), 0.2 * length
    )
    whitened = jnp.stack(
        [spec_real[seg_count] / power_spec, spec_imag[seg_count] / power_spec]
    ).astype(jnp.bfloat16)
    own_rows = my_index * row_count + jnp.arange(row_count, dtype=jnp.int32)
    half_idx = jnp.arange(half_len, dtype=jnp.int32)
    freq_local = own_rows[:, None] + first_len * half_idx[None, :]
    chosen = jnp.take(bank, order, axis=1)
    cuts = jnp.take(cutoff, order)
    bank_real = chosen[0].astype(jnp.float32)
    bank_imag = chosen[1].astype(jnp.float32)
    in_band = freq_local[None] < cuts[:, None, None]
    local_norm = jnp.sum(
        jnp.where(in_band, (bank_real**2 + bank_imag**2) / power_spec, 0.0), axis=(1, 2)
    )
    norm_sq = lax.psum(local_norm, "tmpl")
    per_device = cuts.shape[0] // dev_count
    own_norm = lax.dynamic_slice_in_dim(norm_sq, my_index * per_device, per_device)
    stacked = filtered(whitened, chosen, cuts, freq_local)
    lifted = lax.all_to_all(
        inverse_rows(stacked, own_rows, second_len, length),
        "tmpl",
        split_axis=0,
        concat_axis=1,
        tiled=True,
    )
    field_real, field_imag = inverse_cols(lifted, first_len, second_len)
    magnitude = jnp.sqrt(field_real**2 + field_imag**2)
    return (magnitude / jnp.sqrt(own_norm)[:, None, None]).astype(jnp.bfloat16)


def local(strain, analysis, bank, cutoff, order):
    dev_count = lax.axis_size("tmpl")
    rows = strain.shape[1] // dev_count
    half_len = strain.shape[2] * dev_count // 2
    tiles = rows % 16 == 0 and strain.shape[2] == 64 and half_len % 512 == 0
    if tiles and order.shape[0] == dev_count and strain.shape[0] % 2 == 0 and dev_count % 2 == 0:
        return tiled_local(strain, analysis, bank, cutoff, order)
    return plain_local(strain, analysis, bank, cutoff, order)


def solution(mesh):
    return jax.shard_map(
        local,
        mesh=mesh,
        in_specs=(P("grp", None, "tmpl"), P("grp", "tmpl"), P(None, None, "tmpl", None), P(), P()),
        out_specs=P(("grp", "tmpl"), None, None),
        check_vma=False,
    )
```

```python
import functools
import math

import jax
import jax.numpy as jnp
import numpy as np
from jax import lax
from jax.experimental import pallas as pl
from jax.experimental.pallas import tpu as pltpu
from jax.sharding import PartitionSpec as P

BF16 = jnp.bfloat16
F32 = jnp.float32
STEP = 16
NEAR = (0, 2, 4, 12, 6, 14, 8, 10)


def turns(product, period):
    angle = (product % period) * (2.0 * math.pi / period)
    return np.cos(angle).astype(np.float32), np.sin(angle).astype(np.float32)


def matmul(left, right):
    return jnp.dot(left, right, preferred_element_type=F32)


def matmul_nt(left, right):
    return lax.dot_general(left, right, (((1,), (1,)), ((), ())), preferred_element_type=F32)


def vmem(shape, dtype=BF16):
    return pltpu.VMEM(shape, dtype)


def whole():
    return pl.BlockSpec(memory_space=pltpu.VMEM)


def scalars():
    return pl.BlockSpec(memory_space=pltpu.SMEM)


def params(mib):
    return pltpu.CompilerParams(vmem_limit_bytes=mib << 20)


def halves(count):
    return np.concatenate([np.arange(0, count, 2), np.arange(1, count, 2)])


def aligned(start, size):
    return pl.ds(pl.multiple_of(start, size), size)


def stage_one_kernel(
    place, order, spin, strain, analysis, win_c, win_s, cos, sin, bank, out, packed, sems
):
    segs, cols, _ = strain.shape
    tail = segs * cols
    templates, half_len = bank.shape[1], bank.shape[3]
    rows = out.shape[0] // templates
    first_row = place[1] * rows
    copies = []
    for row in range(templates):
        for part in range(2):
            copies.append(
                pltpu.make_async_copy(
                    bank.at[part, order[row], aligned(first_row, rows), :],
                    out.at[
                        row * rows : (row + 1) * rows,
                        2 * (tail + cols) + part * half_len : 2 * (tail + cols) + (part + 1) * half_len,
                    ],
                    sems.at[2 * row + part],
                )
            )
            copies[-1].start()
    by_cos, by_sin = spin[place[0], 0], spin[place[0], 1]
    scale = 0.5 * math.sqrt(8.0 / 3.0)
    window = scale - scale * (win_c[...] * by_cos - win_s[...] * by_sin)
    for seg in range(segs):
        packed[seg * cols : (seg + 1) * cols, :] = (strain[seg] * window).astype(BF16)
    packed[tail:, :] = analysis[...].astype(BF16)
    real = matmul_nt(cos[...], packed[...])
    imag = -matmul_nt(sin[...], packed[...])
    out[:, 0:tail] = real[:, :tail].astype(BF16)
    out[:, tail : 2 * tail] = imag[:, :tail].astype(BF16)
    joined = jnp.concatenate([real[:, tail:], imag[:, tail:]], 1)
    out[:, 2 * tail : 2 * (tail + cols)] = joined.astype(BF16)
    for copy in copies:
        copy.wait()


def tables_kernel(
    fore_c, fore_s, fore_rc, fore_rs, even_c, even_s, odd_c, odd_s, rows_rc, rows_rs,
    lift_c, lift_s, lift_rc, lift_rs, mid_c, mid_s,
    forward, even_out, odd_out, lift_out_c, lift_out_s,
):
    half_len = fore_c.shape[1]
    second_len = 2 * half_len

    def turn(cos, sin, by_cos, by_sin):
        return cos * by_cos - sin * by_sin, sin * by_cos + cos * by_sin

    first_lane = lax.broadcasted_iota(jnp.int32, fore_c.shape, 1) == 0
    sign = 1.0 - 2.0 * (lax.broadcasted_iota(jnp.int32, fore_c.shape, 0) % 2).astype(F32)

    def fore(step, carry):
        cos, sin = carry
        forward[aligned(step * STEP, STEP), 0:half_len] = cos.astype(BF16)
        forward[aligned(step * STEP, STEP), half_len:] = jnp.where(first_lane, sign, sin).astype(BF16)
        return turn(cos, sin, fore_rc[...], fore_rs[...])

    lax.fori_loop(0, second_len // STEP, fore, (fore_c[...], fore_s[...]))
    quarter = half_len // 2

    def spread(out, cos, sin):
        def body(step, carry):
            cos, sin = carry
            upper = aligned(step * STEP, STEP)
            lower = aligned(quarter + step * STEP, STEP)
            out[upper, 0:half_len] = cos.astype(BF16)
            out[upper, half_len:] = sin.astype(BF16)
            out[lower, 0:half_len] = (-sin).astype(BF16)
            out[lower, half_len:] = cos.astype(BF16)
            return turn(cos, sin, rows_rc[...], rows_rs[...])

        lax.fori_loop(0, quarter // STEP, body, (cos, sin))

    spread(even_out, even_c[...], even_s[...])
    spread(odd_out, odd_c[...], odd_s[...])
    per = lift_out_c.shape[0] // 2

    for parity in range(2):

        def lifts(step, carry, parity=parity):
            cos, sin = carry
            at = aligned(parity * per + step * STEP, STEP)
            lift_out_c[at, :] = cos.astype(BF16)
            lift_out_s[at, :] = sin.astype(BF16)
            return turn(cos, sin, lift_rc[...], lift_rs[...])

        lax.fori_loop(0, per // STEP, lifts, (lift_c[parity], lift_s[parity]))
    lift_out_c[0:STEP, :] = mid_c[...].astype(BF16)
    lift_out_s[0:STEP, :] = mid_s[...].astype(BF16)


def stage_two_kernel(
    segs, cols, place, moved, near_c, near_s, base_c, base_s, mid_c, mid_s, forward_hbm, out,
    forward, stacked, middle, sem,
):
    copy = pltpu.make_async_copy(forward_hbm, forward, sem)
    copy.start()
    sources, rows, _ = moved.shape
    second_len = forward.shape[0]
    half_len = second_len // 2
    quarter = half_len // 2
    tail = segs * cols
    all_rows = (segs + 1) * rows
    width = 2 * cols
    low = lax.broadcasted_iota(jnp.int32, (rows, width), 1) < cols
    own_first = place[0] == 0
    packed_row = lax.broadcasted_iota(jnp.int32, (rows, width), 0) == 0
    drop = jnp.logical_and(packed_row, own_first)

    def pair(left, right):
        return (
            jnp.where(low, left, pltpu.roll(right, cols, 1)),
            jnp.where(low, pltpu.roll(left, cols, 1), right),
        )

    middle[...] = jnp.zeros_like(middle)
    for tile in range(sources // 2):
        lane = slice(tile * width, (tile + 1) * width)
        by_cos, by_sin = base_c[place[0], :, lane], base_s[place[0], :, lane]
        cos = near_c[:, lane] * by_cos - near_s[:, lane] * by_sin
        sin = near_s[:, lane] * by_cos + near_c[:, lane] * by_sin

        def piece(lo, tile=tile):
            hi = lo + width
            return pair(
                moved[2 * tile, :, lo:hi].astype(F32), moved[2 * tile + 1, :, lo:hi].astype(F32)
            )

        def put(seg, real, imag, lane=lane, cos=cos, sin=sin):
            middle[seg : seg + 1, lane] = imag[0:1, :] * mid_c[:, lane]
            middle[rows + seg : rows + seg + 1, lane] = -imag[0:1, :] * mid_s[:, lane]
            imag = jnp.where(drop, 0.0, imag)
            at = seg * rows
            stacked[at : at + rows, lane] = (real * cos + imag * sin).astype(BF16)
            at += all_rows
            stacked[at : at + rows, lane] = (imag * cos - real * sin).astype(BF16)

        for twin in range(segs // 2):
            real_one, real_two = piece(twin * width)
            imag_one, imag_two = piece(tail + twin * width)
            put(2 * twin, real_one, imag_one)
            put(2 * twin + 1, real_two, imag_two)
        real, imag = piece(2 * tail)
        put(segs, real, imag)
    stacked[2 * all_rows :, :] = middle[...].astype(BF16)

    copy.wait()
    first_lane = lax.broadcasted_iota(jnp.int32, (rows, half_len), 1) == 0

    def both(at, lower_at):
        upper = matmul(stacked[at : at + rows, :], forward[...])
        lower = matmul(stacked[lower_at : lower_at + rows, :], forward[...])
        rc, rs = upper[:, :half_len], upper[:, half_len:]
        ic, imag_s = lower[:, :half_len], lower[:, half_len:]
        rz, iz = jnp.where(first_lane, 0.0, rs), jnp.where(first_lane, 0.0, imag_s)
        direct = (rc + iz, ic - rz)
        mirror = (jnp.where(first_lane, rs, rc - iz), -jnp.where(first_lane, imag_s, ic + rz))
        return direct, mirror

    zero = jnp.zeros((rows, half_len), F32)
    level, mirror_level = zero, zero
    for seg in range(segs):
        (real, imag), (mirror_real, mirror_imag) = both(seg * rows, all_rows + seg * rows)
        level = level + (real * real + imag * imag)
        mirror_level = mirror_level + (mirror_real * mirror_real + mirror_imag * mirror_imag)
    direct, mirror = both(segs * rows, all_rows + segs * rows)
    _, (mid_real, mid_imag) = both(2 * all_rows, 2 * all_rows + rows)
    mid_level = jnp.sum((mid_real * mid_real + mid_imag * mid_imag)[:segs], 0, keepdims=True)
    swap = jnp.logical_and(lax.broadcasted_iota(jnp.int32, (rows, half_len), 0) == 0, own_first)
    mirror_level = jnp.where(swap, mid_level, mirror_level)
    mirror_real = jnp.where(swap, mid_real[segs : segs + 1], mirror[0])
    mirror_imag = jnp.where(swap, mid_imag[segs : segs + 1], mirror[1])
    floor = 0.2 * (second_len * 2 * sources * rows)

    def whiten(level, real, imag):
        level = jnp.maximum(level * (1.0 / segs), floor)
        return real / level, imag / level, 1.0 / level

    def ordered(table):
        return jnp.concatenate([table[:, quarter:], pltpu.roll(table[:, :quarter], quarter - 1, 1)], 1)

    upper = whiten(level, *direct)
    lower = [ordered(table) for table in whiten(mirror_level, mirror_real, mirror_imag)]
    eighth = rows // 2
    for part in range(3):
        lane = slice(part * half_len, (part + 1) * half_len)
        for parity in range(2):
            at = slice(parity * eighth, (parity + 1) * eighth)
            block = jnp.concatenate([upper[part][at], lower[part][at]], 0)
            out[parity * rows : (parity + 1) * rows, lane] = block.astype(BF16)


def choose_kernel(place, order, cuts, own, other, out, held, bins):
    rows, sources = own.shape[1], own.shape[0]
    per = sources * rows
    first_len, half_len = 2 * per, own.shape[2] // 2
    for source in range(sources):
        held[source * rows : (source + 1) * rows, :] = own[source]
        held[per + source * rows : per + (source + 1) * rows, :] = other[source]
    cut = cuts[order[place[0]]]
    group = place[1]

    def bin_of(lane):
        return jnp.where(lane < half_len // 2, 2 * lane, 2 * lane - half_len + 1)

    def one_hot(mask):
        return jnp.where(mask, 1.0, 0.0).astype(BF16)

    deep = 128
    wide_row = lax.broadcasted_iota(jnp.int32, (deep, half_len), 0)
    wide_lane = lax.broadcasted_iota(jnp.int32, (deep, half_len), 1)
    for block in range(half_len // deep):
        bins[block * deep : (block + 1) * deep, :] = one_hot(wide_row + block * deep == bin_of(wide_lane))

    def body(step, carry):
        at = step * deep + wide_row
        inner = at % per
        packed = (inner // rows) * rows + 2 * (at % (rows // 2)) + at // per
        mirrored = (at % rows) >= rows // 2
        turned = jnp.where(packed == 0, first_len // 2, first_len - packed)
        row = jnp.where(mirrored, turned, packed)
        share = (row // rows) % 2
        column = (row // (2 * rows)) * rows + row % rows + jnp.where(share == group, 0, per)
        picked = matmul(one_hot(column == wide_lane), held[...]).astype(BF16)
        in_band = row + first_len * bin_of(wide_lane) < cut
        for part in range(2):
            lane = slice(part * half_len, (part + 1) * half_len)
            moved = matmul(picked[:, lane], bins[...])
            out[aligned(step * deep, deep), lane] = jnp.where(in_band, moved, 0.0).astype(BF16)
        return carry

    lax.fori_loop(0, first_len // deep, body, 0)


def inverse_kernel(
    place, near, far, chosen, even_hbm, odd_hbm, lift_c_hbm, lift_s_hbm, cols_hbm, out,
    even_table, odd_table, lift_c, lift_s, cols_table, filtered, lifted, sems,
):
    copies = [
        pltpu.make_async_copy(source, target, sems.at[at])
        for at, (source, target) in enumerate(
            [
                (even_hbm, even_table),
                (odd_hbm, odd_table),
                (lift_c_hbm, lift_c),
                (lift_s_hbm, lift_s),
                (cols_hbm, cols_table),
            ]
        )
    ]
    for copy in copies:
        copy.start()
    half_len = even_table.shape[0]
    second_len = 2 * half_len
    first_len = filtered.shape[0]
    per = first_len // 2
    quarter = half_len // 2
    rows = near.shape[1] // 2
    norm = jnp.zeros((rows, half_len), F32)
    for blocks, turned in ((near, 0), (far, 1)):
        for block, offset in enumerate(NEAR):
            device = jnp.bitwise_xor(place[0], offset ^ turned)
            for parity in range(2):
                row = slice(parity * rows, (parity + 1) * rows)
                at = aligned(parity * per + device * rows, rows)
                white_real = blocks[block, row, :half_len].astype(F32)
                white_imag = blocks[block, row, half_len : 2 * half_len].astype(F32)
                weight = blocks[block, row, 2 * half_len :].astype(F32)
                real = chosen[at, :half_len].astype(F32)
                imag = chosen[at, half_len:].astype(F32)
                norm = norm + (real * real + imag * imag) * weight
                filt_real = (white_real * real + white_imag * imag).astype(BF16)
                filt_imag = (white_imag * real - white_real * imag).astype(BF16)
                filtered[at, 0:quarter] = filt_real[:, :quarter]
                filtered[at, quarter:half_len] = filt_imag[:, :quarter]
                filtered[at, half_len : half_len + quarter] = filt_real[:, quarter:]
                filtered[at, half_len + quarter :] = filt_imag[:, quarter:]
    scale = lax.rsqrt(jnp.sum(norm, keepdims=True))
    for copy in copies[:4]:
        copy.wait()
    deep = 128

    def lift(step, carry):
        at = aligned(step * deep, deep)
        even = matmul(filtered[at, :half_len], even_table[...])
        odd = matmul(filtered[at, half_len:], odd_table[...])
        parity = step // (per // deep)
        target = parity * first_len + (step - parity * (per // deep)) * deep
        for upper in range(2):
            lane = slice(upper * half_len, (upper + 1) * half_len)
            total = even - odd if upper else even + odd
            real, imag = total[:, :half_len], total[:, half_len:]
            cos, sin = lift_c[at, lane].astype(F32), lift_s[at, lane].astype(F32)
            lifted[aligned(target, deep), lane] = (real * cos - imag * sin).astype(BF16)
            lifted[aligned(target + per, deep), lane] = (real * sin + imag * cos).astype(BF16)
        return carry

    lax.fori_loop(0, first_len // deep, lift, 0)
    copies[4].wait()
    tall = 64
    wide = 512

    def field(step, carry):
        upper = aligned(step * tall, tall)
        lower = aligned(per + step * tall, tall)
        for lane in range(0, second_len, wide):
            at = slice(lane, lane + wide)
            even, odd = lifted[:first_len, at], lifted[first_len:, at]
            even_real = matmul(cols_table[upper, :first_len], even)
            even_imag = matmul(cols_table[lower, :first_len], even)
            odd_real = matmul(cols_table[upper, first_len:], odd)
            odd_imag = matmul(cols_table[lower, first_len:], odd)
            real, imag = even_real + odd_real, even_imag + odd_imag
            out[0, upper, at] = (jnp.sqrt(real * real + imag * imag) * scale).astype(BF16)
            real, imag = even_real - odd_real, even_imag - odd_imag
            out[0, lower, at] = (jnp.sqrt(real * real + imag * imag) * scale).astype(BF16)
        return carry

    lax.fori_loop(0, per // tall, field, 0)


def swap_with(array, flip):
    pairs = [(at, at ^ flip) for at in range(lax.axis_size("tmpl"))]
    return lax.ppermute(array, "tmpl", pairs)


def tiled_local(strain, analysis, bank, cutoff, order):
    dev_count = lax.axis_size("tmpl")
    segs, first_len, cols = strain.shape
    second_len = cols * dev_count
    length = first_len * second_len
    half_len = second_len // 2
    rows = first_len // dev_count // 2
    templates = order.shape[0]
    lanes = 2 * (segs + 1) * cols
    place = jnp.stack([lax.axis_index("tmpl"), lax.axis_index("grp")]).astype(jnp.int32)

    first, second, half = np.arange(first_len), np.arange(second_len), np.arange(half_len)
    devices, step = np.arange(dev_count), np.arange(STEP)
    near = halves(rows)
    packed = (devices[:, None] * rows + near[None, :]).reshape(-1, 1)
    cos_one, sin_one = turns(packed * first[None, :], first_len)
    sin_one[0] = 2 * (first % 2) - 1.0
    win_c, win_s = turns(np.arange(cols)[:, None] + second_len * first[None, :], length)
    spin = np.stack(turns(cols * devices, length), 1)

    sent = pl.pallas_call(
        stage_one_kernel,
        out_shape=jax.ShapeDtypeStruct((dev_count * rows, lanes + 2 * half_len), BF16),
        in_specs=[scalars()] * 3 + [whole()] * 6 + [pl.BlockSpec(memory_space=pl.ANY)],
        out_specs=whole(),
        scratch_shapes=[
            vmem(((segs + 1) * cols, first_len)),
            pltpu.SemaphoreType.DMA((2 * templates,)),
        ],
        compiler_params=params(16),
        name="stage_one",
    )(
        place, order, jnp.asarray(spin), jnp.swapaxes(strain, 1, 2), jnp.swapaxes(analysis, 0, 1),
        jnp.asarray(win_c), jnp.asarray(win_s), jnp.asarray(cos_one, BF16), jnp.asarray(sin_one, BF16), bank,
    )
    moved = lax.all_to_all(
        sent.reshape(dev_count, rows, lanes + 2 * half_len), "tmpl", split_axis=0, concat_axis=0, tiled=True
    )
    own = moved[:, :, lanes:]
    other = lax.ppermute(own, "grp", [(0, 1), (1, 0)])

    split = halves(half_len)
    low = 2 * np.arange(rows // 2)
    lift_rows = [np.concatenate([low + odd, first_len - low - odd]) for odd in range(2)]
    lift_init = [turns(at[:, None] * second[None, :], length) for at in lift_rows]
    mid_rows = lift_rows[0].copy()
    mid_rows[rows // 2] = first_len // 2
    step_sign = np.where(np.arange(rows) < rows // 2, rows, -rows)
    tables = [
        *turns(step[:, None] * split[None, :], second_len),
        *turns(STEP * split[None, :], second_len),
        *turns(2 * step[:, None] * half[None, :], second_len),
        *turns((2 * step[:, None] + 1) * half[None, :], second_len),
        *turns(2 * STEP * half[None, :], second_len),
        np.stack([lift_init[0][0], lift_init[1][0]]),
        np.stack([lift_init[0][1], lift_init[1][1]]),
        *turns(step_sign[:, None] * second[None, :], length),
        *turns(mid_rows[:, None] * second[None, :], length),
    ]
    shapes = [(second_len, second_len)] + [(half_len, second_len)] * 2 + [(first_len, second_len)] * 2
    forward, even_table, odd_table, lift_c, lift_s = pl.pallas_call(
        tables_kernel,
        out_shape=[jax.ShapeDtypeStruct(shape, BF16) for shape in shapes],
        in_specs=[whole()] * len(tables),
        out_specs=[whole()] * len(shapes),
        compiler_params=params(24),
        cost_estimate=pl.CostEstimate(flops=10**7, bytes_accessed=2 * 10**7, transcendentals=0),
        name="tables",
    )(*[jnp.asarray(table) for table in tables])

    near_c, near_s = turns(near[:, None] * second[None, :], length)
    base_c, base_s = turns(rows * devices[:, None, None] * second[None, None, :], length)
    mid_c, mid_s = turns(first_len // 2 * second[None, :], length)
    all_rows = 2 * (segs + 2) * rows
    block = pl.pallas_call(
        functools.partial(stage_two_kernel, segs, cols),
        out_shape=jax.ShapeDtypeStruct((2 * rows, 3 * half_len), BF16),
        in_specs=[scalars()] + [whole()] * 7 + [pl.BlockSpec(memory_space=pl.ANY)],
        out_specs=whole(),
        scratch_shapes=[
            vmem(forward.shape),
            vmem((all_rows, second_len)),
            vmem((2 * rows, second_len), F32),
            pltpu.SemaphoreType.DMA,
        ],
        compiler_params=params(24),
        cost_estimate=pl.CostEstimate(flops=10**9, bytes_accessed=4 * 10**6, transcendentals=0),
        name="stage_two",
    )(
        place, moved, jnp.asarray(near_c), jnp.asarray(near_s), jnp.asarray(base_c), jnp.asarray(base_s),
        jnp.asarray(mid_c), jnp.asarray(mid_s), forward,
    )

    beside, one, two = swap_with(block, 2), swap_with(block, 4), swap_with(block, 12)
    both = swap_with(jnp.stack([one, two]), 2)
    far = swap_with(two, 4)
    last = swap_with(far, 2)
    mine = jnp.stack([block, beside, one, two, both[0], both[1], far, last])
    theirs = swap_with(mine, 1)

    chosen = pl.pallas_call(
        choose_kernel,
        out_shape=jax.ShapeDtypeStruct((first_len, 2 * half_len), BF16),
        in_specs=[scalars()] * 3 + [whole()] * 2,
        out_specs=whole(),
        scratch_shapes=[vmem((first_len, 2 * half_len)), vmem((half_len, half_len))],
        compiler_params=params(16),
        cost_estimate=pl.CostEstimate(flops=10**9, bytes_accessed=4 * 10**6, transcendentals=0),
        name="choose",
    )(place, order, cutoff, own, other)

    per = first_len // 2
    cols_parts = []
    for odd in range(2):
        straight = devices[:, None] * rows + low[None, :] + odd
        turned = first_len - straight
        turned[straight == 0] = first_len // 2
        at = np.concatenate([straight, turned], 1).reshape(-1)
        cos, sin = turns(np.arange(per)[:, None] * at[None, :], first_len)
        cols_parts.append(np.block([[cos, -sin], [sin, cos]]))
    cols_table = jnp.asarray(np.concatenate(cols_parts, 1), BF16)
    any_space = pl.BlockSpec(memory_space=pl.ANY)
    return pl.pallas_call(
        inverse_kernel,
        out_shape=jax.ShapeDtypeStruct((1, first_len, second_len), BF16),
        in_specs=[scalars()] + [whole()] * 3 + [any_space] * 5,
        out_specs=whole(),
        scratch_shapes=[
            vmem(even_table.shape),
            vmem(odd_table.shape),
            vmem(lift_c.shape),
            vmem(lift_s.shape),
            vmem(cols_table.shape),
            vmem((first_len, 2 * half_len)),
            vmem((2 * first_len, second_len)),
            pltpu.SemaphoreType.DMA((5,)),
        ],
        compiler_params=params(32),
        name="inverse",
    )(place, mine, theirs, chosen, even_table, odd_table, lift_c, lift_s, cols_table)


def angles(left_idx, right_idx, period):
    product = left_idx[:, None] * right_idx[None, :] % period
    phase_angle = product.astype(jnp.float32) * (2.0 * math.pi / period)
    return (jnp.cos(phase_angle), jnp.sin(phase_angle))


def filtered(white_pair, tmpl_pair, cut_bins, freq_bin):
    white_real = white_pair[0].astype(jnp.float32)
    white_imag = white_pair[1].astype(jnp.float32)
    tmpl_real = tmpl_pair[0].astype(jnp.float32)
    tmpl_imag = tmpl_pair[1].astype(jnp.float32)
    in_band = freq_bin[None] < cut_bins[:, None, None]
    filt_real = jnp.where(in_band, white_real * tmpl_real + white_imag * tmpl_imag, 0.0)
    filt_imag = jnp.where(in_band, white_imag * tmpl_real - white_real * tmpl_imag, 0.0)
    return jnp.concatenate([filt_real, filt_imag], -1).astype(jnp.bfloat16)


def inverse_rows(stacked, row_bins, second_len, length):
    half_len = second_len // 2
    cosine, sine = angles(
        jnp.arange(half_len, dtype=jnp.int32), jnp.arange(second_len, dtype=jnp.int32), second_len
    )
    dft_table = jnp.concatenate(
        [jnp.concatenate([cosine, sine], 1), jnp.concatenate([-sine, cosine], 1)], 0
    ).astype(jnp.bfloat16)
    spread = jnp.einsum("tkf,fg->tkg", stacked, dft_table, preferred_element_type=jnp.float32)
    spread_real = spread[..., :second_len]
    spread_imag = spread[..., second_len:]
    cos_twist, sin_twist = angles(row_bins, jnp.arange(second_len, dtype=jnp.int32), length)
    lift_real = spread_real * cos_twist - spread_imag * sin_twist
    lift_imag = spread_real * sin_twist + spread_imag * cos_twist
    return jnp.concatenate([lift_real, lift_imag], -1).astype(jnp.bfloat16)


def inverse_cols(lifted, first_len, second_len):
    row_idx = jnp.arange(first_len, dtype=jnp.int32)
    cosine, sine = angles(row_idx, row_idx, first_len)
    cosine = cosine.astype(jnp.bfloat16)
    sine = sine.astype(jnp.bfloat16)
    lift_real = lifted[..., :second_len]
    lift_imag = lifted[..., second_len:]
    field_real = jnp.einsum(
        "ak,tkb->tab", cosine, lift_real, preferred_element_type=jnp.float32
    ) - jnp.einsum("ak,tkb->tab", sine, lift_imag, preferred_element_type=jnp.float32)
    field_imag = jnp.einsum(
        "ak,tkb->tab", sine, lift_real, preferred_element_type=jnp.float32
    ) + jnp.einsum("ak,tkb->tab", cosine, lift_imag, preferred_element_type=jnp.float32)
    return (field_real, field_imag)


def plain_local(strain, analysis, bank, cutoff, order):
    highest = lax.Precision.HIGHEST
    dev_count = lax.axis_size("tmpl")
    my_index = lax.axis_index("tmpl")
    seg_count = strain.shape[0]
    first_len = strain.shape[1]
    col_count = strain.shape[2]
    second_len = col_count * dev_count
    length = first_len * second_len
    half_len = second_len // 2
    row_count = first_len // dev_count
    row_idx = jnp.arange(first_len, dtype=jnp.int32)
    col_index = my_index * col_count + jnp.arange(col_count, dtype=jnp.int32)
    sample_idx = row_idx[:, None] * second_len + col_index[None, :]
    window = (
        math.sqrt(8.0 / 3.0) * jnp.sin(sample_idx.astype(jnp.float32) * (math.pi / length)) ** 2
    )
    series = jnp.concatenate([strain * window, analysis[None]], 0)
    cos_one, sin_one = angles(row_idx, row_idx, first_len)
    part_real = jnp.einsum("ka,sab->skb", cos_one, series, precision=highest)
    part_imag = -jnp.einsum("ka,sab->skb", sin_one, series, precision=highest)
    cos_twist, sin_twist = angles(row_idx, col_index, length)
    twist_real = part_real * cos_twist + part_imag * sin_twist
    twist_imag = part_imag * cos_twist - part_real * sin_twist
    moved = lax.all_to_all(
        jnp.stack([twist_real, twist_imag]).astype(jnp.bfloat16),
        "tmpl",
        split_axis=2,
        concat_axis=3,
        tiled=True,
    ).astype(jnp.float32)
    cos_two, sin_two = angles(
        jnp.arange(second_len, dtype=jnp.int32), jnp.arange(half_len, dtype=jnp.int32), second_len
    )
    spec_real = jnp.einsum("skb,bf->skf", moved[0], cos_two, precision=highest) + jnp.einsum(
        "skb,bf->skf", moved[1], sin_two, precision=highest
    )
    spec_imag = jnp.einsum("skb,bf->skf", moved[1], cos_two, precision=highest) - jnp.einsum(
        "skb,bf->skf", moved[0], sin_two, precision=highest
    )
    power_spec = jnp.maximum(
        jnp.mean(spec_real[:seg_count] ** 2 + spec_imag[:seg_count] ** 2, axis=0), 0.2 * length
    )
    whitened = jnp.stack(
        [spec_real[seg_count] / power_spec, spec_imag[seg_count] / power_spec]
    ).astype(jnp.bfloat16)
    own_rows = my_index * row_count + jnp.arange(row_count, dtype=jnp.int32)
    half_idx = jnp.arange(half_len, dtype=jnp.int32)
    freq_local = own_rows[:, None] + first_len * half_idx[None, :]
    chosen = jnp.take(bank, order, axis=1)
    cuts = jnp.take(cutoff, order)
    bank_real = chosen[0].astype(jnp.float32)
    bank_imag = chosen[1].astype(jnp.float32)
    in_band = freq_local[None] < cuts[:, None, None]
    local_norm = jnp.sum(
        jnp.where(in_band, (bank_real**2 + bank_imag**2) / power_spec, 0.0), axis=(1, 2)
    )
    norm_sq = lax.psum(local_norm, "tmpl")
    per_device = cuts.shape[0] // dev_count
    own_norm = lax.dynamic_slice_in_dim(norm_sq, my_index * per_device, per_device)
    stacked = filtered(whitened, chosen, cuts, freq_local)
    lifted = lax.all_to_all(
        inverse_rows(stacked, own_rows, second_len, length),
        "tmpl",
        split_axis=0,
        concat_axis=1,
        tiled=True,
    )
    field_real, field_imag = inverse_cols(lifted, first_len, second_len)
    magnitude = jnp.sqrt(field_real**2 + field_imag**2)
    return (magnitude / jnp.sqrt(own_norm)[:, None, None]).astype(jnp.bfloat16)


def local(strain, analysis, bank, cutoff, order):
    dev_count, segs, cols = lax.axis_size("tmpl"), strain.shape[0], strain.shape[2]
    rows = strain.shape[1] // dev_count // 2
    fits = rows == STEP and cols == 64 and segs % 2 == 0 and dev_count == 2 * len(NEAR)
    if fits and order.shape[0] == dev_count and lax.axis_size("grp") == 2:
        return tiled_local(strain, analysis, bank, cutoff, order)
    return plain_local(strain, analysis, bank, cutoff, order)


def solution(mesh):
    return jax.shard_map(
        local,
        mesh=mesh,
        in_specs=(P("grp", None, "tmpl"), P("grp", "tmpl"), P(None, None, "tmpl", None), P(), P()),
        out_specs=P(("grp", "tmpl"), None, None),
        check_vma=False,
    )
```

```python
import functools
import math

import jax
import jax.numpy as jnp
import numpy as np
from jax import lax
from jax.experimental import pallas as pl
from jax.experimental.pallas import tpu as pltpu
from jax.sharding import PartitionSpec as P

BF16 = jnp.bfloat16
F32 = jnp.float32
STEP = 16
NEAR = (0, 2, 4, 12, 6, 14, 8, 10)


def turns(product, period):
    angle = (product % period) * (2.0 * math.pi / period)
    return np.cos(angle).astype(np.float32), np.sin(angle).astype(np.float32)


def matmul(left, right):
    return jnp.dot(left, right, preferred_element_type=F32)


def matmul_nt(left, right):
    return lax.dot_general(left, right, (((1,), (1,)), ((), ())), preferred_element_type=F32)


def vmem(shape, dtype=BF16):
    return pltpu.VMEM(shape, dtype)


def whole():
    return pl.BlockSpec(memory_space=pltpu.VMEM)


def outside():
    return pl.BlockSpec(memory_space=pltpu.HBM)


def in_hbm(*arrays):
    return [pltpu.with_memory_space_constraint(jnp.asarray(array), pltpu.HBM) for array in arrays]


def position():
    return lax.axis_index("tmpl"), lax.axis_index("grp")


def start_copies(pairs, sems):
    copies = [
        pltpu.make_async_copy(source, target, sems.at[at]) for at, (source, target) in enumerate(pairs)
    ]
    for copy in copies:
        copy.start()
    return copies


def params(mib):
    return pltpu.CompilerParams(vmem_limit_bytes=mib << 20)


def halves(count):
    return np.concatenate([np.arange(0, count, 2), np.arange(1, count, 2)])


def aligned(start, size):
    return pl.ds(pl.multiple_of(start, size), size)


def stage_one_kernel(
    order, strain_hbm, analysis_hbm, spin_hbm, win_c_hbm, win_s_hbm, cos_hbm, sin_hbm, bank, out,
    strain, analysis, spin, win_c, win_s, cos, sin, packed, sems, bank_sems,
):
    segs, cols, _ = strain.shape
    tail = segs * cols
    templates, half_len = bank.shape[1], bank.shape[3]
    rows = out.shape[0] // templates
    place, group = position()
    sources = [
        (spin_hbm.at[place], spin),
        (win_c_hbm, win_c),
        (win_s_hbm, win_s),
        *[(strain_hbm.at[seg], strain.at[seg]) for seg in range(segs)],
        (analysis_hbm, analysis),
        (cos_hbm, cos),
        (sin_hbm, sin),
    ]
    copies = start_copies(sources, sems)
    lane = 2 * (tail + cols)
    bank_pairs = []
    for row in range(templates):
        for part in range(2):
            bank_pairs.append(
                (
                    bank.at[part, order[row], aligned(group * rows, rows), :],
                    out.at[
                        row * rows : (row + 1) * rows,
                        lane + part * half_len : lane + (part + 1) * half_len,
                    ],
                )
            )
    bank_copies = start_copies(bank_pairs, bank_sems)
    for copy in copies[:3]:
        copy.wait()
    scale = 0.5 * math.sqrt(8.0 / 3.0)
    window = scale - scale * (win_c[...] * spin[0:1, :] - win_s[...] * spin[1:2, :])
    for seg in range(segs):
        copies[3 + seg].wait()
        packed[seg * cols : (seg + 1) * cols, :] = (strain[seg] * window).astype(BF16)
    for copy in copies[3 + segs :]:
        copy.wait()
    packed[tail:, :] = analysis[...].astype(BF16)
    real = matmul_nt(cos[...], packed[...])
    imag = -matmul_nt(sin[...], packed[...])
    out[:, 0:tail] = real[:, :tail].astype(BF16)
    out[:, tail : 2 * tail] = imag[:, :tail].astype(BF16)
    joined = jnp.concatenate([real[:, tail:], imag[:, tail:]], 1)
    out[:, 2 * tail : lane] = joined.astype(BF16)
    for copy in bank_copies:
        copy.wait()


def tables_kernel(
    fore_c, fore_s, fore_rc, fore_rs, even_c, even_s, odd_c, odd_s, rows_rc, rows_rs,
    lift_c, lift_s, lift_rc, lift_rs, mid_c, mid_s,
    forward_hbm, even_hbm, odd_hbm, lift_c_hbm, lift_s_hbm,
    forward, even_out, odd_out, lift_out_c, lift_out_s, sems,
):
    half_len = fore_c.shape[1]
    second_len = 2 * half_len

    def turn(cos, sin, by_cos, by_sin):
        return cos * by_cos - sin * by_sin, sin * by_cos + cos * by_sin

    first_lane = lax.broadcasted_iota(jnp.int32, fore_c.shape, 1) == 0
    sign = 1.0 - 2.0 * (lax.broadcasted_iota(jnp.int32, fore_c.shape, 0) % 2).astype(F32)

    def fore(step, carry):
        cos, sin = carry
        forward[aligned(step * STEP, STEP), 0:half_len] = cos.astype(BF16)
        forward[aligned(step * STEP, STEP), half_len:] = jnp.where(first_lane, sign, sin).astype(BF16)
        return turn(cos, sin, fore_rc[...], fore_rs[...])

    lax.fori_loop(0, second_len // STEP, fore, (fore_c[...], fore_s[...]))
    quarter = half_len // 2

    def spread(out, cos, sin):
        def body(step, carry):
            cos, sin = carry
            upper = aligned(step * STEP, STEP)
            lower = aligned(quarter + step * STEP, STEP)
            out[upper, 0:half_len] = cos.astype(BF16)
            out[upper, half_len:] = sin.astype(BF16)
            out[lower, 0:half_len] = (-sin).astype(BF16)
            out[lower, half_len:] = cos.astype(BF16)
            return turn(cos, sin, rows_rc[...], rows_rs[...])

        lax.fori_loop(0, quarter // STEP, body, (cos, sin))

    spread(even_out, even_c[...], even_s[...])
    spread(odd_out, odd_c[...], odd_s[...])
    per = lift_out_c.shape[0] // 2

    for parity in range(2):

        def lifts(step, carry, parity=parity):
            cos, sin = carry
            at = aligned(parity * per + step * STEP, STEP)
            lift_out_c[at, :] = cos.astype(BF16)
            lift_out_s[at, :] = sin.astype(BF16)
            return turn(cos, sin, lift_rc[...], lift_rs[...])

        lax.fori_loop(0, per // STEP, lifts, (lift_c[parity], lift_s[parity]))
    lift_out_c[0:STEP, :] = mid_c[...].astype(BF16)
    lift_out_s[0:STEP, :] = mid_s[...].astype(BF16)
    made = [forward, even_out, odd_out, lift_out_c, lift_out_s]
    kept = [forward_hbm, even_hbm, odd_hbm, lift_c_hbm, lift_s_hbm]
    for copy in start_copies(list(zip(made, kept)), sems):
        copy.wait()


def stage_two_kernel(
    segs, cols, moved, near_c_hbm, near_s_hbm, base_c_hbm, base_s_hbm, mid_c_hbm, mid_s_hbm, forward_hbm, out,
    near_c, near_s, base_c, base_s, mid_c, mid_s, forward, stacked, middle, sems,
):
    place, _ = position()
    pairs = [
        (near_c_hbm, near_c),
        (near_s_hbm, near_s),
        (base_c_hbm.at[place], base_c),
        (base_s_hbm.at[place], base_s),
        (mid_c_hbm, mid_c),
        (mid_s_hbm, mid_s),
        (forward_hbm, forward),
    ]
    copies = start_copies(pairs, sems)
    sources, rows, _ = moved.shape
    second_len = forward.shape[0]
    half_len = second_len // 2
    quarter = half_len // 2
    tail = segs * cols
    all_rows = (segs + 1) * rows
    width = 2 * cols
    low = lax.broadcasted_iota(jnp.int32, (rows, width), 1) < cols
    own_first = place == 0
    packed_row = lax.broadcasted_iota(jnp.int32, (rows, width), 0) == 0
    drop = jnp.logical_and(packed_row, own_first)

    def pair(left, right):
        return (
            jnp.where(low, left, pltpu.roll(right, cols, 1)),
            jnp.where(low, pltpu.roll(left, cols, 1), right),
        )

    middle[...] = jnp.zeros_like(middle)
    for copy in copies[:-1]:
        copy.wait()
    for tile in range(sources // 2):
        lane = slice(tile * width, (tile + 1) * width)
        by_cos, by_sin = base_c[:, lane], base_s[:, lane]
        cos = near_c[:, lane] * by_cos - near_s[:, lane] * by_sin
        sin = near_s[:, lane] * by_cos + near_c[:, lane] * by_sin

        def piece(lo, tile=tile):
            hi = lo + width
            return pair(
                moved[2 * tile, :, lo:hi].astype(F32), moved[2 * tile + 1, :, lo:hi].astype(F32)
            )

        def put(seg, real, imag, lane=lane, cos=cos, sin=sin):
            middle[seg : seg + 1, lane] = imag[0:1, :] * mid_c[:, lane]
            middle[rows + seg : rows + seg + 1, lane] = -imag[0:1, :] * mid_s[:, lane]
            imag = jnp.where(drop, 0.0, imag)
            at = seg * rows
            stacked[at : at + rows, lane] = (real * cos + imag * sin).astype(BF16)
            at += all_rows
            stacked[at : at + rows, lane] = (imag * cos - real * sin).astype(BF16)

        for twin in range(segs // 2):
            real_one, real_two = piece(twin * width)
            imag_one, imag_two = piece(tail + twin * width)
            put(2 * twin, real_one, imag_one)
            put(2 * twin + 1, real_two, imag_two)
        real, imag = piece(2 * tail)
        put(segs, real, imag)
    stacked[2 * all_rows :, :] = middle[...].astype(BF16)

    copies[-1].wait()
    first_lane = lax.broadcasted_iota(jnp.int32, (rows, half_len), 1) == 0

    def both(at, lower_at):
        upper = matmul(stacked[at : at + rows, :], forward[...])
        lower = matmul(stacked[lower_at : lower_at + rows, :], forward[...])
        rc, rs = upper[:, :half_len], upper[:, half_len:]
        ic, imag_s = lower[:, :half_len], lower[:, half_len:]
        rz, iz = jnp.where(first_lane, 0.0, rs), jnp.where(first_lane, 0.0, imag_s)
        direct = (rc + iz, ic - rz)
        mirror = (jnp.where(first_lane, rs, rc - iz), -jnp.where(first_lane, imag_s, ic + rz))
        return direct, mirror

    zero = jnp.zeros((rows, half_len), F32)
    level, mirror_level = zero, zero
    for seg in range(segs):
        (real, imag), (mirror_real, mirror_imag) = both(seg * rows, all_rows + seg * rows)
        level = level + (real * real + imag * imag)
        mirror_level = mirror_level + (mirror_real * mirror_real + mirror_imag * mirror_imag)
    direct, mirror = both(segs * rows, all_rows + segs * rows)
    _, (mid_real, mid_imag) = both(2 * all_rows, 2 * all_rows + rows)
    mid_level = jnp.sum((mid_real * mid_real + mid_imag * mid_imag)[:segs], 0, keepdims=True)
    swap = jnp.logical_and(lax.broadcasted_iota(jnp.int32, (rows, half_len), 0) == 0, own_first)
    mirror_level = jnp.where(swap, mid_level, mirror_level)
    mirror_real = jnp.where(swap, mid_real[segs : segs + 1], mirror[0])
    mirror_imag = jnp.where(swap, mid_imag[segs : segs + 1], mirror[1])
    floor = 0.2 * (second_len * 2 * sources * rows)

    def whiten(level, real, imag):
        level = jnp.maximum(level * (1.0 / segs), floor)
        return real / level, imag / level, 1.0 / level

    def ordered(table):
        return jnp.concatenate([table[:, quarter:], pltpu.roll(table[:, :quarter], quarter - 1, 1)], 1)

    upper = whiten(level, *direct)
    lower = [ordered(table) for table in whiten(mirror_level, mirror_real, mirror_imag)]
    eighth = rows // 2
    for part in range(3):
        lane = slice(part * half_len, (part + 1) * half_len)
        for parity in range(2):
            at = slice(parity * eighth, (parity + 1) * eighth)
            block = jnp.concatenate([upper[part][at], lower[part][at]], 0)
            out[parity * rows : (parity + 1) * rows, lane] = block.astype(BF16)


def choose_kernel(order, cuts, own, other, out, held, bins):
    place, group = position()
    rows, sources = own.shape[1], own.shape[0]
    per = sources * rows
    first_len, half_len = 2 * per, own.shape[2] // 2
    for source in range(sources):
        held[source * rows : (source + 1) * rows, :] = own[source]
        held[per + source * rows : per + (source + 1) * rows, :] = other[source]
    cut = cuts[order[place]]

    def bin_of(lane):
        return jnp.where(lane < half_len // 2, 2 * lane, 2 * lane - half_len + 1)

    def one_hot(mask):
        return jnp.where(mask, 1.0, 0.0).astype(BF16)

    deep = 128
    wide_row = lax.broadcasted_iota(jnp.int32, (deep, half_len), 0)
    wide_lane = lax.broadcasted_iota(jnp.int32, (deep, half_len), 1)
    for block in range(half_len // deep):
        bins[block * deep : (block + 1) * deep, :] = one_hot(wide_row + block * deep == bin_of(wide_lane))

    def body(step, carry):
        at = step * deep + wide_row
        inner = at % per
        packed = (inner // rows) * rows + 2 * (at % (rows // 2)) + at // per
        mirrored = (at % rows) >= rows // 2
        turned = jnp.where(packed == 0, first_len // 2, first_len - packed)
        row = jnp.where(mirrored, turned, packed)
        share = (row // rows) % 2
        column = (row // (2 * rows)) * rows + row % rows + jnp.where(share == group, 0, per)
        picked = matmul(one_hot(column == wide_lane), held[...]).astype(BF16)
        in_band = row + first_len * bin_of(wide_lane) < cut
        for part in range(2):
            lane = slice(part * half_len, (part + 1) * half_len)
            moved = matmul(picked[:, lane], bins[...])
            out[aligned(step * deep, deep), lane] = jnp.where(in_band, moved, 0.0).astype(BF16)
        return carry

    lax.fori_loop(0, first_len // deep, body, 0)


def inverse_kernel(
    near, far, chosen, even_table, odd_table, lift_c, lift_s, cols_table, out, filtered, lifted
):
    place, _ = position()
    half_len = even_table.shape[0]
    second_len = 2 * half_len
    first_len = filtered.shape[0]
    per = first_len // 2
    quarter = half_len // 2
    rows = near.shape[1] // 2
    norm = jnp.zeros((rows, half_len), F32)
    for blocks, turned in ((near, 0), (far, 1)):
        for block, offset in enumerate(NEAR):
            device = jnp.bitwise_xor(place, offset ^ turned)
            for parity in range(2):
                row = slice(parity * rows, (parity + 1) * rows)
                at = aligned(parity * per + device * rows, rows)
                white_real = blocks[block, row, :half_len].astype(F32)
                white_imag = blocks[block, row, half_len : 2 * half_len].astype(F32)
                weight = blocks[block, row, 2 * half_len :].astype(F32)
                real = chosen[at, :half_len].astype(F32)
                imag = chosen[at, half_len:].astype(F32)
                norm = norm + (real * real + imag * imag) * weight
                filt_real = (white_real * real + white_imag * imag).astype(BF16)
                filt_imag = (white_imag * real - white_real * imag).astype(BF16)
                filtered[at, 0:quarter] = filt_real[:, :quarter]
                filtered[at, quarter:half_len] = filt_imag[:, :quarter]
                filtered[at, half_len : half_len + quarter] = filt_real[:, quarter:]
                filtered[at, half_len + quarter :] = filt_imag[:, quarter:]
    scale = lax.rsqrt(jnp.sum(norm, keepdims=True))
    deep = 128

    def lift(step, carry):
        at = aligned(step * deep, deep)
        even = matmul(filtered[at, :half_len], even_table[...])
        odd = matmul(filtered[at, half_len:], odd_table[...])
        parity = step // (per // deep)
        target = parity * first_len + (step - parity * (per // deep)) * deep
        for upper in range(2):
            lane = slice(upper * half_len, (upper + 1) * half_len)
            total = even - odd if upper else even + odd
            real, imag = total[:, :half_len], total[:, half_len:]
            cos, sin = lift_c[at, lane].astype(F32), lift_s[at, lane].astype(F32)
            lifted[aligned(target, deep), lane] = (real * cos - imag * sin).astype(BF16)
            lifted[aligned(target + per, deep), lane] = (real * sin + imag * cos).astype(BF16)
        return carry

    lax.fori_loop(0, first_len // deep, lift, 0)
    tall = 64
    wide = 512

    def field(step, carry):
        upper = aligned(step * tall, tall)
        lower = aligned(per + step * tall, tall)
        for lane in range(0, second_len, wide):
            at = slice(lane, lane + wide)
            even, odd = lifted[:first_len, at], lifted[first_len:, at]
            even_real = matmul(cols_table[upper, :first_len], even)
            even_imag = matmul(cols_table[lower, :first_len], even)
            odd_real = matmul(cols_table[upper, first_len:], odd)
            odd_imag = matmul(cols_table[lower, first_len:], odd)
            real, imag = even_real + odd_real, even_imag + odd_imag
            out[0, upper, at] = (jnp.sqrt(real * real + imag * imag) * scale).astype(BF16)
            real, imag = even_real - odd_real, even_imag - odd_imag
            out[0, lower, at] = (jnp.sqrt(real * real + imag * imag) * scale).astype(BF16)
        return carry

    lax.fori_loop(0, per // tall, field, 0)


def swap_with(array, flip):
    pairs = [(at, at ^ flip) for at in range(lax.axis_size("tmpl"))]
    return lax.ppermute(array, "tmpl", pairs)


def tiled_local(strain, analysis, bank, cutoff, order):
    dev_count = lax.axis_size("tmpl")
    segs, first_len, cols = strain.shape
    second_len = cols * dev_count
    length = first_len * second_len
    half_len = second_len // 2
    rows = first_len // dev_count // 2
    templates = order.shape[0]
    lanes = 2 * (segs + 1) * cols

    first, second, half = np.arange(first_len), np.arange(second_len), np.arange(half_len)
    devices, step = np.arange(dev_count), np.arange(STEP)
    near = halves(rows)
    packed = (devices[:, None] * rows + near[None, :]).reshape(-1, 1)
    cos_one, sin_one = turns(packed * first[None, :], first_len)
    sin_one[0] = 2 * (first % 2) - 1.0
    win_c, win_s = turns(np.arange(cols)[:, None] + second_len * first[None, :], length)
    spin = np.stack(turns(cols * devices, length), 1)[:, :, None] * np.ones((1, 1, first_len), np.float32)

    sent = pl.pallas_call(
        stage_one_kernel,
        grid_spec=pltpu.PrefetchScalarGridSpec(
            num_scalar_prefetch=1,
            grid=(),
            in_specs=[outside()] * 8,
            out_specs=whole(),
            scratch_shapes=[
                vmem((segs, cols, first_len), F32),
                vmem((cols, first_len), F32),
                vmem((2, first_len), F32),
                vmem((cols, first_len), F32),
                vmem((cols, first_len), F32),
                vmem((dev_count * rows, first_len)),
                vmem((dev_count * rows, first_len)),
                vmem(((segs + 1) * cols, first_len)),
                pltpu.SemaphoreType.DMA((segs + 6,)),
                pltpu.SemaphoreType.DMA((2 * templates,)),
            ],
        ),
        out_shape=jax.ShapeDtypeStruct((dev_count * rows, lanes + 2 * half_len), BF16),
        compiler_params=params(16),
        name="stage_one",
    )(
        order,
        *in_hbm(
            jnp.swapaxes(strain, 1, 2), jnp.swapaxes(analysis, 0, 1), spin, win_c, win_s,
            cos_one.astype(BF16), sin_one.astype(BF16), bank,
        ),
    )
    moved = lax.all_to_all(
        sent.reshape(dev_count, rows, lanes + 2 * half_len), "tmpl", split_axis=0, concat_axis=0, tiled=True
    )
    own = moved[:, :, lanes:]
    other = lax.ppermute(own, "grp", [(0, 1), (1, 0)])

    split = halves(half_len)
    low = 2 * np.arange(rows // 2)
    lift_rows = [np.concatenate([low + odd, first_len - low - odd]) for odd in range(2)]
    lift_init = [turns(at[:, None] * second[None, :], length) for at in lift_rows]
    mid_rows = lift_rows[0].copy()
    mid_rows[rows // 2] = first_len // 2
    step_sign = np.where(np.arange(rows) < rows // 2, rows, -rows)
    tables = [
        *turns(step[:, None] * split[None, :], second_len),
        *turns(STEP * split[None, :], second_len),
        *turns(2 * step[:, None] * half[None, :], second_len),
        *turns((2 * step[:, None] + 1) * half[None, :], second_len),
        *turns(2 * STEP * half[None, :], second_len),
        np.stack([lift_init[0][0], lift_init[1][0]]),
        np.stack([lift_init[0][1], lift_init[1][1]]),
        *turns(step_sign[:, None] * second[None, :], length),
        *turns(mid_rows[:, None] * second[None, :], length),
    ]
    shapes = [(second_len, second_len)] + [(half_len, second_len)] * 2 + [(first_len, second_len)] * 2
    forward, even_table, odd_table, lift_c, lift_s = pl.pallas_call(
        tables_kernel,
        out_shape=[pltpu.HBM(shape, BF16) for shape in shapes],
        in_specs=[whole()] * len(tables),
        out_specs=[outside()] * len(shapes),
        scratch_shapes=[*[vmem(shape) for shape in shapes], pltpu.SemaphoreType.DMA((len(shapes),))],
        compiler_params=params(24),
        cost_estimate=pl.CostEstimate(flops=10**7, bytes_accessed=2 * 10**7, transcendentals=0),
        name="tables",
    )(*in_hbm(*tables))

    near_c, near_s = turns(near[:, None] * second[None, :], length)
    base_c, base_s = turns(rows * devices[:, None, None] * second[None, None, :], length)
    mid_c, mid_s = turns(first_len // 2 * second[None, :], length)
    all_rows = 2 * (segs + 2) * rows
    stage_two = pl.pallas_call(
        functools.partial(stage_two_kernel, segs, cols),
        out_shape=jax.ShapeDtypeStruct((2 * rows, 3 * half_len), BF16),
        in_specs=[whole()] + [outside()] * 7,
        out_specs=whole(),
        scratch_shapes=[
            vmem((rows, second_len), F32),
            vmem((rows, second_len), F32),
            *[vmem((1, second_len), F32)] * 4,
            vmem(forward.shape),
            vmem((all_rows, second_len)),
            vmem((2 * rows, second_len), F32),
            pltpu.SemaphoreType.DMA((7,)),
        ],
        compiler_params=params(24),
        cost_estimate=pl.CostEstimate(flops=10**9, bytes_accessed=4 * 10**6, transcendentals=0),
        name="stage_two",
    )
    block = stage_two(moved, *in_hbm(near_c, near_s, base_c, base_s, mid_c, mid_s, forward))

    beside, one, two = swap_with(block, 2), swap_with(block, 4), swap_with(block, 12)
    both = swap_with(jnp.stack([one, two]), 2)
    far = swap_with(two, 4)
    last = swap_with(far, 2)
    mine = jnp.stack([block, beside, one, two, both[0], both[1], far, last])
    theirs = swap_with(mine, 1)

    choose = pl.pallas_call(
        choose_kernel,
        grid_spec=pltpu.PrefetchScalarGridSpec(
            num_scalar_prefetch=2,
            grid=(),
            in_specs=[whole()] * 2,
            out_specs=whole(),
            scratch_shapes=[vmem((first_len, 2 * half_len)), vmem((half_len, half_len))],
        ),
        out_shape=jax.ShapeDtypeStruct((first_len, 2 * half_len), BF16),
        compiler_params=params(16),
        cost_estimate=pl.CostEstimate(flops=10**9, bytes_accessed=4 * 10**6, transcendentals=0),
        name="choose",
    )
    chosen = choose(order, cutoff, own, other)

    per = first_len // 2
    cols_parts = []
    for odd in range(2):
        straight = devices[:, None] * rows + low[None, :] + odd
        turned = first_len - straight
        turned[straight == 0] = first_len // 2
        at = np.concatenate([straight, turned], 1).reshape(-1)
        cos, sin = turns(np.arange(per)[:, None] * at[None, :], first_len)
        cols_parts.append(np.block([[cos, -sin], [sin, cos]]))
    cols_table = jnp.asarray(np.concatenate(cols_parts, 1), BF16)
    return pl.pallas_call(
        inverse_kernel,
        out_shape=jax.ShapeDtypeStruct((1, first_len, second_len), BF16),
        in_specs=[whole()] * 8,
        out_specs=whole(),
        scratch_shapes=[vmem((first_len, 2 * half_len)), vmem((2 * first_len, second_len))],
        compiler_params=params(24),
        name="inverse",
    )(mine, theirs, chosen, even_table, odd_table, lift_c, lift_s, cols_table)


def angles(left_idx, right_idx, period):
    product = left_idx[:, None] * right_idx[None, :] % period
    phase_angle = product.astype(jnp.float32) * (2.0 * math.pi / period)
    return (jnp.cos(phase_angle), jnp.sin(phase_angle))


def filtered(white_pair, tmpl_pair, cut_bins, freq_bin):
    white_real = white_pair[0].astype(jnp.float32)
    white_imag = white_pair[1].astype(jnp.float32)
    tmpl_real = tmpl_pair[0].astype(jnp.float32)
    tmpl_imag = tmpl_pair[1].astype(jnp.float32)
    in_band = freq_bin[None] < cut_bins[:, None, None]
    filt_real = jnp.where(in_band, white_real * tmpl_real + white_imag * tmpl_imag, 0.0)
    filt_imag = jnp.where(in_band, white_imag * tmpl_real - white_real * tmpl_imag, 0.0)
    return jnp.concatenate([filt_real, filt_imag], -1).astype(jnp.bfloat16)


def inverse_rows(stacked, row_bins, second_len, length):
    half_len = second_len // 2
    cosine, sine = angles(
        jnp.arange(half_len, dtype=jnp.int32), jnp.arange(second_len, dtype=jnp.int32), second_len
    )
    dft_table = jnp.concatenate(
        [jnp.concatenate([cosine, sine], 1), jnp.concatenate([-sine, cosine], 1)], 0
    ).astype(jnp.bfloat16)
    spread = jnp.einsum("tkf,fg->tkg", stacked, dft_table, preferred_element_type=jnp.float32)
    spread_real = spread[..., :second_len]
    spread_imag = spread[..., second_len:]
    cos_twist, sin_twist = angles(row_bins, jnp.arange(second_len, dtype=jnp.int32), length)
    lift_real = spread_real * cos_twist - spread_imag * sin_twist
    lift_imag = spread_real * sin_twist + spread_imag * cos_twist
    return jnp.concatenate([lift_real, lift_imag], -1).astype(jnp.bfloat16)


def inverse_cols(lifted, first_len, second_len):
    row_idx = jnp.arange(first_len, dtype=jnp.int32)
    cosine, sine = angles(row_idx, row_idx, first_len)
    cosine = cosine.astype(jnp.bfloat16)
    sine = sine.astype(jnp.bfloat16)
    lift_real = lifted[..., :second_len]
    lift_imag = lifted[..., second_len:]
    field_real = jnp.einsum(
        "ak,tkb->tab", cosine, lift_real, preferred_element_type=jnp.float32
    ) - jnp.einsum("ak,tkb->tab", sine, lift_imag, preferred_element_type=jnp.float32)
    field_imag = jnp.einsum(
        "ak,tkb->tab", sine, lift_real, preferred_element_type=jnp.float32
    ) + jnp.einsum("ak,tkb->tab", cosine, lift_imag, preferred_element_type=jnp.float32)
    return (field_real, field_imag)


def plain_local(strain, analysis, bank, cutoff, order):
    highest = lax.Precision.HIGHEST
    dev_count = lax.axis_size("tmpl")
    my_index = lax.axis_index("tmpl")
    seg_count = strain.shape[0]
    first_len = strain.shape[1]
    col_count = strain.shape[2]
    second_len = col_count * dev_count
    length = first_len * second_len
    half_len = second_len // 2
    row_count = first_len // dev_count
    row_idx = jnp.arange(first_len, dtype=jnp.int32)
    col_index = my_index * col_count + jnp.arange(col_count, dtype=jnp.int32)
    sample_idx = row_idx[:, None] * second_len + col_index[None, :]
    window = (
        math.sqrt(8.0 / 3.0) * jnp.sin(sample_idx.astype(jnp.float32) * (math.pi / length)) ** 2
    )
    series = jnp.concatenate([strain * window, analysis[None]], 0)
    cos_one, sin_one = angles(row_idx, row_idx, first_len)
    part_real = jnp.einsum("ka,sab->skb", cos_one, series, precision=highest)
    part_imag = -jnp.einsum("ka,sab->skb", sin_one, series, precision=highest)
    cos_twist, sin_twist = angles(row_idx, col_index, length)
    twist_real = part_real * cos_twist + part_imag * sin_twist
    twist_imag = part_imag * cos_twist - part_real * sin_twist
    moved = lax.all_to_all(
        jnp.stack([twist_real, twist_imag]).astype(jnp.bfloat16),
        "tmpl",
        split_axis=2,
        concat_axis=3,
        tiled=True,
    ).astype(jnp.float32)
    cos_two, sin_two = angles(
        jnp.arange(second_len, dtype=jnp.int32), jnp.arange(half_len, dtype=jnp.int32), second_len
    )
    spec_real = jnp.einsum("skb,bf->skf", moved[0], cos_two, precision=highest) + jnp.einsum(
        "skb,bf->skf", moved[1], sin_two, precision=highest
    )
    spec_imag = jnp.einsum("skb,bf->skf", moved[1], cos_two, precision=highest) - jnp.einsum(
        "skb,bf->skf", moved[0], sin_two, precision=highest
    )
    power_spec = jnp.maximum(
        jnp.mean(spec_real[:seg_count] ** 2 + spec_imag[:seg_count] ** 2, axis=0), 0.2 * length
    )
    whitened = jnp.stack(
        [spec_real[seg_count] / power_spec, spec_imag[seg_count] / power_spec]
    ).astype(jnp.bfloat16)
    own_rows = my_index * row_count + jnp.arange(row_count, dtype=jnp.int32)
    half_idx = jnp.arange(half_len, dtype=jnp.int32)
    freq_local = own_rows[:, None] + first_len * half_idx[None, :]
    chosen = jnp.take(bank, order, axis=1)
    cuts = jnp.take(cutoff, order)
    bank_real = chosen[0].astype(jnp.float32)
    bank_imag = chosen[1].astype(jnp.float32)
    in_band = freq_local[None] < cuts[:, None, None]
    local_norm = jnp.sum(
        jnp.where(in_band, (bank_real**2 + bank_imag**2) / power_spec, 0.0), axis=(1, 2)
    )
    norm_sq = lax.psum(local_norm, "tmpl")
    per_device = cuts.shape[0] // dev_count
    own_norm = lax.dynamic_slice_in_dim(norm_sq, my_index * per_device, per_device)
    stacked = filtered(whitened, chosen, cuts, freq_local)
    lifted = lax.all_to_all(
        inverse_rows(stacked, own_rows, second_len, length),
        "tmpl",
        split_axis=0,
        concat_axis=1,
        tiled=True,
    )
    field_real, field_imag = inverse_cols(lifted, first_len, second_len)
    magnitude = jnp.sqrt(field_real**2 + field_imag**2)
    return (magnitude / jnp.sqrt(own_norm)[:, None, None]).astype(jnp.bfloat16)


def local(strain, analysis, bank, cutoff, order):
    dev_count, segs, cols = lax.axis_size("tmpl"), strain.shape[0], strain.shape[2]
    rows = strain.shape[1] // dev_count // 2
    fits = rows == STEP and cols == 64 and segs % 2 == 0 and dev_count == 2 * len(NEAR)
    if fits and order.shape[0] == dev_count and lax.axis_size("grp") == 2:
        return tiled_local(strain, analysis, bank, cutoff, order)
    return plain_local(strain, analysis, bank, cutoff, order)


def solution(mesh):
    return jax.shard_map(
        local,
        mesh=mesh,
        in_specs=(P("grp", None, "tmpl"), P("grp", "tmpl"), P(None, None, "tmpl", None), P(), P()),
        out_specs=P(("grp", "tmpl"), None, None),
        check_vma=False,
    )
```

```python
import functools
import math

import jax
import jax.numpy as jnp
import numpy as np
from jax import lax
from jax.experimental import pallas as pl
from jax.experimental.pallas import tpu as pltpu
from jax.sharding import PartitionSpec as P

BF16 = jnp.bfloat16
F32 = jnp.float32
STEP = 16
PIECE = 128
EARLY = (0, 2, 4, 8, 1, 3, 5, 9, 6, 10, 12)
LATE = (14, 7, 11, 13, 15)


def turns(product, period):
    angle = (product % period) * (2.0 * math.pi / period)
    return np.cos(angle).astype(np.float32), np.sin(angle).astype(np.float32)


def matmul(left, right):
    return jnp.dot(left, right, preferred_element_type=F32)


def matmul_nt(left, right):
    return lax.dot_general(left, right, (((1,), (1,)), ((), ())), preferred_element_type=F32)


def vmem(shape, dtype=BF16):
    return pltpu.VMEM(shape, dtype)


def whole():
    return pl.BlockSpec(memory_space=pltpu.VMEM)


def outside():
    return pl.BlockSpec(memory_space=pltpu.HBM)


def in_hbm(*arrays):
    return [pltpu.with_memory_space_constraint(jnp.asarray(array), pltpu.HBM) for array in arrays]


def in_vmem(*arrays):
    return [pltpu.with_memory_space_constraint(array, pltpu.VMEM) for array in arrays]


def position():
    return lax.axis_index("tmpl"), lax.axis_index("grp")


def start_copies(pairs, sems):
    copies = [
        pltpu.make_async_copy(source, target, sems.at[at]) for at, (source, target) in enumerate(pairs)
    ]
    for copy in copies:
        copy.start()
    return copies


def params(mib):
    return pltpu.CompilerParams(vmem_limit_bytes=mib << 20)


def halves(count):
    return np.concatenate([np.arange(0, count, 2), np.arange(1, count, 2)])


def aligned(start, size):
    return pl.ds(pl.multiple_of(start, size), size)


def stage_one_kernel(
    order_hbm, strain_hbm, analysis_hbm, spin_hbm, win_c_hbm, win_s_hbm, cos_hbm, sin_hbm, bank, out,
    order, strain, analysis, spin, win_c, win_s, cos, sin, packed, sems, bank_sems,
):
    segs, cols, _ = strain.shape
    tail = segs * cols
    templates, half_len = bank.shape[1], bank.shape[3]
    rows = out.shape[0] // templates
    place, group = position()
    sources = [
        (spin_hbm.at[place], spin),
        (win_c_hbm, win_c),
        (win_s_hbm, win_s),
        *[(strain_hbm.at[seg], strain.at[seg]) for seg in range(segs)],
        (analysis_hbm, analysis),
        (cos_hbm, cos),
        (sin_hbm, sin),
        (order_hbm, order),
    ]
    copies = start_copies(sources, sems)
    copies.pop().wait()
    lane = 2 * (tail + cols)
    bank_pairs = []
    for row in range(templates):
        for part in range(2):
            bank_pairs.append(
                (
                    bank.at[part, order[row], aligned(group * rows, rows), :],
                    out.at[
                        row * rows : (row + 1) * rows,
                        lane + part * half_len : lane + (part + 1) * half_len,
                    ],
                )
            )
    bank_copies = start_copies(bank_pairs, bank_sems)
    for copy in copies[:3]:
        copy.wait()
    scale = 0.5 * math.sqrt(8.0 / 3.0)
    window = scale - scale * (win_c[...] * spin[0:1, :] - win_s[...] * spin[1:2, :])
    for seg in range(segs):
        copies[3 + seg].wait()
        packed[seg * cols : (seg + 1) * cols, :] = (strain[seg] * window).astype(BF16)
    for copy in copies[3 + segs :]:
        copy.wait()
    packed[tail:, :] = analysis[...].astype(BF16)
    real = matmul_nt(cos[...], packed[...])
    imag = -matmul_nt(sin[...], packed[...])
    out[:, 0:tail] = real[:, :tail].astype(BF16)
    out[:, tail : 2 * tail] = imag[:, :tail].astype(BF16)
    joined = jnp.concatenate([real[:, tail:], imag[:, tail:]], 1)
    out[:, 2 * tail : lane] = joined.astype(BF16)
    for copy in bank_copies:
        copy.wait()


def turn(cos, sin, by_cos, by_sin):
    return cos * by_cos - sin * by_sin, sin * by_cos + cos * by_sin


def forward_kernel(
    fore_c, fore_s, fore_rc, fore_rs, near_c, near_s, base_c, base_s,
    forward_hbm, near_out_c, near_out_s, forward, sem,
):
    half_len = fore_c.shape[1]
    quarter = half_len // 2
    place, _ = position()
    first_lane = lax.broadcasted_iota(jnp.int32, fore_c.shape, 1) == 0
    sign = 1.0 - 2.0 * (lax.broadcasted_iota(jnp.int32, fore_c.shape, 0) % 2).astype(F32)

    def fore(step, carry):
        cos, sin = carry
        for part, table in enumerate((cos, jnp.where(first_lane, sign, sin))):
            for odd in range(2):
                lane = slice(odd * quarter, (odd + 1) * quarter)
                to = slice(part * quarter, (part + 1) * quarter)
                forward[odd, aligned(step * STEP, STEP), to] = table[:, lane].astype(BF16)
        return turn(cos, sin, fore_rc[...], fore_rs[...])

    lax.fori_loop(0, forward.shape[1] // STEP, fore, (fore_c[...], fore_s[...]))
    copy = pltpu.make_async_copy(forward, forward_hbm, sem)
    copy.start()
    near_out_c[...], near_out_s[...] = turn(near_c[...], near_s[...], base_c[place], base_s[place])
    copy.wait()


def inverse_tables_kernel(
    even_c, even_s, odd_c, odd_s, rows_rc, rows_rs, lift_c, lift_s, lift_rc, lift_rs, mid_c, mid_s,
    cols_c, cols_s, cols_rc, cols_rs,
    even_out, odd_out, lift_out_c, lift_out_s, cols_out, rows_out, bins_out,
):
    half_len = even_c.shape[1]
    quarter = half_len // 2
    first_len = cols_c.shape[1]
    per = first_len // 2

    def spread(out, cos, sin):
        def body(step, carry):
            cos, sin = carry
            upper = aligned(step * STEP, STEP)
            lower = aligned(quarter + step * STEP, STEP)
            for lane in range(0, half_len, PIECE):
                real, imag = slice(2 * lane, 2 * lane + PIECE), slice(2 * lane + PIECE, 2 * (lane + PIECE))
                cos_at, sin_at = cos[:, lane : lane + PIECE], sin[:, lane : lane + PIECE]
                out[upper, real] = cos_at.astype(BF16)
                out[upper, imag] = sin_at.astype(BF16)
                out[lower, real] = (-sin_at).astype(BF16)
                out[lower, imag] = cos_at.astype(BF16)
            return turn(cos, sin, rows_rc[...], rows_rs[...])

        lax.fori_loop(0, quarter // STEP, body, (cos, sin))

    spread(even_out, even_c[...], even_s[...])
    spread(odd_out, odd_c[...], odd_s[...])

    for parity in range(2):

        def lifts(step, carry, parity=parity):
            cos, sin = carry
            at = aligned(parity * per + step * STEP, STEP)
            lift_out_c[at, :] = cos
            lift_out_s[at, :] = sin
            return turn(cos, sin, lift_rc[...], lift_rs[...])

        lax.fori_loop(0, per // STEP, lifts, (lift_c[parity], lift_s[parity]))
    lift_out_c[0:STEP, :] = mid_c[...]
    lift_out_s[0:STEP, :] = mid_s[...]

    def columns(step, carry):
        cos, sin = carry
        upper = aligned(step * STEP, STEP)
        lower = aligned(per + step * STEP, STEP)
        for parity in range(2):
            at = slice(parity * per, (parity + 1) * per)
            left = slice(parity * first_len, parity * first_len + per)
            right = slice(parity * first_len + per, (parity + 1) * first_len)
            cols_out[upper, left] = cos[:, at].astype(BF16)
            cols_out[upper, right] = (-sin[:, at]).astype(BF16)
            cols_out[lower, left] = sin[:, at].astype(BF16)
            cols_out[lower, right] = cos[:, at].astype(BF16)
        return turn(cos, sin, cols_rc[...], cols_rs[...])

    lax.fori_loop(0, per // STEP, columns, (cols_c[...], cols_s[...]))
    sort_tables(lift_c.shape[1], rows_out, bins_out)


def stage_two_kernel(
    segs, cols, moved, near_c, near_s, mid_c_hbm, mid_s_hbm, forward_hbm, out,
    mid_c, mid_s, forward, stacked, middle, product, sems,
):
    place, _ = position()
    _, second_len, half_len = forward.shape
    quarter = half_len // 2
    pieces = [(forward_hbm.at[odd], forward.at[odd]) for odd in range(2)]
    pieces += [(mid_c_hbm, mid_c), (mid_s_hbm, mid_s)]
    copies = start_copies(pieces, sems)
    sources, rows, _ = moved.shape
    tail = segs * cols
    all_rows = (segs + 1) * rows
    width = 2 * cols
    low = lax.broadcasted_iota(jnp.int32, (rows, width), 1) < cols
    own_first = place == 0
    packed_row = lax.broadcasted_iota(jnp.int32, (rows, width), 0) == 0
    drop = jnp.logical_and(packed_row, own_first)

    def pair(left, right):
        return (
            jnp.where(low, left, pltpu.roll(right, cols, 1)),
            jnp.where(low, pltpu.roll(left, cols, 1), right),
        )

    middle[...] = jnp.zeros_like(middle)
    for tile in range(sources // 2):
        lane = slice(tile * width, (tile + 1) * width)
        cos, sin = near_c[:, lane], near_s[:, lane]

        def piece(lo, tile=tile):
            hi = lo + width
            return pair(
                moved[2 * tile, :, lo:hi].astype(F32), moved[2 * tile + 1, :, lo:hi].astype(F32)
            )

        def put(seg, real, imag, lane=lane, cos=cos, sin=sin):
            middle[seg : seg + 1, lane] = imag[0:1, :]
            imag = jnp.where(drop, 0.0, imag)
            at = seg * rows
            stacked[at : at + rows, lane] = (real * cos + imag * sin).astype(BF16)
            at += all_rows
            stacked[at : at + rows, lane] = (imag * cos - real * sin).astype(BF16)

        for twin in range(segs // 2):
            real_one, real_two = piece(twin * width)
            imag_one, imag_two = piece(tail + twin * width)
            put(2 * twin, real_one, imag_one)
            put(2 * twin + 1, real_two, imag_two)
        real, imag = piece(2 * tail)
        put(segs, real, imag)
    for copy in copies[2:]:
        copy.wait()
    stacked[2 * all_rows : 2 * all_rows + rows, :] = (middle[...] * mid_c[...]).astype(BF16)
    stacked[2 * all_rows + rows :, :] = (middle[...] * -mid_s[...]).astype(BF16)

    first_lane = lax.broadcasted_iota(jnp.int32, (rows, quarter), 1) == 0
    swap = jnp.logical_and(lax.broadcasted_iota(jnp.int32, (rows, quarter), 0) == 0, own_first)
    floor = 0.2 * (second_len * 2 * sources * rows)
    upper, lower = [], []
    for odd in range(2):
        cos_at = slice(odd * half_len, odd * half_len + quarter)
        sin_at = slice(odd * half_len + quarter, (odd + 1) * half_len)
        copies[odd].wait()
        product[:, odd * half_len : (odd + 1) * half_len] = matmul(stacked[...], forward[odd])

        def parts(at, lower_at, cos_at=cos_at, sin_at=sin_at):
            return (
                product[at : at + rows, cos_at],
                product[at : at + rows, sin_at],
                product[lower_at : lower_at + rows, cos_at],
                product[lower_at : lower_at + rows, sin_at],
            )

        def direct_of(rc, rs, ic, imag_s, odd=odd):
            if not odd:
                rs, imag_s = jnp.where(first_lane, 0.0, rs), jnp.where(first_lane, 0.0, imag_s)
            return rc + imag_s, ic - rs

        def mirror_of(rc, rs, ic, imag_s, odd=odd):
            real, imag = rc - imag_s, ic + rs
            if not odd:
                real, imag = jnp.where(first_lane, rs, real), jnp.where(first_lane, imag_s, imag)
            return real, imag

        level = jnp.zeros((rows, quarter), F32)
        mirror_level = level
        for seg in range(segs):
            four = parts(seg * rows, all_rows + seg * rows)
            real, imag = direct_of(*four)
            level = level + (real * real + imag * imag)
            real, imag = mirror_of(*four)
            mirror_level = mirror_level + (real * real + imag * imag)
        four = parts(segs * rows, all_rows + segs * rows)
        real, imag = direct_of(*four)
        mirror_real, mirror_imag = mirror_of(*four)
        mid_real, mid_imag = mirror_of(*parts(2 * all_rows, 2 * all_rows + rows))
        mid_level = jnp.sum((mid_real * mid_real + mid_imag * mid_imag)[:segs], 0, keepdims=True)
        mirror_level = jnp.where(swap, mid_level, mirror_level)
        mirror_real = jnp.where(swap, mid_real[segs : segs + 1], mirror_real)
        mirror_imag = jnp.where(swap, mid_imag[segs : segs + 1], mirror_imag)
        level = jnp.maximum(level * (1.0 / segs), floor)
        mirror_level = jnp.maximum(mirror_level * (1.0 / segs), floor)
        upper.append((real / level, imag / level, 1.0 / level))
        lower.append((mirror_real / mirror_level, -mirror_imag / mirror_level, 1.0 / mirror_level))
    eighth = rows // 2
    for part in range(3):
        mirrored = (lower[1][part], pltpu.roll(lower[0][part], quarter - 1, 1))
        for odd in range(2):
            lane = slice(part * half_len + odd * quarter, part * half_len + (odd + 1) * quarter)
            for parity in range(2):
                at = slice(parity * eighth, (parity + 1) * eighth)
                block = jnp.concatenate([upper[odd][part][at], mirrored[odd][at]], 0)
                out[parity * rows : (parity + 1) * rows, lane] = block.astype(BF16)


def sort_tables(rows, rows_out, bins_out):
    first_len, half_len = rows_out.shape[0], bins_out.shape[0]
    per = first_len // 2
    _, group = position()
    deep = 128

    def one_hot(mask):
        return jnp.where(mask, 1.0, 0.0).astype(BF16)

    def body(step, carry):
        at = aligned(step * deep, deep)
        row = packed_row_of(step * deep + lax.broadcasted_iota(jnp.int32, (deep, first_len), 0), first_len, rows)
        share = (row // rows) % 2
        column = (row // (2 * rows)) * rows + row % rows + jnp.where(share == group, 0, per)
        rows_out[at, :] = one_hot(column == lax.broadcasted_iota(jnp.int32, (deep, first_len), 1))
        return carry

    lax.fori_loop(0, first_len // deep, body, 0)

    def bins(step, carry):
        row = step * deep + lax.broadcasted_iota(jnp.int32, (deep, half_len), 0)
        lane = lax.broadcasted_iota(jnp.int32, (deep, half_len), 1)
        bins_out[aligned(step * deep, deep), :] = one_hot(row == bin_of(lane, half_len))
        return carry

    lax.fori_loop(0, half_len // deep, bins, 0)


def bin_of(lane, half_len):
    return jnp.where(lane < half_len // 2, 2 * lane, 2 * lane - half_len + 1)


def packed_row_of(at, first_len, rows):
    per = first_len // 2
    packed = (at % per) // rows * rows + 2 * (at % (rows // 2)) + at // per
    turned = jnp.where(packed == 0, first_len // 2, first_len - packed)
    return jnp.where(at % rows >= rows // 2, turned, packed)


def choose_kernel(order, cuts, own, other, by_rows, by_bins, out, held):
    place, _ = position()
    rows, sources = own.shape[1], own.shape[0]
    per = sources * rows
    first_len, half_len = 2 * per, own.shape[2] // 2
    for source in range(sources):
        held[source * rows : (source + 1) * rows, :] = own[source]
        held[per + source * rows : per + (source + 1) * rows, :] = other[source]
    picked = matmul(by_rows[...], held[...]).astype(BF16)
    at = lax.broadcasted_iota(jnp.int32, (first_len, 128), 0)
    room = cuts[order[place]] - packed_row_of(at, first_len, rows)
    for part in range(2):
        moved = matmul(picked[:, part * half_len : (part + 1) * half_len], by_bins[...])
        for lane in range(0, half_len, 128):
            bins = bin_of(lane + lax.broadcasted_iota(jnp.int32, (1, 128), 1), half_len)
            kept = jnp.where(first_len * bins < room, moved[:, lane : lane + 128], 0.0)
            out[:, part * half_len + lane : part * half_len + lane + 128] = kept.astype(BF16)


def filter_blocks(offsets, blocks, chosen, tables, norm, filtered, lifted):
    place, _ = position()
    even_table, odd_table, lift_c, lift_s = tables
    half_len = even_table.shape[0]
    quarter = half_len // 2
    first_len = chosen.shape[0]
    per = first_len // 2
    rows = blocks[0].shape[0] // 2
    groups = []
    for block, offset in zip(blocks, offsets):
        device = jnp.bitwise_xor(place, offset)
        for parity in range(2):
            row = slice(parity * rows, (parity + 1) * rows)
            at = aligned(parity * per + device * rows, rows)
            white_real = block[row, :half_len].astype(F32)
            white_imag = block[row, half_len : 2 * half_len].astype(F32)
            weight = block[row, 2 * half_len :].astype(F32)
            real = chosen[at, :half_len].astype(F32)
            imag = chosen[at, half_len:].astype(F32)
            norm = norm + (real * real + imag * imag) * weight
            filt_real = (white_real * real + white_imag * imag).astype(BF16)
            filt_imag = (white_imag * real - white_real * imag).astype(BF16)
            to = slice(len(groups) * rows, (len(groups) + 1) * rows)
            filtered[to, 0:quarter] = filt_real[:, :quarter]
            filtered[to, quarter:half_len] = filt_imag[:, :quarter]
            filtered[to, half_len : half_len + quarter] = filt_real[:, quarter:]
            filtered[to, half_len + quarter :] = filt_imag[:, quarter:]
            groups.append((to, at, parity * first_len + device * rows))
    for lane in range(0, half_len, PIECE):
        both = slice(2 * lane, 2 * (lane + PIECE))
        even = matmul(filtered[:, :half_len], even_table[:, both])
        odd = matmul(filtered[:, half_len:], odd_table[:, both])
        for upper in range(2):
            lanes = slice(upper * half_len + lane, upper * half_len + lane + PIECE)
            total = even - odd if upper else even + odd
            for row, at, target in groups:
                real, imag = total[row, :PIECE], total[row, PIECE:]
                cos, sin = lift_c[at, lanes], lift_s[at, lanes]
                lifted[aligned(target, rows), lanes] = (real * cos - imag * sin).astype(BF16)
                lifted[aligned(target + per, rows), lanes] = (real * sin + imag * cos).astype(BF16)
    return norm


def early_kernel(near, theirs, both, far, chosen, *refs):
    tables, (lifted, norm, filtered) = refs[:4], refs[4:]
    blocks = [*[near.at[at] for at in range(4)], *[theirs.at[at] for at in range(4)], both.at[0], both.at[1], far]
    zero = jnp.zeros(norm.shape, F32)
    norm[...] = filter_blocks(EARLY, blocks, chosen, tables, zero, filtered, lifted)


def late_kernel(last, theirs, early, early_norm, chosen, *refs):
    tables, (cols_table, out, lifted, filtered) = refs[:4], refs[4:]
    blocks = [last, *[theirs.at[at] for at in range(4)]]
    norm = filter_blocks(LATE, blocks, chosen, tables, early_norm[...], filtered, lifted)
    scale = lax.rsqrt(jnp.sum(norm, keepdims=True))
    first_len = chosen.shape[0]
    per = first_len // 2
    wide = 256
    for lane in range(0, lifted.shape[1], wide):
        at = slice(lane, lane + wide)
        even = matmul(cols_table[:, :first_len], lifted[:first_len, at])
        odd = matmul(cols_table[:, first_len:], lifted[first_len:, at])
        for upper in range(2):
            total = even - odd if upper else even + odd
            power = total[:per] * total[:per] + total[per:] * total[per:]
            size = power * lax.rsqrt(jnp.maximum(power, 1e-37))
            out[0, upper * per : (upper + 1) * per, at] = (size * scale).astype(BF16)


def swap_with(array, flip):
    pairs = [(at, at ^ flip) for at in range(lax.axis_size("tmpl"))]
    return lax.ppermute(array, "tmpl", pairs)


def tiled_local(strain, analysis, bank, cutoff, order):
    dev_count = lax.axis_size("tmpl")
    segs, first_len, cols = strain.shape
    second_len = cols * dev_count
    length = first_len * second_len
    half_len = second_len // 2
    rows = first_len // dev_count // 2
    templates = order.shape[0]
    lanes = 2 * (segs + 1) * cols

    first, second, half = np.arange(first_len), np.arange(second_len), np.arange(half_len)
    devices, step = np.arange(dev_count), np.arange(STEP)
    near = halves(rows)
    packed = (devices[:, None] * rows + near[None, :]).reshape(-1, 1)
    cos_one, sin_one = turns(packed * first[None, :], first_len)
    sin_one[0] = 2 * (first % 2) - 1.0
    win_c, win_s = turns(np.arange(cols)[:, None] + second_len * first[None, :], length)
    spin = np.stack(turns(cols * devices, length), 1)[:, :, None] * np.ones((1, 1, first_len), np.float32)

    sent = pl.pallas_call(
        stage_one_kernel,
        in_specs=[outside()] * 9,
        out_specs=whole(),
        scratch_shapes=[
            pltpu.SMEM((templates,), jnp.int32),
            vmem((segs, cols, first_len), F32),
            vmem((cols, first_len), F32),
            vmem((2, first_len), F32),
            vmem((cols, first_len), F32),
            vmem((cols, first_len), F32),
            vmem((dev_count * rows, first_len)),
            vmem((dev_count * rows, first_len)),
            vmem(((segs + 1) * cols, first_len)),
            pltpu.SemaphoreType.DMA((segs + 7,)),
            pltpu.SemaphoreType.DMA((2 * templates,)),
        ],
        out_shape=pltpu.VMEM((dev_count * rows, lanes + 2 * half_len), BF16),
        compiler_params=params(16),
        name="stage_one",
    )(
        *in_hbm(
            order, jnp.swapaxes(strain, 1, 2), jnp.swapaxes(analysis, 0, 1), spin, win_c, win_s,
            cos_one.astype(BF16), sin_one.astype(BF16), bank,
        ),
    )
    moved = lax.all_to_all(
        sent.reshape(dev_count, rows, lanes + 2 * half_len), "tmpl", split_axis=0, concat_axis=0, tiled=True
    )
    own = moved[:, :, lanes:]
    other = lax.ppermute(own, "grp", [(0, 1), (1, 0)])

    split = halves(half_len)
    low = 2 * np.arange(rows // 2)
    lift_rows = [np.concatenate([low + odd, first_len - low - odd]) for odd in range(2)]
    lift_init = [turns(at[:, None] * second[None, :], length) for at in lift_rows]
    cols_parts = []
    for odd in range(2):
        straight = devices[:, None] * rows + low[None, :] + odd
        turned = np.where(straight == 0, first_len // 2, first_len - straight)
        cols_parts.append(np.concatenate([straight, turned], 1).reshape(-1))
    cols_rows = np.concatenate(cols_parts)
    mid_rows = lift_rows[0].copy()
    mid_rows[rows // 2] = first_len // 2
    step_sign = np.where(np.arange(rows) < rows // 2, rows, -rows)
    fore = [
        *turns(step[:, None] * split[None, :], second_len),
        *turns(STEP * split[None, :], second_len),
        *turns(near[:, None] * second[None, :], length),
        *turns(rows * devices[:, None, None] * second[None, None, :], length),
    ]
    forward, near_c, near_s = pl.pallas_call(
        forward_kernel,
        out_shape=[
            pltpu.HBM((2, second_len, half_len), BF16),
            *[pltpu.VMEM((rows, second_len), F32)] * 2,
        ],
        in_specs=[whole()] * len(fore),
        out_specs=[outside()] + [whole()] * 2,
        scratch_shapes=[vmem((2, second_len, half_len)), pltpu.SemaphoreType.DMA],
        compiler_params=params(16),
        cost_estimate=pl.CostEstimate(flops=10**7, bytes_accessed=2 * 10**7, transcendentals=0),
        name="forward_tables",
    )(*in_hbm(*fore))
    back = [
        *turns(2 * step[:, None] * half[None, :], second_len),
        *turns((2 * step[:, None] + 1) * half[None, :], second_len),
        *turns(2 * STEP * half[None, :], second_len),
        np.stack([lift_init[0][0], lift_init[1][0]]),
        np.stack([lift_init[0][1], lift_init[1][1]]),
        *turns(step_sign[:, None] * second[None, :], length),
        *turns(mid_rows[:, None] * second[None, :], length),
        *turns(step[:, None] * cols_rows[None, :], first_len),
        *turns(STEP * cols_rows[None, :], first_len),
    ]
    shapes = [
        ((half_len, second_len), BF16),
        ((half_len, second_len), BF16),
        ((first_len, second_len), F32),
        ((first_len, second_len), F32),
        ((first_len, 2 * first_len), BF16),
        ((first_len, first_len), BF16),
        ((half_len, half_len), BF16),
    ]
    inverse_tables = pl.pallas_call(
        inverse_tables_kernel,
        out_shape=[pltpu.VMEM(*shape) for shape in shapes],
        in_specs=[whole()] * len(back),
        out_specs=[whole()] * len(shapes),
        compiler_params=params(8),
        cost_estimate=pl.CostEstimate(flops=10**7, bytes_accessed=2 * 10**7, transcendentals=0),
        name="inverse_tables",
    )
    even_table, odd_table, lift_c, lift_s, cols_table, by_rows, by_bins = inverse_tables(*in_hbm(*back))

    mid_c, mid_s = turns(first_len // 2 * second[None, :], length)
    all_rows = 2 * (segs + 2) * rows
    stage_two = pl.pallas_call(
        functools.partial(stage_two_kernel, segs, cols),
        out_shape=jax.ShapeDtypeStruct((2 * rows, 3 * half_len), BF16),
        in_specs=[whole()] * 3 + [outside()] * 3,
        out_specs=whole(),
        scratch_shapes=[
            *[vmem((1, second_len), F32)] * 2,
            vmem(forward.shape),
            vmem((all_rows, second_len)),
            vmem((rows, second_len), F32),
            vmem((all_rows, second_len), F32),
            pltpu.SemaphoreType.DMA((4,)),
        ],
        compiler_params=params(24),
        cost_estimate=pl.CostEstimate(flops=10**9, bytes_accessed=4 * 10**6, transcendentals=0),
        name="stage_two",
    )
    block = stage_two(moved, *in_vmem(near_c, near_s), *in_hbm(mid_c, mid_s, forward))

    two = swap_with(block, 8)
    one = swap_with(block, 4)
    beside = swap_with(block, 2)
    both = swap_with(jnp.stack([one, two]), 2)
    far = swap_with(two, 4)
    near = jnp.stack([block, beside, one, two])
    theirs = swap_with(near, 1)
    last = swap_with(far, 2)
    late = swap_with(jnp.stack([both[0], both[1], far, last]), 1)

    choose = pl.pallas_call(
        choose_kernel,
        grid_spec=pltpu.PrefetchScalarGridSpec(
            num_scalar_prefetch=2,
            grid=(),
            in_specs=[whole()] * 4,
            out_specs=whole(),
            scratch_shapes=[vmem((first_len, 2 * half_len))],
        ),
        out_shape=jax.ShapeDtypeStruct((first_len, 2 * half_len), BF16),
        compiler_params=params(16),
        cost_estimate=pl.CostEstimate(flops=10**9, bytes_accessed=4 * 10**6, transcendentals=0),
        name="choose",
    )
    chosen = choose(order, cutoff, own, other, *in_vmem(by_rows, by_bins))

    spread = [(2 * first_len, second_len), BF16]
    tables = in_vmem(even_table, odd_table, lift_c, lift_s)
    early = pl.pallas_call(
        early_kernel,
        out_shape=[pltpu.VMEM(*spread), pltpu.VMEM((rows, half_len), F32)],
        in_specs=[whole()] * 9,
        out_specs=[whole()] * 2,
        scratch_shapes=[vmem((len(EARLY) * 2 * rows, 2 * half_len))],
        compiler_params=params(16),
        cost_estimate=pl.CostEstimate(flops=10**9, bytes_accessed=4 * 10**6, transcendentals=0),
        name="early",
    )
    lifted, norm = early(near, theirs, both, far, chosen, *tables)
    result, _ = pl.pallas_call(
        late_kernel,
        out_shape=[jax.ShapeDtypeStruct((1, first_len, second_len), BF16), pltpu.VMEM(*spread)],
        in_specs=[whole()] * 10,
        out_specs=[whole()] * 2,
        scratch_shapes=[vmem((len(LATE) * 2 * rows, 2 * half_len))],
        input_output_aliases={2: 1},
        compiler_params=params(16),
        name="late",
    )(last, late, *in_vmem(lifted, norm), chosen, *tables, *in_vmem(cols_table))
    return result


def angles(left_idx, right_idx, period):
    product = left_idx[:, None] * right_idx[None, :] % period
    phase_angle = product.astype(jnp.float32) * (2.0 * math.pi / period)
    return (jnp.cos(phase_angle), jnp.sin(phase_angle))


def filtered(white_pair, tmpl_pair, cut_bins, freq_bin):
    white_real = white_pair[0].astype(jnp.float32)
    white_imag = white_pair[1].astype(jnp.float32)
    tmpl_real = tmpl_pair[0].astype(jnp.float32)
    tmpl_imag = tmpl_pair[1].astype(jnp.float32)
    in_band = freq_bin[None] < cut_bins[:, None, None]
    filt_real = jnp.where(in_band, white_real * tmpl_real + white_imag * tmpl_imag, 0.0)
    filt_imag = jnp.where(in_band, white_imag * tmpl_real - white_real * tmpl_imag, 0.0)
    return jnp.concatenate([filt_real, filt_imag], -1).astype(jnp.bfloat16)


def inverse_rows(stacked, row_bins, second_len, length):
    half_len = second_len // 2
    cosine, sine = angles(
        jnp.arange(half_len, dtype=jnp.int32), jnp.arange(second_len, dtype=jnp.int32), second_len
    )
    dft_table = jnp.concatenate(
        [jnp.concatenate([cosine, sine], 1), jnp.concatenate([-sine, cosine], 1)], 0
    ).astype(jnp.bfloat16)
    spread = jnp.einsum("tkf,fg->tkg", stacked, dft_table, preferred_element_type=jnp.float32)
    spread_real = spread[..., :second_len]
    spread_imag = spread[..., second_len:]
    cos_twist, sin_twist = angles(row_bins, jnp.arange(second_len, dtype=jnp.int32), length)
    lift_real = spread_real * cos_twist - spread_imag * sin_twist
    lift_imag = spread_real * sin_twist + spread_imag * cos_twist
    return jnp.concatenate([lift_real, lift_imag], -1).astype(jnp.bfloat16)


def inverse_cols(lifted, first_len, second_len):
    row_idx = jnp.arange(first_len, dtype=jnp.int32)
    cosine, sine = angles(row_idx, row_idx, first_len)
    cosine = cosine.astype(jnp.bfloat16)
    sine = sine.astype(jnp.bfloat16)
    lift_real = lifted[..., :second_len]
    lift_imag = lifted[..., second_len:]
    field_real = jnp.einsum(
        "ak,tkb->tab", cosine, lift_real, preferred_element_type=jnp.float32
    ) - jnp.einsum("ak,tkb->tab", sine, lift_imag, preferred_element_type=jnp.float32)
    field_imag = jnp.einsum(
        "ak,tkb->tab", sine, lift_real, preferred_element_type=jnp.float32
    ) + jnp.einsum("ak,tkb->tab", cosine, lift_imag, preferred_element_type=jnp.float32)
    return (field_real, field_imag)


def plain_local(strain, analysis, bank, cutoff, order):
    highest = lax.Precision.HIGHEST
    dev_count = lax.axis_size("tmpl")
    my_index = lax.axis_index("tmpl")
    seg_count = strain.shape[0]
    first_len = strain.shape[1]
    col_count = strain.shape[2]
    second_len = col_count * dev_count
    length = first_len * second_len
    half_len = second_len // 2
    row_count = first_len // dev_count
    row_idx = jnp.arange(first_len, dtype=jnp.int32)
    col_index = my_index * col_count + jnp.arange(col_count, dtype=jnp.int32)
    sample_idx = row_idx[:, None] * second_len + col_index[None, :]
    window = (
        math.sqrt(8.0 / 3.0) * jnp.sin(sample_idx.astype(jnp.float32) * (math.pi / length)) ** 2
    )
    series = jnp.concatenate([strain * window, analysis[None]], 0)
    cos_one, sin_one = angles(row_idx, row_idx, first_len)
    part_real = jnp.einsum("ka,sab->skb", cos_one, series, precision=highest)
    part_imag = -jnp.einsum("ka,sab->skb", sin_one, series, precision=highest)
    cos_twist, sin_twist = angles(row_idx, col_index, length)
    twist_real = part_real * cos_twist + part_imag * sin_twist
    twist_imag = part_imag * cos_twist - part_real * sin_twist
    moved = lax.all_to_all(
        jnp.stack([twist_real, twist_imag]).astype(jnp.bfloat16),
        "tmpl",
        split_axis=2,
        concat_axis=3,
        tiled=True,
    ).astype(jnp.float32)
    cos_two, sin_two = angles(
        jnp.arange(second_len, dtype=jnp.int32), jnp.arange(half_len, dtype=jnp.int32), second_len
    )
    spec_real = jnp.einsum("skb,bf->skf", moved[0], cos_two, precision=highest) + jnp.einsum(
        "skb,bf->skf", moved[1], sin_two, precision=highest
    )
    spec_imag = jnp.einsum("skb,bf->skf", moved[1], cos_two, precision=highest) - jnp.einsum(
        "skb,bf->skf", moved[0], sin_two, precision=highest
    )
    power_spec = jnp.maximum(
        jnp.mean(spec_real[:seg_count] ** 2 + spec_imag[:seg_count] ** 2, axis=0), 0.2 * length
    )
    whitened = jnp.stack(
        [spec_real[seg_count] / power_spec, spec_imag[seg_count] / power_spec]
    ).astype(jnp.bfloat16)
    own_rows = my_index * row_count + jnp.arange(row_count, dtype=jnp.int32)
    half_idx = jnp.arange(half_len, dtype=jnp.int32)
    freq_local = own_rows[:, None] + first_len * half_idx[None, :]
    chosen = jnp.take(bank, order, axis=1)
    cuts = jnp.take(cutoff, order)
    bank_real = chosen[0].astype(jnp.float32)
    bank_imag = chosen[1].astype(jnp.float32)
    in_band = freq_local[None] < cuts[:, None, None]
    local_norm = jnp.sum(
        jnp.where(in_band, (bank_real**2 + bank_imag**2) / power_spec, 0.0), axis=(1, 2)
    )
    norm_sq = lax.psum(local_norm, "tmpl")
    per_device = cuts.shape[0] // dev_count
    own_norm = lax.dynamic_slice_in_dim(norm_sq, my_index * per_device, per_device)
    stacked = filtered(whitened, chosen, cuts, freq_local)
    lifted = lax.all_to_all(
        inverse_rows(stacked, own_rows, second_len, length),
        "tmpl",
        split_axis=0,
        concat_axis=1,
        tiled=True,
    )
    field_real, field_imag = inverse_cols(lifted, first_len, second_len)
    magnitude = jnp.sqrt(field_real**2 + field_imag**2)
    return (magnitude / jnp.sqrt(own_norm)[:, None, None]).astype(jnp.bfloat16)


def local(strain, analysis, bank, cutoff, order):
    dev_count, segs, cols = lax.axis_size("tmpl"), strain.shape[0], strain.shape[2]
    rows = strain.shape[1] // dev_count // 2
    fits = rows == STEP and cols == 64 and segs % 2 == 0 and dev_count == len(EARLY + LATE)
    if fits and order.shape[0] == dev_count and lax.axis_size("grp") == 2:
        return tiled_local(strain, analysis, bank, cutoff, order)
    return plain_local(strain, analysis, bank, cutoff, order)


def solution(mesh):
    return jax.shard_map(
        local,
        mesh=mesh,
        in_specs=(P("grp", None, "tmpl"), P("grp", "tmpl"), P(None, None, "tmpl", None), P(), P()),
        out_specs=P(("grp", "tmpl"), None, None),
        check_vma=False,
    )
```

```python
import functools
import math

import jax
import jax.numpy as jnp
import numpy as np
from jax import lax
from jax.experimental import pallas as pl
from jax.experimental.pallas import tpu as pltpu
from jax.sharding import PartitionSpec as P

BF16 = jnp.bfloat16
F32 = jnp.float32
STEP = 16
PIECE = 128
EARLY = (0, 2, 4, 8, 1, 3, 5, 9, 6, 10, 12)
MIDDLE = (7, 11, 13)
LATE = (14, 15)


def turns(product, period):
    angle = (product % period) * (2.0 * math.pi / period)
    return np.cos(angle).astype(np.float32), np.sin(angle).astype(np.float32)


def matmul(left, right):
    return jnp.dot(left, right, preferred_element_type=F32)


def matmul_nt(left, right):
    return lax.dot_general(left, right, (((1,), (1,)), ((), ())), preferred_element_type=F32)


def vmem(shape, dtype=BF16):
    return pltpu.VMEM(shape, dtype)


def whole():
    return pl.BlockSpec(memory_space=pltpu.VMEM)


def outside():
    return pl.BlockSpec(memory_space=pltpu.HBM)


def in_hbm(*arrays):
    return [pltpu.with_memory_space_constraint(jnp.asarray(array), pltpu.HBM) for array in arrays]


def in_vmem(*arrays):
    return [pltpu.with_memory_space_constraint(array, pltpu.VMEM) for array in arrays]


def position():
    return lax.axis_index("tmpl"), lax.axis_index("grp")


def start_copies(pairs, sems):
    copies = [
        pltpu.make_async_copy(source, target, sems.at[at]) for at, (source, target) in enumerate(pairs)
    ]
    for copy in copies:
        copy.start()
    return copies


def params(mib):
    return pltpu.CompilerParams(vmem_limit_bytes=mib << 20)


def turn(cos, sin, by_cos, by_sin):
    return cos * by_cos - sin * by_sin, sin * by_cos + cos * by_sin


def halves(count):
    return np.concatenate([np.arange(0, count, 2), np.arange(1, count, 2)])


def aligned(start, size):
    return pl.ds(pl.multiple_of(start, size), size)


def stage_one_kernel(
    turns_of_eight, order_hbm, strain_hbm, analysis_hbm, spin_hbm, win_hbm, wave_hbm, bank, out,
    order, strain, analysis, spin, win, wave, packed, sems, bank_sems,
):
    segs, cols, first_len = strain.shape
    tail = segs * cols
    templates, half_len = bank.shape[1], bank.shape[3]
    rows = out.shape[0] // templates
    half = first_len // 2
    place, group = position()
    sources = [
        (order_hbm, order),
        (spin_hbm.at[place], spin),
        (win_hbm, win),
        *[(strain_hbm.at[seg], strain.at[seg]) for seg in range(segs)],
        (analysis_hbm, analysis),
        (wave_hbm, wave),
    ]
    copies = start_copies(sources, sems)
    lane = 2 * (tail + cols)
    for copy in copies[:3]:
        copy.wait()
    bank_pairs = []
    for row in range(templates):
        for part in range(2):
            bank_pairs.append(
                (
                    bank.at[part, order[row], aligned(group * rows, rows), :],
                    out.at[
                        row * rows : (row + 1) * rows,
                        lane + part * half_len : lane + (part + 1) * half_len,
                    ],
                )
            )
    bank_copies = start_copies(bank_pairs, bank_sems)
    scale = 0.5 * math.sqrt(8.0 / 3.0)
    win_c, win_s = turn(win[0], win[1], spin[0:1, :], spin[1:2, :])
    window = jnp.concatenate(
        [scale - (win_c * (scale * by_cos) - win_s * (scale * by_sin)) for by_cos, by_sin in turns_of_eight], 0
    )

    def pack(at, values):
        packed[0, at : at + cols, :] = (values[:, :half] + values[:, half:]).astype(BF16)
        packed[1, at : at + cols, :] = (values[:, :half] - values[:, half:]).astype(BF16)

    for seg in range(segs):
        copies[3 + seg].wait()
        pack(seg * cols, strain[seg] * window)
    copies[3 + segs].wait()
    pack(tail, analysis[...])
    copies[4 + segs].wait()
    both = [matmul_nt(wave[odd], packed[odd]) for odd in range(2)]
    count = out.shape[0] // 2

    def woven(part):
        halves_of = [
            table[part * count : (part + 1) * count].reshape(templates, rows // 2, tail + cols) for table in both
        ]
        return jnp.concatenate(halves_of, 1).reshape(2 * count, tail + cols)

    real, imag = woven(0), woven(1)
    out[:, 0:tail] = real[:, :tail].astype(BF16)
    out[:, tail : 2 * tail] = imag[:, :tail].astype(BF16)
    joined = jnp.concatenate([real[:, tail:], imag[:, tail:]], 1)
    out[:, 2 * tail : lane] = joined.astype(BF16)
    for copy in bank_copies:
        copy.wait()


def forward_kernel(
    fore_c, fore_s, fore_rc, fore_rs, near_c, near_s, base_c, base_s,
    forward_hbm, near_out_c, near_out_s, forward, sem,
):
    half_len = fore_c.shape[1]
    quarter = half_len // 2
    place, _ = position()
    first_lane = lax.broadcasted_iota(jnp.int32, fore_c.shape, 1) == 0
    sign = 1.0 - 2.0 * (lax.broadcasted_iota(jnp.int32, fore_c.shape, 0) % 2).astype(F32)

    def fore(step, carry):
        cos, sin = carry
        for part, table in enumerate((cos, jnp.where(first_lane, sign, sin))):
            for odd in range(2):
                lane = slice(odd * quarter, (odd + 1) * quarter)
                to = slice(part * quarter, (part + 1) * quarter)
                forward[odd, aligned(step * STEP, STEP), to] = table[:, lane].astype(BF16)
        return turn(cos, sin, fore_rc[...], fore_rs[...])

    lax.fori_loop(0, forward.shape[1] // STEP, fore, (fore_c[...], fore_s[...]))
    copy = pltpu.make_async_copy(forward, forward_hbm, sem)
    copy.start()
    near_out_c[...], near_out_s[...] = turn(near_c[...], near_s[...], base_c[place], base_s[place])
    copy.wait()


def inverse_tables_kernel(
    even_c, even_s, odd_c, odd_s, rows_rc, rows_rs, lift_c, lift_s, lift_rc, lift_rs, mid_c, mid_s,
    cols_c, cols_s, cols_rc, cols_rs,
    even_out, odd_out, lift_out_c, lift_out_s, cols_out, rows_out, bins_out,
):
    half_len = even_c.shape[1]
    quarter = half_len // 2
    first_len = cols_c.shape[1]
    per = first_len // 2

    def spread(out, cos, sin):
        def body(step, carry):
            cos, sin = carry
            upper = aligned(step * STEP, STEP)
            lower = aligned(quarter + step * STEP, STEP)
            for lane in range(0, half_len, PIECE):
                real, imag = slice(2 * lane, 2 * lane + PIECE), slice(2 * lane + PIECE, 2 * (lane + PIECE))
                cos_at, sin_at = cos[:, lane : lane + PIECE], sin[:, lane : lane + PIECE]
                out[upper, real] = cos_at.astype(BF16)
                out[upper, imag] = sin_at.astype(BF16)
                out[lower, real] = (-sin_at).astype(BF16)
                out[lower, imag] = cos_at.astype(BF16)
            return turn(cos, sin, rows_rc[...], rows_rs[...])

        lax.fori_loop(0, quarter // STEP, body, (cos, sin))

    spread(even_out, even_c[...], even_s[...])
    spread(odd_out, odd_c[...], odd_s[...])

    for parity in range(2):

        def lifts(step, carry, parity=parity):
            cos, sin = carry
            at = aligned(parity * per + step * STEP, STEP)
            lift_out_c[at, :] = cos
            lift_out_s[at, :] = sin
            return turn(cos, sin, lift_rc[...], lift_rs[...])

        lax.fori_loop(0, per // STEP, lifts, (lift_c[parity], lift_s[parity]))
    lift_out_c[0:STEP, :] = mid_c[...]
    lift_out_s[0:STEP, :] = mid_s[...]

    def columns(step, carry):
        cos, sin = carry
        upper = aligned(step * STEP, STEP)
        lower = aligned(per + step * STEP, STEP)
        for parity in range(2):
            at = slice(parity * per, (parity + 1) * per)
            left = slice(parity * first_len, parity * first_len + per)
            right = slice(parity * first_len + per, (parity + 1) * first_len)
            cols_out[upper, left] = cos[:, at].astype(BF16)
            cols_out[upper, right] = (-sin[:, at]).astype(BF16)
            cols_out[lower, left] = sin[:, at].astype(BF16)
            cols_out[lower, right] = cos[:, at].astype(BF16)
        return turn(cos, sin, cols_rc[...], cols_rs[...])

    lax.fori_loop(0, per // STEP, columns, (cols_c[...], cols_s[...]))
    sort_tables(lift_c.shape[1], rows_out, bins_out)


def stage_two_kernel(
    segs, cols, moved, near_c, near_s, mid_c_hbm, mid_s_hbm, forward_hbm, out,
    mid_c, mid_s, forward, stacked, middle, product, sems,
):
    place, _ = position()
    _, half_len, _ = forward.shape
    second_len = 2 * half_len
    quarter = half_len // 2
    pieces = [(forward_hbm.at[odd], forward.at[odd]) for odd in range(2)]
    pieces += [(mid_c_hbm, mid_c), (mid_s_hbm, mid_s)]
    copies = start_copies(pieces, sems)
    sources, rows, _ = moved.shape
    tail = segs * cols
    all_rows = (segs + 1) * rows
    width = 2 * cols
    low = lax.broadcasted_iota(jnp.int32, (rows, width), 1) < cols
    own_first = place == 0
    packed_row = lax.broadcasted_iota(jnp.int32, (rows, width), 0) == 0
    drop = jnp.logical_and(packed_row, own_first)

    def pair(left, right):
        return (
            jnp.where(low, left, pltpu.roll(right, cols, 1)),
            jnp.where(low, pltpu.roll(left, cols, 1), right),
        )

    middle[...] = jnp.zeros_like(middle)
    tiles = sources // 2
    for tile in range(tiles // 2):
        lane = slice(tile * width, (tile + 1) * width)
        lanes = (lane, slice(half_len + tile * width, half_len + (tile + 1) * width))

        def piece(lo, tile=tile):
            hi = lo + width
            found = []
            for source in (2 * tile, 2 * tile + tiles):
                found.append(
                    pair(moved[source, :, lo:hi].astype(F32), moved[source + 1, :, lo:hi].astype(F32))
                )
            return [(found[0][at], found[1][at]) for at in range(2)]

        def put(seg, real, imag, lane=lane, lanes=lanes):
            turned_real, turned_imag = [], []
            for half in range(2):
                middle[seg : seg + 1, lanes[half]] = imag[half][0:1, :]
                kept = jnp.where(drop, 0.0, imag[half])
                cos, sin = near_c[:, lanes[half]], near_s[:, lanes[half]]
                turned_real.append(real[half] * cos + kept * sin)
                turned_imag.append(kept * cos - real[half] * sin)
            for at, (low_half, high_half) in ((seg * rows, turned_real), (all_rows + seg * rows, turned_imag)):
                stacked[0, at : at + rows, lane] = (low_half + high_half).astype(BF16)
                stacked[1, at : at + rows, lane] = (low_half - high_half).astype(BF16)

        for twin in range(segs // 2):
            real_one, real_two = piece(twin * width)
            imag_one, imag_two = piece(tail + twin * width)
            put(2 * twin, real_one, imag_one)
            put(2 * twin + 1, real_two, imag_two)
        real, imag = piece(2 * tail)
        put(segs, real, imag)
    for copy in copies[2:]:
        copy.wait()
    for part, turned in enumerate((middle[...] * mid_c[...], middle[...] * -mid_s[...])):
        at = slice(2 * all_rows + part * rows, 2 * all_rows + (part + 1) * rows)
        stacked[0, at, :] = (turned[:, :half_len] + turned[:, half_len:]).astype(BF16)
        stacked[1, at, :] = (turned[:, :half_len] - turned[:, half_len:]).astype(BF16)

    first_lane = lax.broadcasted_iota(jnp.int32, (rows, quarter), 1) == 0
    swap = jnp.logical_and(lax.broadcasted_iota(jnp.int32, (rows, quarter), 0) == 0, own_first)
    floor = 0.2 * (second_len * 2 * sources * rows)
    upper, lower = [], []
    for odd in range(2):
        cos_at = slice(odd * half_len, odd * half_len + quarter)
        sin_at = slice(odd * half_len + quarter, (odd + 1) * half_len)
        copies[odd].wait()
        product[:, odd * half_len : (odd + 1) * half_len] = matmul(stacked[odd], forward[odd])

        def parts(at, lower_at, cos_at=cos_at, sin_at=sin_at):
            return (
                product[at : at + rows, cos_at],
                product[at : at + rows, sin_at],
                product[lower_at : lower_at + rows, cos_at],
                product[lower_at : lower_at + rows, sin_at],
            )

        def direct_of(rc, rs, ic, imag_s, odd=odd):
            if not odd:
                rs, imag_s = jnp.where(first_lane, 0.0, rs), jnp.where(first_lane, 0.0, imag_s)
            return rc + imag_s, ic - rs

        def mirror_of(rc, rs, ic, imag_s, odd=odd):
            real, imag = rc - imag_s, ic + rs
            if not odd:
                real, imag = jnp.where(first_lane, rs, real), jnp.where(first_lane, imag_s, imag)
            return real, imag

        level = jnp.zeros((rows, quarter), F32)
        mirror_level = level
        for seg in range(segs):
            four = parts(seg * rows, all_rows + seg * rows)
            real, imag = direct_of(*four)
            level = level + (real * real + imag * imag)
            real, imag = mirror_of(*four)
            mirror_level = mirror_level + (real * real + imag * imag)
        four = parts(segs * rows, all_rows + segs * rows)
        real, imag = direct_of(*four)
        mirror_real, mirror_imag = mirror_of(*four)
        mid_real, mid_imag = mirror_of(*parts(2 * all_rows, 2 * all_rows + rows))
        mid_level = jnp.sum((mid_real * mid_real + mid_imag * mid_imag)[:segs], 0, keepdims=True)
        mirror_level = jnp.where(swap, mid_level, mirror_level)
        mirror_real = jnp.where(swap, mid_real[segs : segs + 1], mirror_real)
        mirror_imag = jnp.where(swap, mid_imag[segs : segs + 1], mirror_imag)
        level = jnp.maximum(level * (1.0 / segs), floor)
        mirror_level = jnp.maximum(mirror_level * (1.0 / segs), floor)
        upper.append((real / level, imag / level, 1.0 / level))
        lower.append((mirror_real / mirror_level, -mirror_imag / mirror_level, 1.0 / mirror_level))
    eighth = rows // 2
    for part in range(3):
        mirrored = (lower[1][part], pltpu.roll(lower[0][part], quarter - 1, 1))
        for odd in range(2):
            lane = slice(part * half_len + odd * quarter, part * half_len + (odd + 1) * quarter)
            for parity in range(2):
                at = slice(parity * eighth, (parity + 1) * eighth)
                block = jnp.concatenate([upper[odd][part][at], mirrored[odd][at]], 0)
                out[parity * rows : (parity + 1) * rows, lane] = block.astype(BF16)


def sort_tables(rows, rows_out, bins_out):
    first_len, half_len = rows_out.shape[0], bins_out.shape[0]
    per = first_len // 2
    _, group = position()
    deep = 128

    def one_hot(mask):
        return jnp.where(mask, 1.0, 0.0).astype(BF16)

    def body(step, carry):
        at = aligned(step * deep, deep)
        row = packed_row_of(step * deep + lax.broadcasted_iota(jnp.int32, (deep, first_len), 0), first_len, rows)
        share = (row // rows) % 2
        column = (row // (2 * rows)) * rows + row % rows + jnp.where(share == group, 0, per)
        rows_out[at, :] = one_hot(column == lax.broadcasted_iota(jnp.int32, (deep, first_len), 1))
        return carry

    lax.fori_loop(0, first_len // deep, body, 0)

    def bins(step, carry):
        row = step * deep + lax.broadcasted_iota(jnp.int32, (deep, half_len), 0)
        lane = lax.broadcasted_iota(jnp.int32, (deep, half_len), 1)
        bins_out[aligned(step * deep, deep), :] = one_hot(row == bin_of(lane, half_len))
        return carry

    lax.fori_loop(0, half_len // deep, bins, 0)


def bin_of(lane, half_len):
    return jnp.where(lane < half_len // 2, 2 * lane, 2 * lane - half_len + 1)


def packed_row_of(at, first_len, rows):
    per = first_len // 2
    packed = (at % per) // rows * rows + 2 * (at % (rows // 2)) + at // per
    turned = jnp.where(packed == 0, first_len // 2, first_len - packed)
    return jnp.where(at % rows >= rows // 2, turned, packed)


def choose_kernel(order, cuts, own, other, by_rows, by_bins, out, held):
    place, _ = position()
    rows, sources = own.shape[1], own.shape[0]
    per = sources * rows
    first_len, half_len = 2 * per, own.shape[2] // 2
    for source in range(sources):
        held[source * rows : (source + 1) * rows, :] = own[source]
        held[per + source * rows : per + (source + 1) * rows, :] = other[source]
    picked = matmul(by_rows[...], held[...]).astype(BF16)
    at = lax.broadcasted_iota(jnp.int32, (first_len, 128), 0)
    room = cuts[order[place]] - packed_row_of(at, first_len, rows)
    for part in range(2):
        moved = matmul(picked[:, part * half_len : (part + 1) * half_len], by_bins[...])
        for lane in range(0, half_len, 128):
            bins = bin_of(lane + lax.broadcasted_iota(jnp.int32, (1, 128), 1), half_len)
            kept = jnp.where(first_len * bins < room, moved[:, lane : lane + 128], 0.0)
            out[:, part * half_len + lane : part * half_len + lane + 128] = kept.astype(BF16)


def filter_blocks(offsets, blocks, chosen, tables, norm, filtered, lifted):
    place, _ = position()
    even_table, odd_table, lift_c, lift_s = tables
    half_len = even_table.shape[0]
    quarter = half_len // 2
    first_len = chosen.shape[0]
    per = first_len // 2
    rows = blocks[0].shape[0] // 2
    groups = []
    for block, offset in zip(blocks, offsets):
        device = jnp.bitwise_xor(place, offset)
        for parity in range(2):
            row = slice(parity * rows, (parity + 1) * rows)
            at = aligned(parity * per + device * rows, rows)
            white_real = block[row, :half_len].astype(F32)
            white_imag = block[row, half_len : 2 * half_len].astype(F32)
            weight = block[row, 2 * half_len :].astype(F32)
            real = chosen[at, :half_len].astype(F32)
            imag = chosen[at, half_len:].astype(F32)
            norm = norm + (real * real + imag * imag) * weight
            filt_real = (white_real * real + white_imag * imag).astype(BF16)
            filt_imag = (white_imag * real - white_real * imag).astype(BF16)
            to = slice(len(groups) * rows, (len(groups) + 1) * rows)
            filtered[to, 0:quarter] = filt_real[:, :quarter]
            filtered[to, quarter:half_len] = filt_imag[:, :quarter]
            filtered[to, half_len : half_len + quarter] = filt_real[:, quarter:]
            filtered[to, half_len + quarter :] = filt_imag[:, quarter:]
            groups.append((to, at, parity * first_len + device * rows))
    for lane in range(0, half_len, PIECE):
        both = slice(2 * lane, 2 * (lane + PIECE))
        even = matmul(filtered[:, :half_len], even_table[:, both])
        odd = matmul(filtered[:, half_len:], odd_table[:, both])
        for upper in range(2):
            lanes = slice(upper * half_len + lane, upper * half_len + lane + PIECE)
            total = even - odd if upper else even + odd
            for row, at, target in groups:
                real, imag = total[row, :PIECE], total[row, PIECE:]
                cos, sin = lift_c[at, lanes], lift_s[at, lanes]
                lifted[aligned(target, rows), lanes] = (real * cos - imag * sin).astype(BF16)
                lifted[aligned(target + per, rows), lanes] = (real * sin + imag * cos).astype(BF16)
    return norm


def early_kernel(near, theirs, both, far, chosen, *refs):
    tables, (lifted, norm, filtered) = refs[:4], refs[4:]
    blocks = [*[near.at[at] for at in range(4)], *[theirs.at[at] for at in range(4)], both.at[0], both.at[1], far]
    zero = jnp.zeros(norm.shape, F32)
    norm[...] = filter_blocks(EARLY, blocks, chosen, tables, zero, filtered, lifted)


def middle_kernel(theirs, early, early_norm, chosen, *refs):
    tables, (lifted, norm, filtered) = refs[:4], refs[4:]
    blocks = [theirs.at[at] for at in range(3)]
    norm[...] = filter_blocks(MIDDLE, blocks, chosen, tables, early_norm[...], filtered, lifted)


def late_kernel(last, theirs, early, early_norm, chosen, *refs):
    tables, (cols_table, out, lifted, filtered) = refs[:4], refs[4:]
    norm = filter_blocks(LATE, [last, theirs], chosen, tables, early_norm[...], filtered, lifted)
    scale = lax.rsqrt(jnp.sum(norm, keepdims=True))
    first_len = chosen.shape[0]
    per = first_len // 2
    wide = 256
    for lane in range(0, lifted.shape[1], wide):
        at = slice(lane, lane + wide)
        even = matmul(cols_table[:, :first_len], lifted[:first_len, at])
        odd = matmul(cols_table[:, first_len:], lifted[first_len:, at])
        for upper in range(2):
            total = even - odd if upper else even + odd
            power = total[:per] * total[:per] + total[per:] * total[per:]
            size = power * lax.rsqrt(jnp.maximum(power, 1e-37))
            out[0, upper * per : (upper + 1) * per, at] = (size * scale).astype(BF16)


def swap_with(array, flip):
    pairs = [(at, at ^ flip) for at in range(lax.axis_size("tmpl"))]
    return lax.ppermute(array, "tmpl", pairs)


def tiled_local(strain, analysis, bank, cutoff, order):
    dev_count = lax.axis_size("tmpl")
    segs, first_len, cols = strain.shape
    second_len = cols * dev_count
    length = first_len * second_len
    half_len = second_len // 2
    rows = first_len // dev_count // 2
    templates = order.shape[0]
    lanes = 2 * (segs + 1) * cols

    first, second, half = np.arange(first_len), np.arange(second_len), np.arange(half_len)
    devices, step = np.arange(dev_count), np.arange(STEP)
    near = halves(rows)
    packed = (devices[:, None] * rows + near[None, :]).reshape(dev_count, 2, rows // 2)
    waves = []
    for odd in range(2):
        cos, sin = turns(packed[:, odd].reshape(-1, 1) * first[None, : first_len // 2], first_len)
        if not odd:
            sin[0] = 2 * (first[: first_len // 2] % 2) - 1.0
        waves.append(np.concatenate([cos, -sin]))
    win = np.stack(turns(np.arange(8)[:, None] + second_len * first[None, :], length))
    spin = np.stack(turns(cols * devices, length), 1)[:, :, None] * np.ones((1, 1, first_len), np.float32)
    turns_of_eight = [tuple(float(at) for at in turns(8 * block, length)) for block in range(cols // 8)]

    sent = pl.pallas_call(
        functools.partial(stage_one_kernel, turns_of_eight),
        in_specs=[outside()] * 7,
        out_specs=whole(),
        scratch_shapes=[
            pltpu.SMEM((templates,), jnp.int32),
            vmem((segs, cols, first_len), F32),
            vmem((cols, first_len), F32),
            vmem((2, first_len), F32),
            vmem((2, 8, first_len), F32),
            vmem((2, dev_count * rows, first_len // 2)),
            vmem((2, (segs + 1) * cols, first_len // 2)),
            pltpu.SemaphoreType.DMA((segs + 5,)),
            pltpu.SemaphoreType.DMA((2 * templates,)),
        ],
        out_shape=pltpu.VMEM((dev_count * rows, lanes + 2 * half_len), BF16),
        compiler_params=params(16),
        name="stage_one",
    )(
        *in_hbm(
            order, jnp.swapaxes(strain, 1, 2), jnp.swapaxes(analysis, 0, 1), spin, win,
            np.stack(waves).astype(BF16), bank,
        ),
    )
    moved = lax.all_to_all(
        sent.reshape(dev_count, rows, lanes + 2 * half_len), "tmpl", split_axis=0, concat_axis=0, tiled=True
    )
    own = moved[:, :, lanes:]
    other = lax.ppermute(own, "grp", [(0, 1), (1, 0)])

    split = halves(half_len)
    low = 2 * np.arange(rows // 2)
    lift_rows = [np.concatenate([low + odd, first_len - low - odd]) for odd in range(2)]
    lift_init = [turns(at[:, None] * second[None, :], length) for at in lift_rows]
    cols_parts = []
    for odd in range(2):
        straight = devices[:, None] * rows + low[None, :] + odd
        turned = np.where(straight == 0, first_len // 2, first_len - straight)
        cols_parts.append(np.concatenate([straight, turned], 1).reshape(-1))
    cols_rows = np.concatenate(cols_parts)
    mid_rows = lift_rows[0].copy()
    mid_rows[rows // 2] = first_len // 2
    step_sign = np.where(np.arange(rows) < rows // 2, rows, -rows)
    fore = [
        *turns(step[:, None] * split[None, :], second_len),
        *turns(STEP * split[None, :], second_len),
        *turns(near[:, None] * second[None, :], length),
        *turns(rows * devices[:, None, None] * second[None, None, :], length),
    ]
    forward, near_c, near_s = pl.pallas_call(
        forward_kernel,
        out_shape=[
            pltpu.HBM((2, half_len, half_len), BF16),
            *[pltpu.VMEM((rows, second_len), F32)] * 2,
        ],
        in_specs=[whole()] * len(fore),
        out_specs=[outside()] + [whole()] * 2,
        scratch_shapes=[vmem((2, half_len, half_len)), pltpu.SemaphoreType.DMA],
        compiler_params=params(16),
        cost_estimate=pl.CostEstimate(flops=10**7, bytes_accessed=2 * 10**7, transcendentals=0),
        name="forward_tables",
    )(*in_hbm(*fore))
    back = [
        *turns(2 * step[:, None] * half[None, :], second_len),
        *turns((2 * step[:, None] + 1) * half[None, :], second_len),
        *turns(2 * STEP * half[None, :], second_len),
        np.stack([lift_init[0][0], lift_init[1][0]]),
        np.stack([lift_init[0][1], lift_init[1][1]]),
        *turns(step_sign[:, None] * second[None, :], length),
        *turns(mid_rows[:, None] * second[None, :], length),
        *turns(step[:, None] * cols_rows[None, :], first_len),
        *turns(STEP * cols_rows[None, :], first_len),
    ]
    shapes = [
        ((half_len, second_len), BF16),
        ((half_len, second_len), BF16),
        ((first_len, second_len), F32),
        ((first_len, second_len), F32),
        ((first_len, 2 * first_len), BF16),
        ((first_len, first_len), BF16),
        ((half_len, half_len), BF16),
    ]
    inverse_tables = pl.pallas_call(
        inverse_tables_kernel,
        out_shape=[pltpu.VMEM(*shape) for shape in shapes],
        in_specs=[whole()] * len(back),
        out_specs=[whole()] * len(shapes),
        compiler_params=params(8),
        cost_estimate=pl.CostEstimate(flops=10**7, bytes_accessed=2 * 10**7, transcendentals=0),
        name="inverse_tables",
    )
    even_table, odd_table, lift_c, lift_s, cols_table, by_rows, by_bins = inverse_tables(*in_hbm(*back))

    mid_c, mid_s = turns(first_len // 2 * second[None, :], length)
    all_rows = 2 * (segs + 2) * rows
    stage_two = pl.pallas_call(
        functools.partial(stage_two_kernel, segs, cols),
        out_shape=jax.ShapeDtypeStruct((2 * rows, 3 * half_len), BF16),
        in_specs=[whole()] * 3 + [outside()] * 3,
        out_specs=whole(),
        scratch_shapes=[
            *[vmem((1, second_len), F32)] * 2,
            vmem(forward.shape),
            vmem((2, all_rows, half_len)),
            vmem((rows, second_len), F32),
            vmem((all_rows, second_len), F32),
            pltpu.SemaphoreType.DMA((4,)),
        ],
        compiler_params=params(24),
        cost_estimate=pl.CostEstimate(flops=10**9, bytes_accessed=4 * 10**6, transcendentals=0),
        name="stage_two",
    )
    block = stage_two(moved, *in_vmem(near_c, near_s), *in_hbm(mid_c, mid_s, forward))

    two = swap_with(block, 8)
    one = swap_with(block, 4)
    beside = swap_with(block, 2)
    both = swap_with(jnp.stack([one, two]), 2)
    far = swap_with(two, 4)
    near = jnp.stack([block, beside, one, two])
    theirs = swap_with(near, 1)
    last = swap_with(far, 2)
    more = swap_with(jnp.stack([both[0], both[1], far]), 1)
    late = swap_with(last, 1)

    choose = pl.pallas_call(
        choose_kernel,
        grid_spec=pltpu.PrefetchScalarGridSpec(
            num_scalar_prefetch=2,
            grid=(),
            in_specs=[whole()] * 4,
            out_specs=whole(),
            scratch_shapes=[vmem((first_len, 2 * half_len))],
        ),
        out_shape=jax.ShapeDtypeStruct((first_len, 2 * half_len), BF16),
        compiler_params=params(16),
        cost_estimate=pl.CostEstimate(flops=10**9, bytes_accessed=4 * 10**6, transcendentals=0),
        name="choose",
    )
    chosen = choose(order, cutoff, own, other, *in_vmem(by_rows, by_bins))

    spread = [(2 * first_len, second_len), BF16]
    tables = in_vmem(even_table, odd_table, lift_c, lift_s)
    early = pl.pallas_call(
        early_kernel,
        out_shape=[pltpu.VMEM(*spread), pltpu.VMEM((rows, half_len), F32)],
        in_specs=[whole()] * 9,
        out_specs=[whole()] * 2,
        scratch_shapes=[vmem((len(EARLY) * 2 * rows, 2 * half_len))],
        compiler_params=params(16),
        cost_estimate=pl.CostEstimate(flops=10**9, bytes_accessed=4 * 10**6, transcendentals=0),
        name="early",
    )
    lifted, norm = early(near, theirs, both, far, chosen, *tables)
    middle = pl.pallas_call(
        middle_kernel,
        out_shape=[pltpu.VMEM(*spread), pltpu.VMEM((rows, half_len), F32)],
        in_specs=[whole()] * 8,
        out_specs=[whole()] * 2,
        scratch_shapes=[vmem((len(MIDDLE) * 2 * rows, 2 * half_len))],
        input_output_aliases={1: 0},
        compiler_params=params(16),
        cost_estimate=pl.CostEstimate(flops=10**9, bytes_accessed=4 * 10**6, transcendentals=0),
        name="middle",
    )
    lifted, norm = middle(more, *in_vmem(lifted, norm), chosen, *tables)
    result, _ = pl.pallas_call(
        late_kernel,
        out_shape=[jax.ShapeDtypeStruct((1, first_len, second_len), BF16), pltpu.VMEM(*spread)],
        in_specs=[whole()] * 10,
        out_specs=[whole()] * 2,
        scratch_shapes=[vmem((len(LATE) * 2 * rows, 2 * half_len))],
        input_output_aliases={2: 1},
        compiler_params=params(16),
        name="late",
    )(last, late, *in_vmem(lifted, norm), chosen, *tables, *in_vmem(cols_table))
    return result


def angles(left_idx, right_idx, period):
    product = left_idx[:, None] * right_idx[None, :] % period
    phase_angle = product.astype(jnp.float32) * (2.0 * math.pi / period)
    return (jnp.cos(phase_angle), jnp.sin(phase_angle))


def filtered(white_pair, tmpl_pair, cut_bins, freq_bin):
    white_real = white_pair[0].astype(jnp.float32)
    white_imag = white_pair[1].astype(jnp.float32)
    tmpl_real = tmpl_pair[0].astype(jnp.float32)
    tmpl_imag = tmpl_pair[1].astype(jnp.float32)
    in_band = freq_bin[None] < cut_bins[:, None, None]
    filt_real = jnp.where(in_band, white_real * tmpl_real + white_imag * tmpl_imag, 0.0)
    filt_imag = jnp.where(in_band, white_imag * tmpl_real - white_real * tmpl_imag, 0.0)
    return jnp.concatenate([filt_real, filt_imag], -1).astype(jnp.bfloat16)


def inverse_rows(stacked, row_bins, second_len, length):
    half_len = second_len // 2
    cosine, sine = angles(
        jnp.arange(half_len, dtype=jnp.int32), jnp.arange(second_len, dtype=jnp.int32), second_len
    )
    dft_table = jnp.concatenate(
        [jnp.concatenate([cosine, sine], 1), jnp.concatenate([-sine, cosine], 1)], 0
    ).astype(jnp.bfloat16)
    spread = jnp.einsum("tkf,fg->tkg", stacked, dft_table, preferred_element_type=jnp.float32)
    spread_real = spread[..., :second_len]
    spread_imag = spread[..., second_len:]
    cos_twist, sin_twist = angles(row_bins, jnp.arange(second_len, dtype=jnp.int32), length)
    lift_real = spread_real * cos_twist - spread_imag * sin_twist
    lift_imag = spread_real * sin_twist + spread_imag * cos_twist
    return jnp.concatenate([lift_real, lift_imag], -1).astype(jnp.bfloat16)


def inverse_cols(lifted, first_len, second_len):
    row_idx = jnp.arange(first_len, dtype=jnp.int32)
    cosine, sine = angles(row_idx, row_idx, first_len)
    cosine = cosine.astype(jnp.bfloat16)
    sine = sine.astype(jnp.bfloat16)
    lift_real = lifted[..., :second_len]
    lift_imag = lifted[..., second_len:]
    field_real = jnp.einsum(
        "ak,tkb->tab", cosine, lift_real, preferred_element_type=jnp.float32
    ) - jnp.einsum("ak,tkb->tab", sine, lift_imag, preferred_element_type=jnp.float32)
    field_imag = jnp.einsum(
        "ak,tkb->tab", sine, lift_real, preferred_element_type=jnp.float32
    ) + jnp.einsum("ak,tkb->tab", cosine, lift_imag, preferred_element_type=jnp.float32)
    return (field_real, field_imag)


def plain_local(strain, analysis, bank, cutoff, order):
    highest = lax.Precision.HIGHEST
    dev_count = lax.axis_size("tmpl")
    my_index = lax.axis_index("tmpl")
    seg_count = strain.shape[0]
    first_len = strain.shape[1]
    col_count = strain.shape[2]
    second_len = col_count * dev_count
    length = first_len * second_len
    half_len = second_len // 2
    row_count = first_len // dev_count
    row_idx = jnp.arange(first_len, dtype=jnp.int32)
    col_index = my_index * col_count + jnp.arange(col_count, dtype=jnp.int32)
    sample_idx = row_idx[:, None] * second_len + col_index[None, :]
    window = (
        math.sqrt(8.0 / 3.0) * jnp.sin(sample_idx.astype(jnp.float32) * (math.pi / length)) ** 2
    )
    series = jnp.concatenate([strain * window, analysis[None]], 0)
    cos_one, sin_one = angles(row_idx, row_idx, first_len)
    part_real = jnp.einsum("ka,sab->skb", cos_one, series, precision=highest)
    part_imag = -jnp.einsum("ka,sab->skb", sin_one, series, precision=highest)
    cos_twist, sin_twist = angles(row_idx, col_index, length)
    twist_real = part_real * cos_twist + part_imag * sin_twist
    twist_imag = part_imag * cos_twist - part_real * sin_twist
    moved = lax.all_to_all(
        jnp.stack([twist_real, twist_imag]).astype(jnp.bfloat16),
        "tmpl",
        split_axis=2,
        concat_axis=3,
        tiled=True,
    ).astype(jnp.float32)
    cos_two, sin_two = angles(
        jnp.arange(second_len, dtype=jnp.int32), jnp.arange(half_len, dtype=jnp.int32), second_len
    )
    spec_real = jnp.einsum("skb,bf->skf", moved[0], cos_two, precision=highest) + jnp.einsum(
        "skb,bf->skf", moved[1], sin_two, precision=highest
    )
    spec_imag = jnp.einsum("skb,bf->skf", moved[1], cos_two, precision=highest) - jnp.einsum(
        "skb,bf->skf", moved[0], sin_two, precision=highest
    )
    power_spec = jnp.maximum(
        jnp.mean(spec_real[:seg_count] ** 2 + spec_imag[:seg_count] ** 2, axis=0), 0.2 * length
    )
    whitened = jnp.stack(
        [spec_real[seg_count] / power_spec, spec_imag[seg_count] / power_spec]
    ).astype(jnp.bfloat16)
    own_rows = my_index * row_count + jnp.arange(row_count, dtype=jnp.int32)
    half_idx = jnp.arange(half_len, dtype=jnp.int32)
    freq_local = own_rows[:, None] + first_len * half_idx[None, :]
    chosen = jnp.take(bank, order, axis=1)
    cuts = jnp.take(cutoff, order)
    bank_real = chosen[0].astype(jnp.float32)
    bank_imag = chosen[1].astype(jnp.float32)
    in_band = freq_local[None] < cuts[:, None, None]
    local_norm = jnp.sum(
        jnp.where(in_band, (bank_real**2 + bank_imag**2) / power_spec, 0.0), axis=(1, 2)
    )
    norm_sq = lax.psum(local_norm, "tmpl")
    per_device = cuts.shape[0] // dev_count
    own_norm = lax.dynamic_slice_in_dim(norm_sq, my_index * per_device, per_device)
    stacked = filtered(whitened, chosen, cuts, freq_local)
    lifted = lax.all_to_all(
        inverse_rows(stacked, own_rows, second_len, length),
        "tmpl",
        split_axis=0,
        concat_axis=1,
        tiled=True,
    )
    field_real, field_imag = inverse_cols(lifted, first_len, second_len)
    magnitude = jnp.sqrt(field_real**2 + field_imag**2)
    return (magnitude / jnp.sqrt(own_norm)[:, None, None]).astype(jnp.bfloat16)


def local(strain, analysis, bank, cutoff, order):
    dev_count, segs, cols = lax.axis_size("tmpl"), strain.shape[0], strain.shape[2]
    rows = strain.shape[1] // dev_count // 2
    fits = rows == STEP and cols == 64 and segs % 2 == 0 and dev_count == len(EARLY + MIDDLE + LATE)
    if fits and order.shape[0] == dev_count and lax.axis_size("grp") == 2:
        return tiled_local(strain, analysis, bank, cutoff, order)
    return plain_local(strain, analysis, bank, cutoff, order)


def solution(mesh):
    return jax.shard_map(
        local,
        mesh=mesh,
        in_specs=(P("grp", None, "tmpl"), P("grp", "tmpl"), P(None, None, "tmpl", None), P(), P()),
        out_specs=P(("grp", "tmpl"), None, None),
        check_vma=False,
    )
```

```python
import functools
import math

import jax
import jax.numpy as jnp
import numpy as np
from jax import lax
from jax.experimental import pallas as pl
from jax.experimental.pallas import tpu as pltpu
from jax.sharding import PartitionSpec as P

BF16 = jnp.bfloat16
F32 = jnp.float32
STEP = 16
PIECE = 128
EARLY = (0, 2, 4, 8, 1, 3, 5, 9, 6, 10, 12)
MIDDLE = (7, 11, 13)
LATE = (14, 15)


def turns(product, period):
    angle = (product % period) * (2.0 * math.pi / period)
    return np.cos(angle).astype(np.float32), np.sin(angle).astype(np.float32)


def matmul(left, right):
    return jnp.dot(left, right, preferred_element_type=F32)


def matmul_nt(left, right):
    return lax.dot_general(left, right, (((1,), (1,)), ((), ())), preferred_element_type=F32)


def vmem(shape, dtype=BF16):
    return pltpu.VMEM(shape, dtype)


def whole():
    return pl.BlockSpec(memory_space=pltpu.VMEM)


def outside():
    return pl.BlockSpec(memory_space=pltpu.HBM)


def in_hbm(*arrays):
    return [pltpu.with_memory_space_constraint(jnp.asarray(array), pltpu.HBM) for array in arrays]


def in_vmem(*arrays):
    return [pltpu.with_memory_space_constraint(array, pltpu.VMEM) for array in arrays]


def position():
    return lax.axis_index("tmpl"), lax.axis_index("grp")


def start_copies(pairs, sems):
    copies = [
        pltpu.make_async_copy(source, target, sems.at[at]) for at, (source, target) in enumerate(pairs)
    ]
    for copy in copies:
        copy.start()
    return copies


def params(mib):
    return pltpu.CompilerParams(vmem_limit_bytes=mib << 20)


def turn(cos, sin, by_cos, by_sin):
    return cos * by_cos - sin * by_sin, sin * by_cos + cos * by_sin


def halves(count):
    return np.concatenate([np.arange(0, count, 2), np.arange(1, count, 2)])


def aligned(start, size):
    return pl.ds(pl.multiple_of(start, size), size)


def stage_one_kernel(
    turns_of_eight, order_hbm, strain_hbm, analysis_hbm, spin_hbm, win_hbm, wave_hbm, bank, out,
    order, strain, analysis, spin, win, wave, packed, sems, bank_sems,
):
    segs, cols, first_len = strain.shape
    tail = segs * cols
    templates, half_len = bank.shape[1], bank.shape[3]
    rows = out.shape[0] // templates
    half = first_len // 2
    place, group = position()
    sources = [
        (order_hbm, order),
        (spin_hbm.at[place], spin),
        (win_hbm, win),
        *[(strain_hbm.at[seg], strain.at[seg]) for seg in range(segs)],
        (analysis_hbm, analysis),
        (wave_hbm, wave),
    ]
    copies = start_copies(sources, sems)
    lane = 2 * (tail + cols)
    for copy in copies[:3]:
        copy.wait()
    bank_pairs = []
    for row in range(templates):
        for part in range(2):
            bank_pairs.append(
                (
                    bank.at[part, order[row], aligned(group * rows, rows), :],
                    out.at[
                        row * rows : (row + 1) * rows,
                        lane + part * half_len : lane + (part + 1) * half_len,
                    ],
                )
            )
    bank_copies = start_copies(bank_pairs, bank_sems)
    scale = 0.5 * math.sqrt(8.0 / 3.0)
    win_c, win_s = turn(win[0], win[1], spin[0:1, :], spin[1:2, :])
    window = jnp.concatenate(
        [scale - (win_c * (scale * by_cos) - win_s * (scale * by_sin)) for by_cos, by_sin in turns_of_eight], 0
    )

    def pack(at, values):
        packed[0, at : at + cols, :] = (values[:, :half] + values[:, half:]).astype(BF16)
        packed[1, at : at + cols, :] = (values[:, :half] - values[:, half:]).astype(BF16)

    for seg in range(segs):
        copies[3 + seg].wait()
        pack(seg * cols, strain[seg] * window)
    copies[3 + segs].wait()
    pack(tail, analysis[...])
    copies[4 + segs].wait()
    both = [matmul_nt(wave[odd], packed[odd]) for odd in range(2)]
    count = out.shape[0] // 2

    def woven(part):
        halves_of = [
            table[part * count : (part + 1) * count].reshape(templates, rows // 2, tail + cols) for table in both
        ]
        return jnp.concatenate(halves_of, 1).reshape(2 * count, tail + cols)

    real, imag = woven(0), woven(1)
    out[:, 0:tail] = real[:, :tail].astype(BF16)
    out[:, tail : 2 * tail] = imag[:, :tail].astype(BF16)
    joined = jnp.concatenate([real[:, tail:], imag[:, tail:]], 1)
    out[:, 2 * tail : lane] = joined.astype(BF16)
    for copy in bank_copies:
        copy.wait()


def forward_kernel(
    fore_c, fore_s, fore_rc, fore_rs, near_c, near_s, base_c, base_s,
    forward, near_out_c, near_out_s,
):
    half_len = fore_c.shape[1]
    quarter = half_len // 2
    place, _ = position()
    first_lane = lax.broadcasted_iota(jnp.int32, fore_c.shape, 1) == 0
    sign = 1.0 - 2.0 * (lax.broadcasted_iota(jnp.int32, fore_c.shape, 0) % 2).astype(F32)

    def fore(step, carry):
        cos, sin = carry
        for part, table in enumerate((cos, jnp.where(first_lane, sign, sin))):
            for odd in range(2):
                lane = slice(odd * quarter, (odd + 1) * quarter)
                to = slice(part * quarter, (part + 1) * quarter)
                forward[odd, aligned(step * STEP, STEP), to] = table[:, lane].astype(BF16)
        return turn(cos, sin, fore_rc[...], fore_rs[...])

    lax.fori_loop(0, forward.shape[1] // STEP, fore, (fore_c[...], fore_s[...]))
    near_out_c[...], near_out_s[...] = turn(near_c[...], near_s[...], base_c[place], base_s[place])


def inverse_tables_kernel(
    even_c, even_s, odd_c, odd_s, rows_rc, rows_rs, lift_c, lift_s, lift_rc, lift_rs, mid_c, mid_s,
    cols_c, cols_s, cols_rc, cols_rs,
    even_out, odd_out, lift_out_c, lift_out_s, cols_out, rows_out, bins_out,
):
    half_len = even_c.shape[1]
    quarter = half_len // 2
    first_len = cols_c.shape[1]
    per = first_len // 2

    def spread(out, cos, sin):
        def body(step, carry):
            cos, sin = carry
            upper = aligned(step * STEP, STEP)
            lower = aligned(quarter + step * STEP, STEP)
            for lane in range(0, half_len, PIECE):
                real, imag = slice(2 * lane, 2 * lane + PIECE), slice(2 * lane + PIECE, 2 * (lane + PIECE))
                cos_at, sin_at = cos[:, lane : lane + PIECE], sin[:, lane : lane + PIECE]
                out[upper, real] = cos_at.astype(BF16)
                out[upper, imag] = sin_at.astype(BF16)
                out[lower, real] = (-sin_at).astype(BF16)
                out[lower, imag] = cos_at.astype(BF16)
            return turn(cos, sin, rows_rc[...], rows_rs[...])

        lax.fori_loop(0, quarter // STEP, body, (cos, sin))

    spread(even_out, even_c[...], even_s[...])
    spread(odd_out, odd_c[...], odd_s[...])

    for parity in range(2):

        def lifts(step, carry, parity=parity):
            cos, sin = carry
            at = aligned(parity * per + step * STEP, STEP)
            lift_out_c[at, :] = cos
            lift_out_s[at, :] = sin
            return turn(cos, sin, lift_rc[...], lift_rs[...])

        lax.fori_loop(0, per // STEP, lifts, (lift_c[parity], lift_s[parity]))
    lift_out_c[0:STEP, :] = mid_c[...]
    lift_out_s[0:STEP, :] = mid_s[...]

    def columns(step, carry):
        cos, sin = carry
        upper = aligned(step * STEP, STEP)
        lower = aligned(per + step * STEP, STEP)
        for parity in range(2):
            at = slice(parity * per, (parity + 1) * per)
            left = slice(parity * first_len, parity * first_len + per)
            right = slice(parity * first_len + per, (parity + 1) * first_len)
            cols_out[upper, left] = cos[:, at].astype(BF16)
            cols_out[upper, right] = (-sin[:, at]).astype(BF16)
            cols_out[lower, left] = sin[:, at].astype(BF16)
            cols_out[lower, right] = cos[:, at].astype(BF16)
        return turn(cos, sin, cols_rc[...], cols_rs[...])

    lax.fori_loop(0, per // STEP, columns, (cols_c[...], cols_s[...]))
    sort_tables(lift_c.shape[1], rows_out, bins_out)


def stage_two_kernel(
    segs, cols, moved, near_c, near_s, mid_c_hbm, mid_s_hbm, forward, out,
    mid_c, mid_s, stacked, middle, product, sems,
):
    place, _ = position()
    _, half_len, _ = forward.shape
    second_len = 2 * half_len
    quarter = half_len // 2
    copies = start_copies([(mid_c_hbm, mid_c), (mid_s_hbm, mid_s)], sems)
    sources, rows, _ = moved.shape
    tail = segs * cols
    all_rows = (segs + 1) * rows
    width = 2 * cols
    low = lax.broadcasted_iota(jnp.int32, (rows, width), 1) < cols
    own_first = place == 0
    packed_row = lax.broadcasted_iota(jnp.int32, (rows, width), 0) == 0
    drop = jnp.logical_and(packed_row, own_first)

    def pair(left, right):
        return (
            jnp.where(low, left, pltpu.roll(right, cols, 1)),
            jnp.where(low, pltpu.roll(left, cols, 1), right),
        )

    middle[...] = jnp.zeros_like(middle)
    tiles = sources // 2
    for tile in range(tiles // 2):
        lane = slice(tile * width, (tile + 1) * width)
        lanes = (lane, slice(half_len + tile * width, half_len + (tile + 1) * width))

        def piece(lo, tile=tile):
            hi = lo + width
            found = []
            for source in (2 * tile, 2 * tile + tiles):
                found.append(
                    pair(moved[source, :, lo:hi].astype(F32), moved[source + 1, :, lo:hi].astype(F32))
                )
            return [(found[0][at], found[1][at]) for at in range(2)]

        def put(seg, real, imag, lane=lane, lanes=lanes):
            turned_real, turned_imag = [], []
            for half in range(2):
                middle[seg : seg + 1, lanes[half]] = imag[half][0:1, :]
                kept = jnp.where(drop, 0.0, imag[half])
                cos, sin = near_c[:, lanes[half]], near_s[:, lanes[half]]
                turned_real.append(real[half] * cos + kept * sin)
                turned_imag.append(kept * cos - real[half] * sin)
            for at, (low_half, high_half) in ((seg * rows, turned_real), (all_rows + seg * rows, turned_imag)):
                stacked[0, at : at + rows, lane] = (low_half + high_half).astype(BF16)
                stacked[1, at : at + rows, lane] = (low_half - high_half).astype(BF16)

        for twin in range(segs // 2):
            real_one, real_two = piece(twin * width)
            imag_one, imag_two = piece(tail + twin * width)
            put(2 * twin, real_one, imag_one)
            put(2 * twin + 1, real_two, imag_two)
        real, imag = piece(2 * tail)
        put(segs, real, imag)
    for copy in copies:
        copy.wait()
    for part, turned in enumerate((middle[...] * mid_c[...], middle[...] * -mid_s[...])):
        at = slice(2 * all_rows + part * rows, 2 * all_rows + (part + 1) * rows)
        stacked[0, at, :] = (turned[:, :half_len] + turned[:, half_len:]).astype(BF16)
        stacked[1, at, :] = (turned[:, :half_len] - turned[:, half_len:]).astype(BF16)

    first_lane = lax.broadcasted_iota(jnp.int32, (rows, quarter), 1) == 0
    swap = jnp.logical_and(lax.broadcasted_iota(jnp.int32, (rows, quarter), 0) == 0, own_first)
    floor = 0.2 * (second_len * 2 * sources * rows)
    upper, lower = [], []
    for odd in range(2):
        cos_at = slice(odd * half_len, odd * half_len + quarter)
        sin_at = slice(odd * half_len + quarter, (odd + 1) * half_len)
        product[:, odd * half_len : (odd + 1) * half_len] = matmul(stacked[odd], forward[odd])

        def parts(at, lower_at, cos_at=cos_at, sin_at=sin_at):
            return (
                product[at : at + rows, cos_at],
                product[at : at + rows, sin_at],
                product[lower_at : lower_at + rows, cos_at],
                product[lower_at : lower_at + rows, sin_at],
            )

        def direct_of(rc, rs, ic, imag_s, odd=odd):
            if not odd:
                rs, imag_s = jnp.where(first_lane, 0.0, rs), jnp.where(first_lane, 0.0, imag_s)
            return rc + imag_s, ic - rs

        def mirror_of(rc, rs, ic, imag_s, odd=odd):
            real, imag = rc - imag_s, ic + rs
            if not odd:
                real, imag = jnp.where(first_lane, rs, real), jnp.where(first_lane, imag_s, imag)
            return real, imag

        level = jnp.zeros((rows, quarter), F32)
        mirror_level = level
        for seg in range(segs):
            four = parts(seg * rows, all_rows + seg * rows)
            real, imag = direct_of(*four)
            level = level + (real * real + imag * imag)
            real, imag = mirror_of(*four)
            mirror_level = mirror_level + (real * real + imag * imag)
        four = parts(segs * rows, all_rows + segs * rows)
        real, imag = direct_of(*four)
        mirror_real, mirror_imag = mirror_of(*four)
        mid_real, mid_imag = mirror_of(*parts(2 * all_rows, 2 * all_rows + rows))
        mid_level = jnp.sum((mid_real * mid_real + mid_imag * mid_imag)[:segs], 0, keepdims=True)
        mirror_level = jnp.where(swap, mid_level, mirror_level)
        mirror_real = jnp.where(swap, mid_real[segs : segs + 1], mirror_real)
        mirror_imag = jnp.where(swap, mid_imag[segs : segs + 1], mirror_imag)
        level = jnp.maximum(level * (1.0 / segs), floor)
        mirror_level = jnp.maximum(mirror_level * (1.0 / segs), floor)
        upper.append((real / level, imag / level, 1.0 / level))
        lower.append((mirror_real / mirror_level, -mirror_imag / mirror_level, 1.0 / mirror_level))
    eighth = rows // 2
    for part in range(3):
        mirrored = (lower[1][part], pltpu.roll(lower[0][part], quarter - 1, 1))
        for odd in range(2):
            lane = slice(part * half_len + odd * quarter, part * half_len + (odd + 1) * quarter)
            for parity in range(2):
                at = slice(parity * eighth, (parity + 1) * eighth)
                block = jnp.concatenate([upper[odd][part][at], mirrored[odd][at]], 0)
                out[parity * rows : (parity + 1) * rows, lane] = block.astype(BF16)


def sort_tables(rows, rows_out, bins_out):
    _, per, _ = rows_out.shape
    _, group = position()

    def one_hot(mask):
        return jnp.where(mask, 1.0, 0.0).astype(BF16)

    at = lax.broadcasted_iota(jnp.int32, (per, per), 0)
    lane = lax.broadcasted_iota(jnp.int32, (per, per), 1)
    for turned in range(2):
        row = packed_row_of(at, turned, 2 * per, rows)
        share = (row // rows) % 2
        source = row // (2 * rows) - turned * (per // (2 * rows))
        column = source * rows + row % rows + jnp.where(share == group, 0, per // 2)
        rows_out[turned] = one_hot(column == lane)
    wide = bins_out.shape[0]
    at = lax.broadcasted_iota(jnp.int32, (wide, wide), 0)
    lane = lax.broadcasted_iota(jnp.int32, (wide, wide), 1)
    bins_out[...] = one_hot(at == jnp.where(lane < wide // 2, 2 * lane, 2 * lane - wide + 1))


def packed_row_of(at, turned, first_len, rows):
    half = first_len // 4
    packed = at % half // (rows // 2) * rows + 2 * (at % (rows // 2)) + at // half
    if not turned:
        return packed
    return jnp.where(packed == 0, first_len // 2, first_len - packed)


def choose_kernel(order, cuts, own, other, by_rows, by_bins, out, held):
    place, _ = position()
    sources, rows, _ = own.shape
    per = sources * rows
    half_len = own.shape[2] // 2
    for source in range(sources):
        turned, at = source // (sources // 2), source % (sources // 2) * rows
        held[turned, at : at + rows, :] = own[source]
        held[turned, per // 2 + at : per // 2 + at + rows, :] = other[source]
    cut = cuts[order[place]]
    moved, room = [], []
    for turned in range(2):
        moved.append(matmul(by_rows[turned], held[turned]).reshape(per // (rows // 2), rows // 2, 2 * half_len))
        at = lax.broadcasted_iota(jnp.int32, (per, 128), 0)
        room.append((cut - packed_row_of(at, turned, 2 * per, rows)).reshape(per // (rows // 2), rows // 2, 128))
    picked = jnp.concatenate(moved, 1).reshape(2 * per, 2 * half_len).astype(BF16)
    room = jnp.concatenate(room, 1).reshape(2 * per, 128)
    wide = by_bins.shape[0]
    for part in range(2):
        for block in range(half_len // wide):
            lane = part * half_len + block * wide
            sorted_bins = matmul(picked[:, lane : lane + wide], by_bins[...])
            for odd in range(2):
                for at in range(0, wide // 2, 128):
                    first = block * (wide // 2) + at
                    bins = 2 * (first + lax.broadcasted_iota(jnp.int32, (1, 128), 1)) + odd
                    from_lane = odd * (wide // 2) + at
                    kept = jnp.where(
                        2 * per * bins < room, sorted_bins[:, from_lane : from_lane + 128], 0.0
                    )
                    to = part * half_len + odd * (half_len // 2) + first
                    out[:, to : to + 128] = kept.astype(BF16)


def filter_blocks(offsets, blocks, chosen, tables, norm, filtered, lifted):
    place, _ = position()
    even_table, odd_table, lift_c, lift_s = tables
    half_len = even_table.shape[0]
    quarter = half_len // 2
    first_len = chosen.shape[0]
    per = first_len // 2
    rows = blocks[0].shape[0] // 2
    groups = []
    for block, offset in zip(blocks, offsets):
        device = jnp.bitwise_xor(place, offset)
        for parity in range(2):
            row = slice(parity * rows, (parity + 1) * rows)
            at = aligned(parity * per + device * rows, rows)
            white_real = block[row, :half_len].astype(F32)
            white_imag = block[row, half_len : 2 * half_len].astype(F32)
            weight = block[row, 2 * half_len :].astype(F32)
            real = chosen[at, :half_len].astype(F32)
            imag = chosen[at, half_len:].astype(F32)
            norm = norm + (real * real + imag * imag) * weight
            filt_real = (white_real * real + white_imag * imag).astype(BF16)
            filt_imag = (white_imag * real - white_real * imag).astype(BF16)
            to = slice(len(groups) * rows, (len(groups) + 1) * rows)
            filtered[to, 0:quarter] = filt_real[:, :quarter]
            filtered[to, quarter:half_len] = filt_imag[:, :quarter]
            filtered[to, half_len : half_len + quarter] = filt_real[:, quarter:]
            filtered[to, half_len + quarter :] = filt_imag[:, quarter:]
            groups.append((to, at, parity * first_len + device * rows))
    for lane in range(0, half_len, PIECE):
        both = slice(2 * lane, 2 * (lane + PIECE))
        even = matmul(filtered[:, :half_len], even_table[:, both])
        odd = matmul(filtered[:, half_len:], odd_table[:, both])
        for upper in range(2):
            lanes = slice(upper * half_len + lane, upper * half_len + lane + PIECE)
            total = even - odd if upper else even + odd
            for row, at, target in groups:
                real, imag = total[row, :PIECE], total[row, PIECE:]
                cos, sin = lift_c[at, lanes], lift_s[at, lanes]
                lifted[aligned(target, rows), lanes] = (real * cos - imag * sin).astype(BF16)
                lifted[aligned(target + per, rows), lanes] = (real * sin + imag * cos).astype(BF16)
    return norm


def early_kernel(near, theirs, both, far, chosen, *refs):
    tables, (lifted, norm, filtered) = refs[:4], refs[4:]
    blocks = [*[near.at[at] for at in range(4)], *[theirs.at[at] for at in range(4)], both.at[0], both.at[1], far]
    zero = jnp.zeros(norm.shape, F32)
    norm[...] = filter_blocks(EARLY, blocks, chosen, tables, zero, filtered, lifted)


def middle_kernel(theirs, early, early_norm, chosen, *refs):
    tables, (lifted, norm, filtered) = refs[:4], refs[4:]
    blocks = [theirs.at[at] for at in range(3)]
    norm[...] = filter_blocks(MIDDLE, blocks, chosen, tables, early_norm[...], filtered, lifted)


def late_kernel(last, theirs, early, early_norm, chosen, *refs):
    tables, (cols_table, out, lifted, filtered, result, sems) = refs[:4], refs[4:]
    norm = filter_blocks(LATE, [last, theirs], chosen, tables, early_norm[...], filtered, lifted)
    scale = lax.rsqrt(jnp.sum(norm, keepdims=True))
    first_len = chosen.shape[0]
    per = first_len // 2
    wide = 256
    lanes = [slice(lane, lane + wide) for lane in range(0, lifted.shape[1], wide)]

    def products(at):
        return (
            matmul(cols_table[:, :first_len], lifted[:first_len, at]),
            matmul(cols_table[:, first_len:], lifted[first_len:, at]),
        )

    copies = []
    following = products(lanes[0])
    for block, at in enumerate(lanes):
        even, odd = following
        if block + 1 < len(lanes):
            following = products(lanes[block + 1])
        for upper in range(2):
            total = even - odd if upper else even + odd
            power = total[:per] * total[:per] + total[per:] * total[per:]
            size = power * lax.rsqrt(jnp.maximum(power, 1e-37))
            result[upper * per : (upper + 1) * per, at] = (size * scale).astype(BF16)
        copies.append(pltpu.make_async_copy(result.at[:, at], out.at[0, :, at], sems.at[block]))
        copies[-1].start()
    for copy in copies:
        copy.wait()


def swap_with(array, flip):
    pairs = [(at, at ^ flip) for at in range(lax.axis_size("tmpl"))]
    return lax.ppermute(array, "tmpl", pairs)


def tiled_local(strain, analysis, bank, cutoff, order):
    dev_count = lax.axis_size("tmpl")
    segs, first_len, cols = strain.shape
    second_len = cols * dev_count
    length = first_len * second_len
    half_len = second_len // 2
    rows = first_len // dev_count // 2
    templates = order.shape[0]
    lanes = 2 * (segs + 1) * cols

    first, second, half = np.arange(first_len), np.arange(second_len), np.arange(half_len)
    devices, step = np.arange(dev_count), np.arange(STEP)
    near = halves(rows)
    packed = (devices[:, None] * rows + near[None, :]).reshape(dev_count, 2, rows // 2)
    waves = []
    for odd in range(2):
        cos, sin = turns(packed[:, odd].reshape(-1, 1) * first[None, : first_len // 2], first_len)
        if not odd:
            sin[0] = 2 * (first[: first_len // 2] % 2) - 1.0
        waves.append(np.concatenate([cos, -sin]))
    win = np.stack(turns(np.arange(8)[:, None] + second_len * first[None, :], length))
    spin = np.stack(turns(cols * devices, length), 1)[:, :, None] * np.ones((1, 1, first_len), np.float32)
    turns_of_eight = [tuple(float(at) for at in turns(8 * block, length)) for block in range(cols // 8)]

    sent = pl.pallas_call(
        functools.partial(stage_one_kernel, turns_of_eight),
        in_specs=[outside()] * 7,
        out_specs=whole(),
        scratch_shapes=[
            pltpu.SMEM((templates,), jnp.int32),
            vmem((segs, cols, first_len), F32),
            vmem((cols, first_len), F32),
            vmem((2, first_len), F32),
            vmem((2, 8, first_len), F32),
            vmem((2, dev_count * rows, first_len // 2)),
            vmem((2, (segs + 1) * cols, first_len // 2)),
            pltpu.SemaphoreType.DMA((segs + 5,)),
            pltpu.SemaphoreType.DMA((2 * templates,)),
        ],
        out_shape=pltpu.VMEM((dev_count * rows, lanes + 2 * half_len), BF16),
        compiler_params=params(16),
        name="stage_one",
    )(
        *in_hbm(
            order, jnp.swapaxes(strain, 1, 2), jnp.swapaxes(analysis, 0, 1), spin, win,
            np.stack(waves).astype(BF16), bank,
        ),
    )
    moved = lax.all_to_all(
        sent.reshape(dev_count, rows, lanes + 2 * half_len), "tmpl", split_axis=0, concat_axis=0, tiled=True
    )
    own = moved[:, :, lanes:]
    other = lax.ppermute(own, "grp", [(0, 1), (1, 0)])

    split = halves(half_len)
    low = 2 * np.arange(rows // 2)
    lift_rows = [np.concatenate([low + odd, first_len - low - odd]) for odd in range(2)]
    lift_init = [turns(at[:, None] * second[None, :], length) for at in lift_rows]
    cols_parts = []
    for odd in range(2):
        straight = devices[:, None] * rows + low[None, :] + odd
        turned = np.where(straight == 0, first_len // 2, first_len - straight)
        cols_parts.append(np.concatenate([straight, turned], 1).reshape(-1))
    cols_rows = np.concatenate(cols_parts)
    mid_rows = lift_rows[0].copy()
    mid_rows[rows // 2] = first_len // 2
    step_sign = np.where(np.arange(rows) < rows // 2, rows, -rows)
    fore = [
        *turns(step[:, None] * split[None, :], second_len),
        *turns(STEP * split[None, :], second_len),
        *turns(near[:, None] * second[None, :], length),
        *turns(rows * devices[:, None, None] * second[None, None, :], length),
    ]
    forward, near_c, near_s = pl.pallas_call(
        forward_kernel,
        out_shape=[
            pltpu.VMEM((2, half_len, half_len), BF16),
            *[pltpu.VMEM((rows, second_len), F32)] * 2,
        ],
        in_specs=[whole()] * len(fore),
        out_specs=[whole()] * 3,
        compiler_params=params(16),
        cost_estimate=pl.CostEstimate(flops=10**7, bytes_accessed=2 * 10**7, transcendentals=0),
        name="forward_tables",
    )(*in_hbm(*fore))
    back = [
        *turns(2 * step[:, None] * half[None, :], second_len),
        *turns((2 * step[:, None] + 1) * half[None, :], second_len),
        *turns(2 * STEP * half[None, :], second_len),
        np.stack([lift_init[0][0], lift_init[1][0]]),
        np.stack([lift_init[0][1], lift_init[1][1]]),
        *turns(step_sign[:, None] * second[None, :], length),
        *turns(mid_rows[:, None] * second[None, :], length),
        *turns(step[:, None] * cols_rows[None, :], first_len),
        *turns(STEP * cols_rows[None, :], first_len),
    ]
    shapes = [
        ((half_len, second_len), BF16),
        ((half_len, second_len), BF16),
        ((first_len, second_len), F32),
        ((first_len, second_len), F32),
        ((first_len, 2 * first_len), BF16),
        ((2, first_len // 2, first_len // 2), BF16),
        ((256, 256), BF16),
    ]
    inverse_tables = pl.pallas_call(
        inverse_tables_kernel,
        out_shape=[pltpu.VMEM(*shape) for shape in shapes],
        in_specs=[whole()] * len(back),
        out_specs=[whole()] * len(shapes),
        compiler_params=params(8),
        cost_estimate=pl.CostEstimate(flops=10**7, bytes_accessed=2 * 10**7, transcendentals=0),
        name="inverse_tables",
    )
    even_table, odd_table, lift_c, lift_s, cols_table, by_rows, by_bins = inverse_tables(*in_hbm(*back))

    mid_c, mid_s = turns(first_len // 2 * second[None, :], length)
    all_rows = 2 * (segs + 2) * rows
    stage_two = pl.pallas_call(
        functools.partial(stage_two_kernel, segs, cols),
        out_shape=jax.ShapeDtypeStruct((2 * rows, 3 * half_len), BF16),
        in_specs=[whole()] * 3 + [outside()] * 2 + [whole()],
        out_specs=whole(),
        scratch_shapes=[
            *[vmem((1, second_len), F32)] * 2,
            vmem((2, all_rows, half_len)),
            vmem((rows, second_len), F32),
            vmem((all_rows, second_len), F32),
            pltpu.SemaphoreType.DMA((2,)),
        ],
        compiler_params=params(24),
        cost_estimate=pl.CostEstimate(flops=10**9, bytes_accessed=4 * 10**6, transcendentals=0),
        name="stage_two",
    )
    block = stage_two(moved, *in_vmem(near_c, near_s), *in_hbm(mid_c, mid_s), *in_vmem(forward))

    two = swap_with(block, 8)
    one = swap_with(block, 4)
    beside = swap_with(block, 2)
    both = swap_with(jnp.stack([one, two]), 2)
    far = swap_with(two, 4)
    near = jnp.stack([block, beside, one, two])
    theirs = swap_with(near, 1)
    last = swap_with(far, 2)
    more = swap_with(jnp.stack([both[0], both[1], far]), 1)
    late = swap_with(last, 1)

    choose = pl.pallas_call(
        choose_kernel,
        grid_spec=pltpu.PrefetchScalarGridSpec(
            num_scalar_prefetch=2,
            grid=(),
            in_specs=[whole()] * 4,
            out_specs=whole(),
            scratch_shapes=[vmem((2, first_len // 2, 2 * half_len))],
        ),
        out_shape=jax.ShapeDtypeStruct((first_len, 2 * half_len), BF16),
        compiler_params=params(16),
        cost_estimate=pl.CostEstimate(flops=10**9, bytes_accessed=4 * 10**6, transcendentals=0),
        name="choose",
    )
    chosen = choose(order, cutoff, own, other, *in_vmem(by_rows, by_bins))

    spread = [(2 * first_len, second_len), BF16]
    tables = in_vmem(even_table, odd_table, lift_c, lift_s)
    early = pl.pallas_call(
        early_kernel,
        out_shape=[pltpu.VMEM(*spread), pltpu.VMEM((rows, half_len), F32)],
        in_specs=[whole()] * 9,
        out_specs=[whole()] * 2,
        scratch_shapes=[vmem((len(EARLY) * 2 * rows, 2 * half_len))],
        compiler_params=params(16),
        cost_estimate=pl.CostEstimate(flops=10**9, bytes_accessed=4 * 10**6, transcendentals=0),
        name="early",
    )
    lifted, norm = early(near, theirs, both, far, chosen, *tables)
    middle = pl.pallas_call(
        middle_kernel,
        out_shape=[pltpu.VMEM(*spread), pltpu.VMEM((rows, half_len), F32)],
        in_specs=[whole()] * 8,
        out_specs=[whole()] * 2,
        scratch_shapes=[vmem((len(MIDDLE) * 2 * rows, 2 * half_len))],
        input_output_aliases={1: 0},
        compiler_params=params(16),
        cost_estimate=pl.CostEstimate(flops=10**9, bytes_accessed=4 * 10**6, transcendentals=0),
        name="middle",
    )
    lifted, norm = middle(more, *in_vmem(lifted, norm), chosen, *tables)
    result, _ = pl.pallas_call(
        late_kernel,
        out_shape=[pltpu.HBM((1, first_len, second_len), BF16), pltpu.VMEM(*spread)],
        in_specs=[whole()] * 10,
        out_specs=[outside(), whole()],
        scratch_shapes=[
            vmem((len(LATE) * 2 * rows, 2 * half_len)),
            vmem((first_len, second_len)),
            pltpu.SemaphoreType.DMA((second_len // 256,)),
        ],
        input_output_aliases={2: 1},
        compiler_params=params(16),
        name="late",
    )(last, late, *in_vmem(lifted, norm), chosen, *tables, *in_vmem(cols_table))
    return result


def angles(left_idx, right_idx, period):
    product = left_idx[:, None] * right_idx[None, :] % period
    phase_angle = product.astype(jnp.float32) * (2.0 * math.pi / period)
    return (jnp.cos(phase_angle), jnp.sin(phase_angle))


def filtered(white_pair, tmpl_pair, cut_bins, freq_bin):
    white_real = white_pair[0].astype(jnp.float32)
    white_imag = white_pair[1].astype(jnp.float32)
    tmpl_real = tmpl_pair[0].astype(jnp.float32)
    tmpl_imag = tmpl_pair[1].astype(jnp.float32)
    in_band = freq_bin[None] < cut_bins[:, None, None]
    filt_real = jnp.where(in_band, white_real * tmpl_real + white_imag * tmpl_imag, 0.0)
    filt_imag = jnp.where(in_band, white_imag * tmpl_real - white_real * tmpl_imag, 0.0)
    return jnp.concatenate([filt_real, filt_imag], -1).astype(jnp.bfloat16)


def inverse_rows(stacked, row_bins, second_len, length):
    half_len = second_len // 2
    cosine, sine = angles(
        jnp.arange(half_len, dtype=jnp.int32), jnp.arange(second_len, dtype=jnp.int32), second_len
    )
    dft_table = jnp.concatenate(
        [jnp.concatenate([cosine, sine], 1), jnp.concatenate([-sine, cosine], 1)], 0
    ).astype(jnp.bfloat16)
    spread = jnp.einsum("tkf,fg->tkg", stacked, dft_table, preferred_element_type=jnp.float32)
    spread_real = spread[..., :second_len]
    spread_imag = spread[..., second_len:]
    cos_twist, sin_twist = angles(row_bins, jnp.arange(second_len, dtype=jnp.int32), length)
    lift_real = spread_real * cos_twist - spread_imag * sin_twist
    lift_imag = spread_real * sin_twist + spread_imag * cos_twist
    return jnp.concatenate([lift_real, lift_imag], -1).astype(jnp.bfloat16)


def inverse_cols(lifted, first_len, second_len):
    row_idx = jnp.arange(first_len, dtype=jnp.int32)
    cosine, sine = angles(row_idx, row_idx, first_len)
    cosine = cosine.astype(jnp.bfloat16)
    sine = sine.astype(jnp.bfloat16)
    lift_real = lifted[..., :second_len]
    lift_imag = lifted[..., second_len:]
    field_real = jnp.einsum(
        "ak,tkb->tab", cosine, lift_real, preferred_element_type=jnp.float32
    ) - jnp.einsum("ak,tkb->tab", sine, lift_imag, preferred_element_type=jnp.float32)
    field_imag = jnp.einsum(
        "ak,tkb->tab", sine, lift_real, preferred_element_type=jnp.float32
    ) + jnp.einsum("ak,tkb->tab", cosine, lift_imag, preferred_element_type=jnp.float32)
    return (field_real, field_imag)


def plain_local(strain, analysis, bank, cutoff, order):
    highest = lax.Precision.HIGHEST
    dev_count = lax.axis_size("tmpl")
    my_index = lax.axis_index("tmpl")
    seg_count = strain.shape[0]
    first_len = strain.shape[1]
    col_count = strain.shape[2]
    second_len = col_count * dev_count
    length = first_len * second_len
    half_len = second_len // 2
    row_count = first_len // dev_count
    row_idx = jnp.arange(first_len, dtype=jnp.int32)
    col_index = my_index * col_count + jnp.arange(col_count, dtype=jnp.int32)
    sample_idx = row_idx[:, None] * second_len + col_index[None, :]
    window = (
        math.sqrt(8.0 / 3.0) * jnp.sin(sample_idx.astype(jnp.float32) * (math.pi / length)) ** 2
    )
    series = jnp.concatenate([strain * window, analysis[None]], 0)
    cos_one, sin_one = angles(row_idx, row_idx, first_len)
    part_real = jnp.einsum("ka,sab->skb", cos_one, series, precision=highest)
    part_imag = -jnp.einsum("ka,sab->skb", sin_one, series, precision=highest)
    cos_twist, sin_twist = angles(row_idx, col_index, length)
    twist_real = part_real * cos_twist + part_imag * sin_twist
    twist_imag = part_imag * cos_twist - part_real * sin_twist
    moved = lax.all_to_all(
        jnp.stack([twist_real, twist_imag]).astype(jnp.bfloat16),
        "tmpl",
        split_axis=2,
        concat_axis=3,
        tiled=True,
    ).astype(jnp.float32)
    cos_two, sin_two = angles(
        jnp.arange(second_len, dtype=jnp.int32), jnp.arange(half_len, dtype=jnp.int32), second_len
    )
    spec_real = jnp.einsum("skb,bf->skf", moved[0], cos_two, precision=highest) + jnp.einsum(
        "skb,bf->skf", moved[1], sin_two, precision=highest
    )
    spec_imag = jnp.einsum("skb,bf->skf", moved[1], cos_two, precision=highest) - jnp.einsum(
        "skb,bf->skf", moved[0], sin_two, precision=highest
    )
    power_spec = jnp.maximum(
        jnp.mean(spec_real[:seg_count] ** 2 + spec_imag[:seg_count] ** 2, axis=0), 0.2 * length
    )
    whitened = jnp.stack(
        [spec_real[seg_count] / power_spec, spec_imag[seg_count] / power_spec]
    ).astype(jnp.bfloat16)
    own_rows = my_index * row_count + jnp.arange(row_count, dtype=jnp.int32)
    half_idx = jnp.arange(half_len, dtype=jnp.int32)
    freq_local = own_rows[:, None] + first_len * half_idx[None, :]
    chosen = jnp.take(bank, order, axis=1)
    cuts = jnp.take(cutoff, order)
    bank_real = chosen[0].astype(jnp.float32)
    bank_imag = chosen[1].astype(jnp.float32)
    in_band = freq_local[None] < cuts[:, None, None]
    local_norm = jnp.sum(
        jnp.where(in_band, (bank_real**2 + bank_imag**2) / power_spec, 0.0), axis=(1, 2)
    )
    norm_sq = lax.psum(local_norm, "tmpl")
    per_device = cuts.shape[0] // dev_count
    own_norm = lax.dynamic_slice_in_dim(norm_sq, my_index * per_device, per_device)
    stacked = filtered(whitened, chosen, cuts, freq_local)
    lifted = lax.all_to_all(
        inverse_rows(stacked, own_rows, second_len, length),
        "tmpl",
        split_axis=0,
        concat_axis=1,
        tiled=True,
    )
    field_real, field_imag = inverse_cols(lifted, first_len, second_len)
    magnitude = jnp.sqrt(field_real**2 + field_imag**2)
    return (magnitude / jnp.sqrt(own_norm)[:, None, None]).astype(jnp.bfloat16)


def local(strain, analysis, bank, cutoff, order):
    dev_count, segs, cols = lax.axis_size("tmpl"), strain.shape[0], strain.shape[2]
    rows = strain.shape[1] // dev_count // 2
    fits = rows == STEP and cols == 64 and segs % 2 == 0 and dev_count == len(EARLY + MIDDLE + LATE)
    if fits and order.shape[0] == dev_count and lax.axis_size("grp") == 2:
        return tiled_local(strain, analysis, bank, cutoff, order)
    return plain_local(strain, analysis, bank, cutoff, order)


def solution(mesh):
    return jax.shard_map(
        local,
        mesh=mesh,
        in_specs=(P("grp", None, "tmpl"), P("grp", "tmpl"), P(None, None, "tmpl", None), P(), P()),
        out_specs=P(("grp", "tmpl"), None, None),
        check_vma=False,
    )
```

```python
import functools
import math

import jax
import jax.numpy as jnp
import numpy as np
from jax import lax
from jax.experimental import pallas as pl
from jax.experimental.pallas import tpu as pltpu
from jax.sharding import PartitionSpec as P

BF16 = jnp.bfloat16
F32 = jnp.float32
STEP = 16
PIECE = 128
EARLY = (0, 2, 4, 8, 1, 3, 5, 9)
MIDDLE = (6, 10, 12, 7, 11, 13)
LATE = (14, 15)


def turns(product, period):
    angle = (product % period) * (2.0 * math.pi / period)
    return np.cos(angle).astype(np.float32), np.sin(angle).astype(np.float32)


def matmul(left, right):
    return jnp.dot(left, right, preferred_element_type=F32)


def matmul_nt(left, right):
    return lax.dot_general(left, right, (((1,), (1,)), ((), ())), preferred_element_type=F32)


def vmem(shape, dtype=BF16):
    return pltpu.VMEM(shape, dtype)


def whole():
    return pl.BlockSpec(memory_space=pltpu.VMEM)


def outside():
    return pl.BlockSpec(memory_space=pltpu.HBM)


def in_hbm(*arrays):
    return [pltpu.with_memory_space_constraint(jnp.asarray(array), pltpu.HBM) for array in arrays]


def in_vmem(*arrays):
    return [pltpu.with_memory_space_constraint(array, pltpu.VMEM) for array in arrays]


def position():
    return lax.axis_index("tmpl"), lax.axis_index("grp")


def start_copies(pairs, sems):
    copies = [
        pltpu.make_async_copy(source, target, sems.at[at]) for at, (source, target) in enumerate(pairs)
    ]
    for copy in copies:
        copy.start()
    return copies


def params(mib):
    return pltpu.CompilerParams(vmem_limit_bytes=mib << 20)


def turn(cos, sin, by_cos, by_sin):
    return cos * by_cos - sin * by_sin, sin * by_cos + cos * by_sin


def halves(count):
    return np.concatenate([np.arange(0, count, 2), np.arange(1, count, 2)])


def aligned(start, size):
    return pl.ds(pl.multiple_of(start, size), size)


def stage_one_kernel(
    turns_of_eight, order_hbm, strain_hbm, analysis_hbm, spin_hbm, win_hbm, wave_hbm, bank, out,
    order, strain, analysis, spin, win, wave, packed, sems, bank_sem,
):
    segs, cols, first_len = strain.shape
    tail = segs * cols
    templates, half_len = bank.shape[1], bank.shape[3]
    rows = out.shape[0] // templates
    half = first_len // 2
    place, group = position()
    sources = [
        (order_hbm, order),
        (spin_hbm.at[place], spin),
        (win_hbm, win),
        *[(strain_hbm.at[seg], strain.at[seg]) for seg in range(segs)],
        (analysis_hbm, analysis),
        (wave_hbm, wave),
    ]
    copies = start_copies(sources, sems)
    lane = 2 * (tail + cols)
    for copy in copies[:3]:
        copy.wait()
    bank_pairs = []
    for row in range(templates):
        for part in range(2):
            bank_pairs.append(
                (
                    bank.at[part, order[row], aligned(group * rows, rows), :],
                    out.at[
                        row * rows : (row + 1) * rows,
                        lane + part * half_len : lane + (part + 1) * half_len,
                    ],
                )
            )
    for source, target in bank_pairs:
        pltpu.make_async_copy(source, target, bank_sem).start()
    scale = 0.5 * math.sqrt(8.0 / 3.0)
    win_c, win_s = turn(win[0], win[1], spin[0:1, :], spin[1:2, :])
    window = jnp.concatenate(
        [scale - (win_c * (scale * by_cos) - win_s * (scale * by_sin)) for by_cos, by_sin in turns_of_eight], 0
    )

    def pack(at, values):
        packed[0, at : at + cols, :] = (values[:, :half] + values[:, half:]).astype(BF16)
        packed[1, at : at + cols, :] = (values[:, :half] - values[:, half:]).astype(BF16)

    for seg in range(segs):
        copies[3 + seg].wait()
        pack(seg * cols, strain[seg] * window)
    copies[3 + segs].wait()
    pack(tail, analysis[...])
    copies[4 + segs].wait()
    both = [matmul_nt(wave[odd], packed[odd]) for odd in range(2)]
    count = out.shape[0] // 2

    def woven(part):
        halves_of = [
            table[part * count : (part + 1) * count].reshape(templates, rows // 2, tail + cols) for table in both
        ]
        return jnp.concatenate(halves_of, 1).reshape(2 * count, tail + cols)

    real, imag = woven(0), woven(1)
    out[:, 0:tail] = real[:, :tail].astype(BF16)
    out[:, tail : 2 * tail] = imag[:, :tail].astype(BF16)
    joined = jnp.concatenate([real[:, tail:], imag[:, tail:]], 1)
    out[:, 2 * tail : lane] = joined.astype(BF16)
    whole_bank = out.at[:, lane:]
    pltpu.make_async_copy(whole_bank, whole_bank, bank_sem).wait()


def forward_kernel(
    fore_c, fore_s, fore_rc, fore_rs, near_c, near_s, base_c, base_s,
    forward, near_out_c, near_out_s,
):
    half_len = fore_c.shape[1]
    quarter = half_len // 2
    place, _ = position()
    first_lane = lax.broadcasted_iota(jnp.int32, fore_c.shape, 1) == 0
    sign = 1.0 - 2.0 * (lax.broadcasted_iota(jnp.int32, fore_c.shape, 0) % 2).astype(F32)

    def fore(step, carry):
        cos, sin = carry
        for part, table in enumerate((cos, jnp.where(first_lane, sign, sin))):
            for odd in range(2):
                lane = slice(odd * quarter, (odd + 1) * quarter)
                to = slice(part * quarter, (part + 1) * quarter)
                forward[odd, aligned(step * STEP, STEP), to] = table[:, lane].astype(BF16)
        return turn(cos, sin, fore_rc[...], fore_rs[...])

    lax.fori_loop(0, forward.shape[1] // STEP, fore, (fore_c[...], fore_s[...]))
    near_out_c[...], near_out_s[...] = turn(near_c[...], near_s[...], base_c[place], base_s[place])


def inverse_tables_kernel(
    even_c, even_s, odd_c, odd_s, rows_rc, rows_rs, lift_c, lift_s, lift_rc, lift_rs, mid_c, mid_s,
    even_out, odd_out, lift_out_c, lift_out_s,
):
    half_len = even_c.shape[1]
    quarter = half_len // 2
    per = lift_out_c.shape[0] // 2

    def spread(out, cos, sin):
        def body(step, carry):
            cos, sin = carry
            upper = aligned(step * STEP, STEP)
            lower = aligned(quarter + step * STEP, STEP)
            for lane in range(0, half_len, PIECE):
                real, imag = slice(2 * lane, 2 * lane + PIECE), slice(2 * lane + PIECE, 2 * (lane + PIECE))
                cos_at, sin_at = cos[:, lane : lane + PIECE], sin[:, lane : lane + PIECE]
                out[upper, real] = cos_at.astype(BF16)
                out[upper, imag] = sin_at.astype(BF16)
                out[lower, real] = (-sin_at).astype(BF16)
                out[lower, imag] = cos_at.astype(BF16)
            return turn(cos, sin, rows_rc[...], rows_rs[...])

        lax.fori_loop(0, quarter // STEP, body, (cos, sin))

    spread(even_out, even_c[...], even_s[...])
    spread(odd_out, odd_c[...], odd_s[...])

    for parity in range(2):

        def lifts(step, carry, parity=parity):
            cos, sin = carry
            at = aligned(parity * per + step * STEP, STEP)
            lift_out_c[at, :] = cos
            lift_out_s[at, :] = sin
            return turn(cos, sin, lift_rc[...], lift_rs[...])

        lax.fori_loop(0, per // STEP, lifts, (lift_c[parity], lift_s[parity]))
    lift_out_c[0:STEP, :] = mid_c[...]
    lift_out_s[0:STEP, :] = mid_s[...]


def column_tables_kernel(rows, cols_c, cols_s, cols_rc, cols_rs, cols_out, rows_out, bins_out):
    first_len = cols_c.shape[1]
    per = first_len // 2

    def columns(step, carry):
        cos, sin = carry
        upper = aligned(step * STEP, STEP)
        lower = aligned(per + step * STEP, STEP)
        for parity in range(2):
            at = slice(parity * per, (parity + 1) * per)
            left = slice(parity * first_len, parity * first_len + per)
            right = slice(parity * first_len + per, (parity + 1) * first_len)
            cols_out[upper, left] = cos[:, at].astype(BF16)
            cols_out[upper, right] = (-sin[:, at]).astype(BF16)
            cols_out[lower, left] = sin[:, at].astype(BF16)
            cols_out[lower, right] = cos[:, at].astype(BF16)
        return turn(cos, sin, cols_rc[...], cols_rs[...])

    lax.fori_loop(0, per // STEP, columns, (cols_c[...], cols_s[...]))
    sort_tables(rows, rows_out, bins_out)


def stage_two_kernel(
    segs, cols, moved, near_c, near_s, mid_c_hbm, mid_s_hbm, forward, out,
    mid_c, mid_s, stacked, middle, product, sems,
):
    place, _ = position()
    _, half_len, _ = forward.shape
    second_len = 2 * half_len
    quarter = half_len // 2
    copies = start_copies([(mid_c_hbm, mid_c), (mid_s_hbm, mid_s)], sems)
    sources, rows, _ = moved.shape
    tail = segs * cols
    all_rows = (segs + 1) * rows
    width = 2 * cols
    low = lax.broadcasted_iota(jnp.int32, (rows, width), 1) < cols
    own_first = place == 0
    packed_row = lax.broadcasted_iota(jnp.int32, (rows, width), 0) == 0
    drop = jnp.logical_and(packed_row, own_first)

    def pair(left, right):
        return (
            jnp.where(low, left, pltpu.roll(right, cols, 1)),
            jnp.where(low, pltpu.roll(left, cols, 1), right),
        )

    middle[...] = jnp.zeros_like(middle)
    tiles = sources // 2
    for tile in range(tiles // 2):
        lane = slice(tile * width, (tile + 1) * width)
        lanes = (lane, slice(half_len + tile * width, half_len + (tile + 1) * width))

        def piece(lo, tile=tile):
            hi = lo + width
            found = []
            for source in (2 * tile, 2 * tile + tiles):
                found.append(
                    pair(moved[source, :, lo:hi].astype(F32), moved[source + 1, :, lo:hi].astype(F32))
                )
            return [(found[0][at], found[1][at]) for at in range(2)]

        def put(seg, real, imag, lane=lane, lanes=lanes):
            turned_real, turned_imag = [], []
            for half in range(2):
                middle[seg : seg + 1, lanes[half]] = imag[half][0:1, :]
                kept = jnp.where(drop, 0.0, imag[half])
                cos, sin = near_c[:, lanes[half]], near_s[:, lanes[half]]
                turned_real.append(real[half] * cos + kept * sin)
                turned_imag.append(kept * cos - real[half] * sin)
            for at, (low_half, high_half) in ((seg * rows, turned_real), (all_rows + seg * rows, turned_imag)):
                stacked[0, at : at + rows, lane] = (low_half + high_half).astype(BF16)
                stacked[1, at : at + rows, lane] = (low_half - high_half).astype(BF16)

        for twin in range(segs // 2):
            real_one, real_two = piece(twin * width)
            imag_one, imag_two = piece(tail + twin * width)
            put(2 * twin, real_one, imag_one)
            put(2 * twin + 1, real_two, imag_two)
        real, imag = piece(2 * tail)
        put(segs, real, imag)
    for copy in copies:
        copy.wait()
    for part, turned in enumerate((middle[...] * mid_c[...], middle[...] * -mid_s[...])):
        at = slice(2 * all_rows + part * rows, 2 * all_rows + (part + 1) * rows)
        stacked[0, at, :] = (turned[:, :half_len] + turned[:, half_len:]).astype(BF16)
        stacked[1, at, :] = (turned[:, :half_len] - turned[:, half_len:]).astype(BF16)

    first_lane = lax.broadcasted_iota(jnp.int32, (rows, quarter), 1) == 0
    swap = jnp.logical_and(lax.broadcasted_iota(jnp.int32, (rows, quarter), 0) == 0, own_first)
    floor = 0.2 * (second_len * 2 * sources * rows)
    upper, lower = [], []
    for odd in range(2):
        cos_at = slice(odd * half_len, odd * half_len + quarter)
        sin_at = slice(odd * half_len + quarter, (odd + 1) * half_len)
        product[:, odd * half_len : (odd + 1) * half_len] = matmul(stacked[odd], forward[odd])

        def parts(at, lower_at, cos_at=cos_at, sin_at=sin_at):
            return (
                product[at : at + rows, cos_at],
                product[at : at + rows, sin_at],
                product[lower_at : lower_at + rows, cos_at],
                product[lower_at : lower_at + rows, sin_at],
            )

        def direct_of(rc, rs, ic, imag_s, odd=odd):
            if not odd:
                rs, imag_s = jnp.where(first_lane, 0.0, rs), jnp.where(first_lane, 0.0, imag_s)
            return rc + imag_s, ic - rs

        def mirror_of(rc, rs, ic, imag_s, odd=odd):
            real, imag = rc - imag_s, ic + rs
            if not odd:
                real, imag = jnp.where(first_lane, rs, real), jnp.where(first_lane, imag_s, imag)
            return real, imag

        level = jnp.zeros((rows, quarter), F32)
        mirror_level = level
        for seg in range(segs):
            four = parts(seg * rows, all_rows + seg * rows)
            real, imag = direct_of(*four)
            level = level + (real * real + imag * imag)
            real, imag = mirror_of(*four)
            mirror_level = mirror_level + (real * real + imag * imag)
        four = parts(segs * rows, all_rows + segs * rows)
        real, imag = direct_of(*four)
        mirror_real, mirror_imag = mirror_of(*four)
        mid_real, mid_imag = mirror_of(*parts(2 * all_rows, 2 * all_rows + rows))
        mid_level = jnp.sum((mid_real * mid_real + mid_imag * mid_imag)[:segs], 0, keepdims=True)
        mirror_level = jnp.where(swap, mid_level, mirror_level)
        mirror_real = jnp.where(swap, mid_real[segs : segs + 1], mirror_real)
        mirror_imag = jnp.where(swap, mid_imag[segs : segs + 1], mirror_imag)
        level = jnp.maximum(level * (1.0 / segs), floor)
        mirror_level = jnp.maximum(mirror_level * (1.0 / segs), floor)
        upper.append((real / level, imag / level, 1.0 / level))
        lower.append((mirror_real / mirror_level, -mirror_imag / mirror_level, 1.0 / mirror_level))
    eighth = rows // 2
    for part in range(3):
        mirrored = (lower[1][part], pltpu.roll(lower[0][part], quarter - 1, 1))
        for odd in range(2):
            lane = slice(part * half_len + odd * quarter, part * half_len + (odd + 1) * quarter)
            for parity in range(2):
                at = slice(parity * eighth, (parity + 1) * eighth)
                block = jnp.concatenate([upper[odd][part][at], mirrored[odd][at]], 0)
                out[parity * rows : (parity + 1) * rows, lane] = block.astype(BF16)


def sort_tables(rows, rows_out, bins_out):
    _, per, _ = rows_out.shape
    _, group = position()

    def one_hot(mask):
        return jnp.where(mask, 1.0, 0.0).astype(BF16)

    at = lax.broadcasted_iota(jnp.int32, (per, per), 0)
    lane = lax.broadcasted_iota(jnp.int32, (per, per), 1)
    for turned in range(2):
        row = packed_row_of(at, turned, 2 * per, rows)
        share = (row // rows) % 2
        source = row // (2 * rows) - turned * (per // (2 * rows))
        column = source * rows + row % rows + jnp.where(share == group, 0, per // 2)
        rows_out[turned] = one_hot(column == lane)
    wide = bins_out.shape[0]
    at = lax.broadcasted_iota(jnp.int32, (wide, wide), 0)
    lane = lax.broadcasted_iota(jnp.int32, (wide, wide), 1)
    bins_out[...] = one_hot(at == jnp.where(lane < wide // 2, 2 * lane, 2 * lane - wide + 1))


def packed_row_of(at, turned, first_len, rows):
    half = first_len // 4
    packed = at % half // (rows // 2) * rows + 2 * (at % (rows // 2)) + at // half
    if not turned:
        return packed
    return jnp.where(packed == 0, first_len // 2, first_len - packed)


def choose_kernel(order, cuts, own, other, by_rows, by_bins, out, held):
    place, _ = position()
    sources, rows, _ = own.shape
    per = sources * rows
    half_len = own.shape[2] // 2
    for source in range(sources):
        turned, at = source // (sources // 2), source % (sources // 2) * rows
        held[turned, at : at + rows, :] = own[source]
        held[turned, per // 2 + at : per // 2 + at + rows, :] = other[source]
    cut = cuts[order[place]]
    moved, room = [], []
    for turned in range(2):
        moved.append(matmul(by_rows[turned], held[turned]).reshape(per // (rows // 2), rows // 2, 2 * half_len))
        at = lax.broadcasted_iota(jnp.int32, (per, 128), 0)
        room.append((cut - packed_row_of(at, turned, 2 * per, rows)).reshape(per // (rows // 2), rows // 2, 128))
    picked = jnp.concatenate(moved, 1).reshape(2 * per, 2 * half_len).astype(BF16)
    room = jnp.concatenate(room, 1).reshape(2 * per, 128)
    wide = by_bins.shape[0]
    for part in range(2):
        for block in range(half_len // wide):
            lane = part * half_len + block * wide
            sorted_bins = matmul(picked[:, lane : lane + wide], by_bins[...])
            for odd in range(2):
                for at in range(0, wide // 2, 128):
                    first = block * (wide // 2) + at
                    bins = 2 * (first + lax.broadcasted_iota(jnp.int32, (1, 128), 1)) + odd
                    from_lane = odd * (wide // 2) + at
                    kept = jnp.where(
                        2 * per * bins < room, sorted_bins[:, from_lane : from_lane + 128], 0.0
                    )
                    to = part * half_len + odd * (half_len // 2) + first
                    out[:, to : to + 128] = kept.astype(BF16)


def filter_blocks(offsets, blocks, chosen, tables, norm, filtered, lifted):
    place, _ = position()
    even_table, odd_table, lift_c, lift_s = tables
    half_len = even_table.shape[0]
    quarter = half_len // 2
    first_len = chosen.shape[0]
    per = first_len // 2
    rows = blocks[0].shape[0] // 2
    groups = []
    for block, offset in zip(blocks, offsets):
        device = jnp.bitwise_xor(place, offset)
        for parity in range(2):
            row = slice(parity * rows, (parity + 1) * rows)
            at = aligned(parity * per + device * rows, rows)
            white_real = block[row, :half_len].astype(F32)
            white_imag = block[row, half_len : 2 * half_len].astype(F32)
            weight = block[row, 2 * half_len :].astype(F32)
            real = chosen[at, :half_len].astype(F32)
            imag = chosen[at, half_len:].astype(F32)
            norm = norm + (real * real + imag * imag) * weight
            filt_real = (white_real * real + white_imag * imag).astype(BF16)
            filt_imag = (white_imag * real - white_real * imag).astype(BF16)
            to = slice(len(groups) * rows, (len(groups) + 1) * rows)
            filtered[to, 0:quarter] = filt_real[:, :quarter]
            filtered[to, quarter:half_len] = filt_imag[:, :quarter]
            filtered[to, half_len : half_len + quarter] = filt_real[:, quarter:]
            filtered[to, half_len + quarter :] = filt_imag[:, quarter:]
            groups.append((to, at, parity * first_len + device * rows))
    for lane in range(0, half_len, PIECE):
        both = slice(2 * lane, 2 * (lane + PIECE))
        even = matmul(filtered[:, :half_len], even_table[:, both])
        odd = matmul(filtered[:, half_len:], odd_table[:, both])
        for upper in range(2):
            lanes = slice(upper * half_len + lane, upper * half_len + lane + PIECE)
            total = even - odd if upper else even + odd
            for row, at, target in groups:
                real, imag = total[row, :PIECE], total[row, PIECE:]
                cos, sin = lift_c[at, lanes], lift_s[at, lanes]
                lifted[aligned(target, rows), lanes] = (real * cos - imag * sin).astype(BF16)
                lifted[aligned(target + per, rows), lanes] = (real * sin + imag * cos).astype(BF16)
    return norm


def early_kernel(near, theirs, chosen, *refs):
    tables, (lifted, norm, filtered) = refs[:4], refs[4:]
    blocks = [*[near.at[at] for at in range(4)], *[theirs.at[at] for at in range(4)]]
    zero = jnp.zeros(norm.shape, F32)
    norm[...] = filter_blocks(EARLY, blocks, chosen, tables, zero, filtered, lifted)


def middle_kernel(both, far, theirs, early, early_norm, chosen, *refs):
    tables, (lifted, norm, filtered) = refs[:4], refs[4:]
    blocks = [both.at[0], both.at[1], far, *[theirs.at[at] for at in range(3)]]
    norm[...] = filter_blocks(MIDDLE, blocks, chosen, tables, early_norm[...], filtered, lifted)


def late_kernel(last, theirs, early, early_norm, chosen, *refs):
    tables, (cols_table, out, lifted, filtered, result, sems) = refs[:4], refs[4:]
    norm = filter_blocks(LATE, [last, theirs], chosen, tables, early_norm[...], filtered, lifted)
    scale = lax.rsqrt(jnp.sum(norm, keepdims=True))
    first_len = chosen.shape[0]
    per = first_len // 2
    wide = 256
    lanes = [slice(lane, lane + wide) for lane in range(0, lifted.shape[1], wide)]

    def products(at):
        return (
            matmul(cols_table[:, :first_len], lifted[:first_len, at]),
            matmul(cols_table[:, first_len:], lifted[first_len:, at]),
        )

    copies = []
    following = products(lanes[0])
    for block, at in enumerate(lanes):
        even, odd = following
        if block + 1 < len(lanes):
            following = products(lanes[block + 1])
        for upper in range(2):
            total = even - odd if upper else even + odd
            power = total[:per] * total[:per] + total[per:] * total[per:]
            size = power * lax.rsqrt(jnp.maximum(power, 1e-37))
            result[upper * per : (upper + 1) * per, at] = (size * scale).astype(BF16)
        copies.append(pltpu.make_async_copy(result.at[:, at], out.at[0, :, at], sems.at[block]))
        copies[-1].start()
    for copy in copies:
        copy.wait()


def swap_with(array, flip):
    pairs = [(at, at ^ flip) for at in range(lax.axis_size("tmpl"))]
    return lax.ppermute(array, "tmpl", pairs)


def tiled_local(strain, analysis, bank, cutoff, order):
    dev_count = lax.axis_size("tmpl")
    segs, first_len, cols = strain.shape
    second_len = cols * dev_count
    length = first_len * second_len
    half_len = second_len // 2
    rows = first_len // dev_count // 2
    templates = order.shape[0]
    lanes = 2 * (segs + 1) * cols

    first, second, half = np.arange(first_len), np.arange(second_len), np.arange(half_len)
    devices, step = np.arange(dev_count), np.arange(STEP)
    near = halves(rows)
    packed = (devices[:, None] * rows + near[None, :]).reshape(dev_count, 2, rows // 2)
    waves = []
    for odd in range(2):
        cos, sin = turns(packed[:, odd].reshape(-1, 1) * first[None, : first_len // 2], first_len)
        if not odd:
            sin[0] = 2 * (first[: first_len // 2] % 2) - 1.0
        waves.append(np.concatenate([cos, -sin]))
    win = np.stack(turns(np.arange(8)[:, None] + second_len * first[None, :], length))
    spin = np.stack(turns(cols * devices, length), 1)[:, :, None] * np.ones((1, 1, first_len), np.float32)
    turns_of_eight = [tuple(float(at) for at in turns(8 * block, length)) for block in range(cols // 8)]

    sent = pl.pallas_call(
        functools.partial(stage_one_kernel, turns_of_eight),
        in_specs=[outside()] * 7,
        out_specs=whole(),
        scratch_shapes=[
            pltpu.SMEM((templates,), jnp.int32),
            vmem((segs, cols, first_len), F32),
            vmem((cols, first_len), F32),
            vmem((2, first_len), F32),
            vmem((2, 8, first_len), F32),
            vmem((2, dev_count * rows, first_len // 2)),
            vmem((2, (segs + 1) * cols, first_len // 2)),
            pltpu.SemaphoreType.DMA((segs + 5,)),
            pltpu.SemaphoreType.DMA,
        ],
        out_shape=pltpu.VMEM((dev_count * rows, lanes + 2 * half_len), BF16),
        compiler_params=params(16),
        name="stage_one",
    )(
        *in_hbm(
            order, jnp.swapaxes(strain, 1, 2), jnp.swapaxes(analysis, 0, 1), spin, win,
            np.stack(waves).astype(BF16), bank,
        ),
    )
    moved = lax.all_to_all(
        sent.reshape(dev_count, rows, lanes + 2 * half_len), "tmpl", split_axis=0, concat_axis=0, tiled=True
    )
    own = moved[:, :, lanes:]
    other = lax.ppermute(own, "grp", [(0, 1), (1, 0)])

    split = halves(half_len)
    low = 2 * np.arange(rows // 2)
    lift_rows = [np.concatenate([low + odd, first_len - low - odd]) for odd in range(2)]
    lift_init = [turns(at[:, None] * second[None, :], length) for at in lift_rows]
    cols_parts = []
    for odd in range(2):
        straight = devices[:, None] * rows + low[None, :] + odd
        turned = np.where(straight == 0, first_len // 2, first_len - straight)
        cols_parts.append(np.concatenate([straight, turned], 1).reshape(-1))
    cols_rows = np.concatenate(cols_parts)
    mid_rows = lift_rows[0].copy()
    mid_rows[rows // 2] = first_len // 2
    step_sign = np.where(np.arange(rows) < rows // 2, rows, -rows)
    fore = [
        *turns(step[:, None] * split[None, :], second_len),
        *turns(STEP * split[None, :], second_len),
        *turns(near[:, None] * second[None, :], length),
        *turns(rows * devices[:, None, None] * second[None, None, :], length),
    ]
    forward, near_c, near_s = pl.pallas_call(
        forward_kernel,
        out_shape=[
            pltpu.VMEM((2, half_len, half_len), BF16),
            *[pltpu.VMEM((rows, second_len), F32)] * 2,
        ],
        in_specs=[whole()] * len(fore),
        out_specs=[whole()] * 3,
        compiler_params=params(16),
        cost_estimate=pl.CostEstimate(flops=10**7, bytes_accessed=2 * 10**7, transcendentals=0),
        name="forward_tables",
    )(*in_hbm(*fore))
    back = [
        *turns(2 * step[:, None] * half[None, :], second_len),
        *turns((2 * step[:, None] + 1) * half[None, :], second_len),
        *turns(2 * STEP * half[None, :], second_len),
        np.stack([lift_init[0][0], lift_init[1][0]]),
        np.stack([lift_init[0][1], lift_init[1][1]]),
        *turns(step_sign[:, None] * second[None, :], length),
        *turns(mid_rows[:, None] * second[None, :], length),
    ]
    columns = [
        *turns(step[:, None] * cols_rows[None, :], first_len),
        *turns(STEP * cols_rows[None, :], first_len),
    ]
    shapes = [
        ((half_len, second_len), BF16),
        ((half_len, second_len), BF16),
        ((first_len, second_len), F32),
        ((first_len, second_len), F32),
    ]
    column_shapes = [
        ((first_len, 2 * first_len), BF16),
        ((2, first_len // 2, first_len // 2), BF16),
        ((256, 256), BF16),
    ]
    inverse_tables = pl.pallas_call(
        inverse_tables_kernel,
        out_shape=[pltpu.VMEM(*shape) for shape in shapes],
        in_specs=[whole()] * len(back),
        out_specs=[whole()] * len(shapes),
        compiler_params=params(8),
        cost_estimate=pl.CostEstimate(flops=10**7, bytes_accessed=2 * 10**7, transcendentals=0),
        name="inverse_tables",
    )
    even_table, odd_table, lift_c, lift_s = inverse_tables(*in_hbm(*back))
    column_tables = pl.pallas_call(
        functools.partial(column_tables_kernel, rows),
        out_shape=[pltpu.VMEM(*shape) for shape in column_shapes],
        in_specs=[whole()] * len(columns),
        out_specs=[whole()] * len(column_shapes),
        compiler_params=params(8),
        cost_estimate=pl.CostEstimate(flops=10**7, bytes_accessed=10**7, transcendentals=0),
        name="column_tables",
    )
    cols_table, by_rows, by_bins = column_tables(*in_hbm(*columns))

    mid_c, mid_s = turns(first_len // 2 * second[None, :], length)
    all_rows = 2 * (segs + 2) * rows
    stage_two = pl.pallas_call(
        functools.partial(stage_two_kernel, segs, cols),
        out_shape=jax.ShapeDtypeStruct((2 * rows, 3 * half_len), BF16),
        in_specs=[whole()] * 3 + [outside()] * 2 + [whole()],
        out_specs=whole(),
        scratch_shapes=[
            *[vmem((1, second_len), F32)] * 2,
            vmem((2, all_rows, half_len)),
            vmem((rows, second_len), F32),
            vmem((all_rows, second_len), F32),
            pltpu.SemaphoreType.DMA((2,)),
        ],
        compiler_params=params(24),
        cost_estimate=pl.CostEstimate(flops=10**9, bytes_accessed=4 * 10**6, transcendentals=0),
        name="stage_two",
    )
    block = stage_two(moved, *in_vmem(near_c, near_s), *in_hbm(mid_c, mid_s), *in_vmem(forward))

    two = swap_with(block, 8)
    one = swap_with(block, 4)
    beside = swap_with(block, 2)
    both = swap_with(jnp.stack([one, two]), 2)
    far = swap_with(two, 4)
    near = jnp.stack([block, beside, one, two])
    theirs = swap_with(near, 1)
    last = swap_with(far, 2)
    more = swap_with(jnp.stack([both[0], both[1], far]), 1)
    late = swap_with(last, 1)

    choose = pl.pallas_call(
        choose_kernel,
        grid_spec=pltpu.PrefetchScalarGridSpec(
            num_scalar_prefetch=2,
            grid=(),
            in_specs=[whole()] * 4,
            out_specs=whole(),
            scratch_shapes=[vmem((2, first_len // 2, 2 * half_len))],
        ),
        out_shape=jax.ShapeDtypeStruct((first_len, 2 * half_len), BF16),
        compiler_params=params(16),
        cost_estimate=pl.CostEstimate(flops=10**9, bytes_accessed=4 * 10**6, transcendentals=0),
        name="choose",
    )
    chosen = choose(order, cutoff, own, other, *in_vmem(by_rows, by_bins))

    spread = [(2 * first_len, second_len), BF16]
    tables = in_vmem(even_table, odd_table, lift_c, lift_s)
    early = pl.pallas_call(
        early_kernel,
        out_shape=[pltpu.VMEM(*spread), pltpu.VMEM((rows, half_len), F32)],
        in_specs=[whole()] * 7,
        out_specs=[whole()] * 2,
        scratch_shapes=[vmem((len(EARLY) * 2 * rows, 2 * half_len))],
        compiler_params=params(16),
        cost_estimate=pl.CostEstimate(flops=10**9, bytes_accessed=4 * 10**6, transcendentals=0),
        name="early",
    )
    lifted, norm = early(near, theirs, chosen, *tables)
    middle = pl.pallas_call(
        middle_kernel,
        out_shape=[pltpu.VMEM(*spread), pltpu.VMEM((rows, half_len), F32)],
        in_specs=[whole()] * 10,
        out_specs=[whole()] * 2,
        scratch_shapes=[vmem((len(MIDDLE) * 2 * rows, 2 * half_len))],
        input_output_aliases={3: 0},
        compiler_params=params(16),
        cost_estimate=pl.CostEstimate(flops=10**9, bytes_accessed=4 * 10**6, transcendentals=0),
        name="middle",
    )
    lifted, norm = middle(both, far, more, *in_vmem(lifted, norm), chosen, *tables)
    result, _ = pl.pallas_call(
        late_kernel,
        out_shape=[pltpu.HBM((1, first_len, second_len), BF16), pltpu.VMEM(*spread)],
        in_specs=[whole()] * 10,
        out_specs=[outside(), whole()],
        scratch_shapes=[
            vmem((len(LATE) * 2 * rows, 2 * half_len)),
            vmem((first_len, second_len)),
            pltpu.SemaphoreType.DMA((second_len // 256,)),
        ],
        input_output_aliases={2: 1},
        compiler_params=params(16),
        name="late",
    )(last, late, *in_vmem(lifted, norm), chosen, *tables, *in_vmem(cols_table))
    return result


def angles(left_idx, right_idx, period):
    product = left_idx[:, None] * right_idx[None, :] % period
    phase_angle = product.astype(jnp.float32) * (2.0 * math.pi / period)
    return (jnp.cos(phase_angle), jnp.sin(phase_angle))


def filtered(white_pair, tmpl_pair, cut_bins, freq_bin):
    white_real = white_pair[0].astype(jnp.float32)
    white_imag = white_pair[1].astype(jnp.float32)
    tmpl_real = tmpl_pair[0].astype(jnp.float32)
    tmpl_imag = tmpl_pair[1].astype(jnp.float32)
    in_band = freq_bin[None] < cut_bins[:, None, None]
    filt_real = jnp.where(in_band, white_real * tmpl_real + white_imag * tmpl_imag, 0.0)
    filt_imag = jnp.where(in_band, white_imag * tmpl_real - white_real * tmpl_imag, 0.0)
    return jnp.concatenate([filt_real, filt_imag], -1).astype(jnp.bfloat16)


def inverse_rows(stacked, row_bins, second_len, length):
    half_len = second_len // 2
    cosine, sine = angles(
        jnp.arange(half_len, dtype=jnp.int32), jnp.arange(second_len, dtype=jnp.int32), second_len
    )
    dft_table = jnp.concatenate(
        [jnp.concatenate([cosine, sine], 1), jnp.concatenate([-sine, cosine], 1)], 0
    ).astype(jnp.bfloat16)
    spread = jnp.einsum("tkf,fg->tkg", stacked, dft_table, preferred_element_type=jnp.float32)
    spread_real = spread[..., :second_len]
    spread_imag = spread[..., second_len:]
    cos_twist, sin_twist = angles(row_bins, jnp.arange(second_len, dtype=jnp.int32), length)
    lift_real = spread_real * cos_twist - spread_imag * sin_twist
    lift_imag = spread_real * sin_twist + spread_imag * cos_twist
    return jnp.concatenate([lift_real, lift_imag], -1).astype(jnp.bfloat16)


def inverse_cols(lifted, first_len, second_len):
    row_idx = jnp.arange(first_len, dtype=jnp.int32)
    cosine, sine = angles(row_idx, row_idx, first_len)
    cosine = cosine.astype(jnp.bfloat16)
    sine = sine.astype(jnp.bfloat16)
    lift_real = lifted[..., :second_len]
    lift_imag = lifted[..., second_len:]
    field_real = jnp.einsum(
        "ak,tkb->tab", cosine, lift_real, preferred_element_type=jnp.float32
    ) - jnp.einsum("ak,tkb->tab", sine, lift_imag, preferred_element_type=jnp.float32)
    field_imag = jnp.einsum(
        "ak,tkb->tab", sine, lift_real, preferred_element_type=jnp.float32
    ) + jnp.einsum("ak,tkb->tab", cosine, lift_imag, preferred_element_type=jnp.float32)
    return (field_real, field_imag)


def plain_local(strain, analysis, bank, cutoff, order):
    highest = lax.Precision.HIGHEST
    dev_count = lax.axis_size("tmpl")
    my_index = lax.axis_index("tmpl")
    seg_count = strain.shape[0]
    first_len = strain.shape[1]
    col_count = strain.shape[2]
    second_len = col_count * dev_count
    length = first_len * second_len
    half_len = second_len // 2
    row_count = first_len // dev_count
    row_idx = jnp.arange(first_len, dtype=jnp.int32)
    col_index = my_index * col_count + jnp.arange(col_count, dtype=jnp.int32)
    sample_idx = row_idx[:, None] * second_len + col_index[None, :]
    window = (
        math.sqrt(8.0 / 3.0) * jnp.sin(sample_idx.astype(jnp.float32) * (math.pi / length)) ** 2
    )
    series = jnp.concatenate([strain * window, analysis[None]], 0)
    cos_one, sin_one = angles(row_idx, row_idx, first_len)
    part_real = jnp.einsum("ka,sab->skb", cos_one, series, precision=highest)
    part_imag = -jnp.einsum("ka,sab->skb", sin_one, series, precision=highest)
    cos_twist, sin_twist = angles(row_idx, col_index, length)
    twist_real = part_real * cos_twist + part_imag * sin_twist
    twist_imag = part_imag * cos_twist - part_real * sin_twist
    moved = lax.all_to_all(
        jnp.stack([twist_real, twist_imag]).astype(jnp.bfloat16),
        "tmpl",
        split_axis=2,
        concat_axis=3,
        tiled=True,
    ).astype(jnp.float32)
    cos_two, sin_two = angles(
        jnp.arange(second_len, dtype=jnp.int32), jnp.arange(half_len, dtype=jnp.int32), second_len
    )
    spec_real = jnp.einsum("skb,bf->skf", moved[0], cos_two, precision=highest) + jnp.einsum(
        "skb,bf->skf", moved[1], sin_two, precision=highest
    )
    spec_imag = jnp.einsum("skb,bf->skf", moved[1], cos_two, precision=highest) - jnp.einsum(
        "skb,bf->skf", moved[0], sin_two, precision=highest
    )
    power_spec = jnp.maximum(
        jnp.mean(spec_real[:seg_count] ** 2 + spec_imag[:seg_count] ** 2, axis=0), 0.2 * length
    )
    whitened = jnp.stack(
        [spec_real[seg_count] / power_spec, spec_imag[seg_count] / power_spec]
    ).astype(jnp.bfloat16)
    own_rows = my_index * row_count + jnp.arange(row_count, dtype=jnp.int32)
    half_idx = jnp.arange(half_len, dtype=jnp.int32)
    freq_local = own_rows[:, None] + first_len * half_idx[None, :]
    chosen = jnp.take(bank, order, axis=1)
    cuts = jnp.take(cutoff, order)
    bank_real = chosen[0].astype(jnp.float32)
    bank_imag = chosen[1].astype(jnp.float32)
    in_band = freq_local[None] < cuts[:, None, None]
    local_norm = jnp.sum(
        jnp.where(in_band, (bank_real**2 + bank_imag**2) / power_spec, 0.0), axis=(1, 2)
    )
    norm_sq = lax.psum(local_norm, "tmpl")
    per_device = cuts.shape[0] // dev_count
    own_norm = lax.dynamic_slice_in_dim(norm_sq, my_index * per_device, per_device)
    stacked = filtered(whitened, chosen, cuts, freq_local)
    lifted = lax.all_to_all(
        inverse_rows(stacked, own_rows, second_len, length),
        "tmpl",
        split_axis=0,
        concat_axis=1,
        tiled=True,
    )
    field_real, field_imag = inverse_cols(lifted, first_len, second_len)
    magnitude = jnp.sqrt(field_real**2 + field_imag**2)
    return (magnitude / jnp.sqrt(own_norm)[:, None, None]).astype(jnp.bfloat16)


def local(strain, analysis, bank, cutoff, order):
    dev_count, segs, cols = lax.axis_size("tmpl"), strain.shape[0], strain.shape[2]
    rows = strain.shape[1] // dev_count // 2
    fits = rows == STEP and cols == 64 and segs % 2 == 0 and dev_count == len(EARLY + MIDDLE + LATE)
    if fits and order.shape[0] == dev_count and lax.axis_size("grp") == 2:
        return tiled_local(strain, analysis, bank, cutoff, order)
    return plain_local(strain, analysis, bank, cutoff, order)


def solution(mesh):
    return jax.shard_map(
        local,
        mesh=mesh,
        in_specs=(P("grp", None, "tmpl"), P("grp", "tmpl"), P(None, None, "tmpl", None), P(), P()),
        out_specs=P(("grp", "tmpl"), None, None),
        check_vma=False,
    )
```

```python
import functools
import math

import jax
import jax.numpy as jnp
import numpy as np
from jax import lax
from jax.experimental import pallas as pl
from jax.experimental.pallas import tpu as pltpu
from jax.sharding import PartitionSpec as P

BF16 = jnp.bfloat16
F32 = jnp.float32
STEP = 16
PIECE = 128
EARLY = (0, 2, 4, 8, 1, 3, 5, 9)
MIDDLE = (6, 10, 12, 7, 11, 13)
LATE = (14, 15)


def turns(product, period):
    angle = (product % period) * (2.0 * math.pi / period)
    return np.cos(angle).astype(np.float32), np.sin(angle).astype(np.float32)


def matmul(left, right):
    return jnp.dot(left, right, preferred_element_type=F32)


def matmul_nt(left, right):
    return lax.dot_general(left, right, (((1,), (1,)), ((), ())), preferred_element_type=F32)


def vmem(shape, dtype=BF16):
    return pltpu.VMEM(shape, dtype)


def whole():
    return pl.BlockSpec(memory_space=pltpu.VMEM)


def outside():
    return pl.BlockSpec(memory_space=pltpu.HBM)


def in_hbm(*arrays):
    return [pltpu.with_memory_space_constraint(jnp.asarray(array), pltpu.HBM) for array in arrays]


def in_vmem(*arrays):
    return [pltpu.with_memory_space_constraint(array, pltpu.VMEM) for array in arrays]


def position():
    return lax.axis_index("tmpl"), lax.axis_index("grp")


def start_copies(pairs, sems):
    copies = [
        pltpu.make_async_copy(source, target, sems.at[at]) for at, (source, target) in enumerate(pairs)
    ]
    for copy in copies:
        copy.start()
    return copies


def params(mib):
    return pltpu.CompilerParams(vmem_limit_bytes=mib << 20)


def turn(cos, sin, by_cos, by_sin):
    return cos * by_cos - sin * by_sin, sin * by_cos + cos * by_sin


def halves(count):
    return np.concatenate([np.arange(0, count, 2), np.arange(1, count, 2)])


def aligned(start, size):
    return pl.ds(pl.multiple_of(start, size), size)


def stage_one_kernel(
    turns_of_eight, order_hbm, strain_hbm, analysis_hbm, spin_hbm, win_hbm, wave_hbm, bank, out,
    order, strain, analysis, spin, win, wave, packed, sems, bank_sem,
):
    segs, cols, first_len = strain.shape
    tail = segs * cols
    templates, half_len = bank.shape[1], bank.shape[3]
    rows = out.shape[0] // templates
    half = first_len // 2
    place, group = position()
    sources = [
        (order_hbm, order),
        (spin_hbm.at[place], spin),
        (win_hbm, win),
        *[(strain_hbm.at[seg], strain.at[seg]) for seg in range(segs)],
        (analysis_hbm, analysis),
        (wave_hbm, wave),
    ]
    copies = start_copies(sources, sems)
    lane = 2 * (tail + cols)
    for copy in copies[:3]:
        copy.wait()
    bank_pairs = []
    for row in range(templates):
        for part in range(2):
            bank_pairs.append(
                (
                    bank.at[part, order[row], aligned(group * rows, rows), :],
                    out.at[
                        row * rows : (row + 1) * rows,
                        lane + part * half_len : lane + (part + 1) * half_len,
                    ],
                )
            )
    for source, target in bank_pairs:
        pltpu.make_async_copy(source, target, bank_sem).start()
    scale = 0.5 * math.sqrt(8.0 / 3.0)
    win_c, win_s = turn(win[0], win[1], spin[0:1, :], spin[1:2, :])
    window = jnp.concatenate(
        [scale - (win_c * (scale * by_cos) - win_s * (scale * by_sin)) for by_cos, by_sin in turns_of_eight], 0
    )

    def pack(at, values):
        packed[0, at : at + cols, :] = (values[:, :half] + values[:, half:]).astype(BF16)
        packed[1, at : at + cols, :] = (values[:, :half] - values[:, half:]).astype(BF16)

    for seg in range(segs):
        copies[3 + seg].wait()
        pack(seg * cols, strain[seg] * window)
    copies[3 + segs].wait()
    pack(tail, analysis[...])
    copies[4 + segs].wait()
    both = [matmul_nt(wave[odd], packed[odd]) for odd in range(2)]
    count = out.shape[0] // 2

    def woven(part):
        halves_of = [
            table[part * count : (part + 1) * count].reshape(templates, rows // 2, tail + cols) for table in both
        ]
        return jnp.concatenate(halves_of, 1).reshape(2 * count, tail + cols)

    real, imag = woven(0), woven(1)
    out[:, 0:tail] = real[:, :tail].astype(BF16)
    out[:, tail : 2 * tail] = imag[:, :tail].astype(BF16)
    joined = jnp.concatenate([real[:, tail:], imag[:, tail:]], 1)
    out[:, 2 * tail : lane] = joined.astype(BF16)
    whole_bank = out.at[:, lane:]
    pltpu.make_async_copy(whole_bank, whole_bank, bank_sem).wait()


def forward_kernel(
    fore_c, fore_s, fore_rc, fore_rs, near_c, near_s, base_c, base_s,
    forward, near_out_c, near_out_s,
):
    half_len = fore_c.shape[1]
    quarter = half_len // 2
    place, _ = position()
    first_lane = lax.broadcasted_iota(jnp.int32, fore_c.shape, 1) == 0
    sign = 1.0 - 2.0 * (lax.broadcasted_iota(jnp.int32, fore_c.shape, 0) % 2).astype(F32)

    def fore(step, carry):
        cos, sin = carry
        for part, table in enumerate((cos, jnp.where(first_lane, sign, sin))):
            for odd in range(2):
                lane = slice(odd * quarter, (odd + 1) * quarter)
                to = slice(part * quarter, (part + 1) * quarter)
                forward[odd, aligned(step * STEP, STEP), to] = table[:, lane].astype(BF16)
        return turn(cos, sin, fore_rc[...], fore_rs[...])

    lax.fori_loop(0, forward.shape[1] // STEP, fore, (fore_c[...], fore_s[...]))
    near_out_c[...], near_out_s[...] = turn(near_c[...], near_s[...], base_c[place], base_s[place])


def inverse_tables_kernel(
    even_c, even_s, odd_c, odd_s, rows_rc, rows_rs, lift_c, lift_s, lift_rc, lift_rs, mid_c, mid_s,
    even_out, odd_out, lift_out_c, lift_out_s,
):
    half_len = even_c.shape[1]
    quarter = half_len // 2
    per = lift_out_c.shape[0] // 2

    def spread(out, cos, sin):
        def body(step, carry):
            cos, sin = carry
            upper = aligned(step * STEP, STEP)
            lower = aligned(quarter + step * STEP, STEP)
            for lane in range(0, half_len, PIECE):
                real, imag = slice(2 * lane, 2 * lane + PIECE), slice(2 * lane + PIECE, 2 * (lane + PIECE))
                cos_at, sin_at = cos[:, lane : lane + PIECE], sin[:, lane : lane + PIECE]
                out[upper, real] = cos_at.astype(BF16)
                out[upper, imag] = sin_at.astype(BF16)
                out[lower, real] = (-sin_at).astype(BF16)
                out[lower, imag] = cos_at.astype(BF16)
            return turn(cos, sin, rows_rc[...], rows_rs[...])

        lax.fori_loop(0, quarter // STEP, body, (cos, sin))

    spread(even_out, even_c[...], even_s[...])
    spread(odd_out, odd_c[...], odd_s[...])

    for parity in range(2):

        def lifts(step, carry, parity=parity):
            cos, sin = carry
            at = aligned(parity * per + step * STEP, STEP)
            lift_out_c[at, :] = cos
            lift_out_s[at, :] = sin
            return turn(cos, sin, lift_rc[...], lift_rs[...])

        lax.fori_loop(0, per // STEP, lifts, (lift_c[parity], lift_s[parity]))
    lift_out_c[0:STEP, :] = mid_c[...]
    lift_out_s[0:STEP, :] = mid_s[...]


def column_tables_kernel(rows, cols_c, cols_s, cols_rc, cols_rs, cols_out, rows_out, bins_out):
    first_len = cols_c.shape[1]
    per = first_len // 2

    def columns(step, carry):
        cos, sin = carry
        upper = aligned(step * STEP, STEP)
        lower = aligned(per + step * STEP, STEP)
        for parity in range(2):
            at = slice(parity * per, (parity + 1) * per)
            left = slice(parity * first_len, parity * first_len + per)
            right = slice(parity * first_len + per, (parity + 1) * first_len)
            cols_out[upper, left] = cos[:, at].astype(BF16)
            cols_out[upper, right] = (-sin[:, at]).astype(BF16)
            cols_out[lower, left] = sin[:, at].astype(BF16)
            cols_out[lower, right] = cos[:, at].astype(BF16)
        return turn(cos, sin, cols_rc[...], cols_rs[...])

    lax.fori_loop(0, per // STEP, columns, (cols_c[...], cols_s[...]))
    sort_tables(rows, rows_out, bins_out)


def stage_two_kernel(
    segs, cols, moved, near_c, near_s, mid_c_hbm, mid_s_hbm, forward, out,
    mid_c, mid_s, stacked, middle, product, sems,
):
    place, _ = position()
    _, half_len, _ = forward.shape
    second_len = 2 * half_len
    quarter = half_len // 2
    copies = start_copies([(mid_c_hbm, mid_c), (mid_s_hbm, mid_s)], sems)
    sources, rows, _ = moved.shape
    tail = segs * cols
    all_rows = (segs + 1) * rows
    width = 2 * cols
    low = lax.broadcasted_iota(jnp.int32, (rows, width), 1) < cols
    own_first = place == 0
    packed_row = lax.broadcasted_iota(jnp.int32, (rows, width), 0) == 0
    drop = jnp.logical_and(packed_row, own_first)

    def pair(left, right):
        return (
            jnp.where(low, left, pltpu.roll(right, cols, 1)),
            jnp.where(low, pltpu.roll(left, cols, 1), right),
        )

    middle[...] = jnp.zeros_like(middle)
    tiles = sources // 2
    for tile in range(tiles // 2):
        lane = slice(tile * width, (tile + 1) * width)
        lanes = (lane, slice(half_len + tile * width, half_len + (tile + 1) * width))

        def piece(lo, tile=tile):
            hi = lo + width
            found = []
            for source in (2 * tile, 2 * tile + tiles):
                found.append(
                    pair(moved[source, :, lo:hi].astype(F32), moved[source + 1, :, lo:hi].astype(F32))
                )
            return [(found[0][at], found[1][at]) for at in range(2)]

        def put(seg, real, imag, lane=lane, lanes=lanes):
            turned_real, turned_imag = [], []
            for half in range(2):
                middle[seg : seg + 1, lanes[half]] = imag[half][0:1, :]
                kept = jnp.where(drop, 0.0, imag[half])
                cos, sin = near_c[:, lanes[half]], near_s[:, lanes[half]]
                turned_real.append(real[half] * cos + kept * sin)
                turned_imag.append(kept * cos - real[half] * sin)
            for at, (low_half, high_half) in ((seg * rows, turned_real), (all_rows + seg * rows, turned_imag)):
                stacked[0, at : at + rows, lane] = (low_half + high_half).astype(BF16)
                stacked[1, at : at + rows, lane] = (low_half - high_half).astype(BF16)

        for twin in range(segs // 2):
            real_one, real_two = piece(twin * width)
            imag_one, imag_two = piece(tail + twin * width)
            put(2 * twin, real_one, imag_one)
            put(2 * twin + 1, real_two, imag_two)
        real, imag = piece(2 * tail)
        put(segs, real, imag)
    for copy in copies:
        copy.wait()
    for part, turned in enumerate((middle[...] * mid_c[...], middle[...] * -mid_s[...])):
        at = slice(2 * all_rows + part * rows, 2 * all_rows + (part + 1) * rows)
        stacked[0, at, :] = (turned[:, :half_len] + turned[:, half_len:]).astype(BF16)
        stacked[1, at, :] = (turned[:, :half_len] - turned[:, half_len:]).astype(BF16)

    first_lane = lax.broadcasted_iota(jnp.int32, (rows, quarter), 1) == 0
    swap = jnp.logical_and(lax.broadcasted_iota(jnp.int32, (rows, quarter), 0) == 0, own_first)
    floor = 0.2 * (second_len * 2 * sources * rows)
    upper, lower = [], []
    for odd in range(2):
        cos_at = slice(odd * half_len, odd * half_len + quarter)
        sin_at = slice(odd * half_len + quarter, (odd + 1) * half_len)
        product[:, odd * half_len : (odd + 1) * half_len] = matmul(stacked[odd], forward[odd])

        def parts(at, lower_at, cos_at=cos_at, sin_at=sin_at):
            return (
                product[at : at + rows, cos_at],
                product[at : at + rows, sin_at],
                product[lower_at : lower_at + rows, cos_at],
                product[lower_at : lower_at + rows, sin_at],
            )

        def direct_of(rc, rs, ic, imag_s, odd=odd):
            if not odd:
                rs, imag_s = jnp.where(first_lane, 0.0, rs), jnp.where(first_lane, 0.0, imag_s)
            return rc + imag_s, ic - rs

        def mirror_of(rc, rs, ic, imag_s, odd=odd):
            real, imag = rc - imag_s, ic + rs
            if not odd:
                real, imag = jnp.where(first_lane, rs, real), jnp.where(first_lane, imag_s, imag)
            return real, imag

        level = jnp.zeros((rows, quarter), F32)
        mirror_level = level
        for seg in range(segs):
            four = parts(seg * rows, all_rows + seg * rows)
            real, imag = direct_of(*four)
            level = level + (real * real + imag * imag)
            real, imag = mirror_of(*four)
            mirror_level = mirror_level + (real * real + imag * imag)
        four = parts(segs * rows, all_rows + segs * rows)
        real, imag = direct_of(*four)
        mirror_real, mirror_imag = mirror_of(*four)
        mid_real, mid_imag = mirror_of(*parts(2 * all_rows, 2 * all_rows + rows))
        mid_level = jnp.sum((mid_real * mid_real + mid_imag * mid_imag)[:segs], 0, keepdims=True)
        mirror_level = jnp.where(swap, mid_level, mirror_level)
        mirror_real = jnp.where(swap, mid_real[segs : segs + 1], mirror_real)
        mirror_imag = jnp.where(swap, mid_imag[segs : segs + 1], mirror_imag)
        level = jnp.maximum(level * (1.0 / segs), floor)
        mirror_level = jnp.maximum(mirror_level * (1.0 / segs), floor)
        upper.append((real / level, imag / level, 1.0 / level))
        lower.append((mirror_real / mirror_level, -mirror_imag / mirror_level, 1.0 / mirror_level))
    eighth = rows // 2
    for part in range(3):
        mirrored = (lower[1][part], pltpu.roll(lower[0][part], quarter - 1, 1))
        for odd in range(2):
            lane = slice(part * half_len + odd * quarter, part * half_len + (odd + 1) * quarter)
            for parity in range(2):
                at = slice(parity * eighth, (parity + 1) * eighth)
                block = jnp.concatenate([upper[odd][part][at], mirrored[odd][at]], 0)
                out[parity * rows : (parity + 1) * rows, lane] = block.astype(BF16)


def sort_tables(rows, rows_out, bins_out):
    _, per, _ = rows_out.shape
    _, group = position()

    def one_hot(mask):
        return jnp.where(mask, 1.0, 0.0).astype(BF16)

    at = lax.broadcasted_iota(jnp.int32, (per, per), 0)
    lane = lax.broadcasted_iota(jnp.int32, (per, per), 1)
    for turned in range(2):
        row = packed_row_of(at, turned, 2 * per, rows)
        share = (row // rows) % 2
        source = row // (2 * rows) - turned * (per // (2 * rows))
        column = source * rows + row % rows + jnp.where(share == group, 0, per // 2)
        rows_out[turned] = one_hot(column == lane)
    wide = bins_out.shape[0]
    at = lax.broadcasted_iota(jnp.int32, (wide, wide), 0)
    lane = lax.broadcasted_iota(jnp.int32, (wide, wide), 1)
    bins_out[...] = one_hot(at == jnp.where(lane < wide // 2, 2 * lane, 2 * lane - wide + 1))


def packed_row_of(at, turned, first_len, rows):
    half = first_len // 4
    packed = at % half // (rows // 2) * rows + 2 * (at % (rows // 2)) + at // half
    if not turned:
        return packed
    return jnp.where(packed == 0, first_len // 2, first_len - packed)


def choose_kernel(order, cuts, own, other, by_rows, by_bins, out, held):
    place, _ = position()
    sources, rows, _ = own.shape
    per = sources * rows
    half_len = own.shape[2] // 2
    for source in range(sources):
        turned, at = source // (sources // 2), source % (sources // 2) * rows
        held[turned, at : at + rows, :] = own[source]
        held[turned, per // 2 + at : per // 2 + at + rows, :] = other[source]
    cut = cuts[order[place]]
    moved, room = [], []
    for turned in range(2):
        moved.append(matmul(by_rows[turned], held[turned]).reshape(per // (rows // 2), rows // 2, 2 * half_len))
        at = lax.broadcasted_iota(jnp.int32, (per, 128), 0)
        room.append((cut - packed_row_of(at, turned, 2 * per, rows)).reshape(per // (rows // 2), rows // 2, 128))
    picked = jnp.concatenate(moved, 1).reshape(2 * per, 2 * half_len).astype(BF16)
    room = jnp.concatenate(room, 1).reshape(2 * per, 128)
    wide = by_bins.shape[0]
    for part in range(2):
        for block in range(half_len // wide):
            lane = part * half_len + block * wide
            sorted_bins = matmul(picked[:, lane : lane + wide], by_bins[...])
            for odd in range(2):
                for at in range(0, wide // 2, 128):
                    first = block * (wide // 2) + at
                    bins = 2 * (first + lax.broadcasted_iota(jnp.int32, (1, 128), 1)) + odd
                    from_lane = odd * (wide // 2) + at
                    kept = jnp.where(
                        2 * per * bins < room, sorted_bins[:, from_lane : from_lane + 128], 0.0
                    )
                    to = part * half_len + odd * (half_len // 2) + first
                    out[:, to : to + 128] = kept.astype(BF16)


def filter_blocks(offsets, blocks, chosen, tables, norm, filtered, lifted):
    place, _ = position()
    even_table, odd_table, lift_c, lift_s = tables
    half_len = even_table.shape[0]
    quarter = half_len // 2
    first_len = chosen.shape[0]
    per = first_len // 2
    rows = blocks[0].shape[0] // 2
    groups = []
    for block, offset in zip(blocks, offsets):
        device = jnp.bitwise_xor(place, offset)
        for parity in range(2):
            row = slice(parity * rows, (parity + 1) * rows)
            at = aligned(parity * per + device * rows, rows)
            white_real = block[row, :half_len].astype(F32)
            white_imag = block[row, half_len : 2 * half_len].astype(F32)
            weight = block[row, 2 * half_len :].astype(F32)
            real = chosen[at, :half_len].astype(F32)
            imag = chosen[at, half_len:].astype(F32)
            norm = norm + (real * real + imag * imag) * weight
            filt_real = (white_real * real + white_imag * imag).astype(BF16)
            filt_imag = (white_imag * real - white_real * imag).astype(BF16)
            to = slice(len(groups) * rows, (len(groups) + 1) * rows)
            filtered[to, 0:quarter] = filt_real[:, :quarter]
            filtered[to, quarter:half_len] = filt_imag[:, :quarter]
            filtered[to, half_len : half_len + quarter] = filt_real[:, quarter:]
            filtered[to, half_len + quarter :] = filt_imag[:, quarter:]
            groups.append((to, at, parity * first_len + device * rows))
    for lane in range(0, half_len, PIECE):
        both = slice(2 * lane, 2 * (lane + PIECE))
        even = matmul(filtered[:, :half_len], even_table[:, both])
        odd = matmul(filtered[:, half_len:], odd_table[:, both])
        for upper in range(2):
            lanes = slice(upper * half_len + lane, upper * half_len + lane + PIECE)
            total = even - odd if upper else even + odd
            for row, at, target in groups:
                real, imag = total[row, :PIECE], total[row, PIECE:]
                cos, sin = lift_c[at, lanes], lift_s[at, lanes]
                lifted[aligned(target, rows), lanes] = (real * cos - imag * sin).astype(BF16)
                lifted[aligned(target + per, rows), lanes] = (real * sin + imag * cos).astype(BF16)
    return norm


def early_kernel(near, theirs, chosen, *refs):
    tables, (lifted, norm, filtered) = refs[:4], refs[4:]
    blocks = [*[near.at[at] for at in range(4)], *[theirs.at[at] for at in range(4)]]
    zero = jnp.zeros(norm.shape, F32)
    norm[...] = filter_blocks(EARLY, blocks, chosen, tables, zero, filtered, lifted)


def middle_kernel(six, ten, far, theirs, early, early_norm, chosen, *refs):
    tables, (lifted, norm, filtered) = refs[:4], refs[4:]
    blocks = [six, ten, far, *[theirs.at[at] for at in range(3)]]
    norm[...] = filter_blocks(MIDDLE, blocks, chosen, tables, early_norm[...], filtered, lifted)


def late_kernel(last, theirs, early, early_norm, chosen, *refs):
    tables, (cols_table, out, lifted, filtered, result, sems) = refs[:4], refs[4:]
    norm = filter_blocks(LATE, [last, theirs], chosen, tables, early_norm[...], filtered, lifted)
    scale = lax.rsqrt(jnp.sum(norm, keepdims=True))
    first_len = chosen.shape[0]
    per = first_len // 2
    wide = 256
    lanes = [slice(lane, lane + wide) for lane in range(0, lifted.shape[1], wide)]

    def products(at):
        return (
            matmul(cols_table[:, :first_len], lifted[:first_len, at]),
            matmul(cols_table[:, first_len:], lifted[first_len:, at]),
        )

    copies = []
    following = products(lanes[0])
    for block, at in enumerate(lanes):
        even, odd = following
        if block + 1 < len(lanes):
            following = products(lanes[block + 1])
        for upper in range(2):
            total = even - odd if upper else even + odd
            power = total[:per] * total[:per] + total[per:] * total[per:]
            size = power * lax.rsqrt(jnp.maximum(power, 1e-37))
            result[upper * per : (upper + 1) * per, at] = (size * scale).astype(BF16)
        copies.append(pltpu.make_async_copy(result.at[:, at], out.at[0, :, at], sems.at[block]))
        copies[-1].start()
    for copy in copies:
        copy.wait()


def swap_with(array, flip):
    pairs = [(at, at ^ flip) for at in range(lax.axis_size("tmpl"))]
    return lax.ppermute(array, "tmpl", pairs)


def tiled_local(strain, analysis, bank, cutoff, order):
    dev_count = lax.axis_size("tmpl")
    segs, first_len, cols = strain.shape
    second_len = cols * dev_count
    length = first_len * second_len
    half_len = second_len // 2
    rows = first_len // dev_count // 2
    templates = order.shape[0]
    lanes = 2 * (segs + 1) * cols

    first, second, half = np.arange(first_len), np.arange(second_len), np.arange(half_len)
    devices, step = np.arange(dev_count), np.arange(STEP)
    near = halves(rows)
    packed = (devices[:, None] * rows + near[None, :]).reshape(dev_count, 2, rows // 2)
    waves = []
    for odd in range(2):
        cos, sin = turns(packed[:, odd].reshape(-1, 1) * first[None, : first_len // 2], first_len)
        if not odd:
            sin[0] = 2 * (first[: first_len // 2] % 2) - 1.0
        waves.append(np.concatenate([cos, -sin]))
    win = np.stack(turns(np.arange(8)[:, None] + second_len * first[None, :], length))
    spin = np.stack(turns(cols * devices, length), 1)[:, :, None] * np.ones((1, 1, first_len), np.float32)
    turns_of_eight = [tuple(float(at) for at in turns(8 * block, length)) for block in range(cols // 8)]

    sent = pl.pallas_call(
        functools.partial(stage_one_kernel, turns_of_eight),
        in_specs=[outside()] * 7,
        out_specs=whole(),
        scratch_shapes=[
            pltpu.SMEM((templates,), jnp.int32),
            vmem((segs, cols, first_len), F32),
            vmem((cols, first_len), F32),
            vmem((2, first_len), F32),
            vmem((2, 8, first_len), F32),
            vmem((2, dev_count * rows, first_len // 2)),
            vmem((2, (segs + 1) * cols, first_len // 2)),
            pltpu.SemaphoreType.DMA((segs + 5,)),
            pltpu.SemaphoreType.DMA,
        ],
        out_shape=pltpu.VMEM((dev_count * rows, lanes + 2 * half_len), BF16),
        compiler_params=params(16),
        name="stage_one",
    )(
        *in_hbm(
            order, jnp.swapaxes(strain, 1, 2), jnp.swapaxes(analysis, 0, 1), spin, win,
            np.stack(waves).astype(BF16), bank,
        ),
    )
    moved = lax.all_to_all(
        sent.reshape(dev_count, rows, lanes + 2 * half_len), "tmpl", split_axis=0, concat_axis=0, tiled=True
    )
    own = moved[:, :, lanes:]
    other = lax.ppermute(own, "grp", [(0, 1), (1, 0)])

    split = halves(half_len)
    low = 2 * np.arange(rows // 2)
    lift_rows = [np.concatenate([low + odd, first_len - low - odd]) for odd in range(2)]
    lift_init = [turns(at[:, None] * second[None, :], length) for at in lift_rows]
    cols_parts = []
    for odd in range(2):
        straight = devices[:, None] * rows + low[None, :] + odd
        turned = np.where(straight == 0, first_len // 2, first_len - straight)
        cols_parts.append(np.concatenate([straight, turned], 1).reshape(-1))
    cols_rows = np.concatenate(cols_parts)
    mid_rows = lift_rows[0].copy()
    mid_rows[rows // 2] = first_len // 2
    step_sign = np.where(np.arange(rows) < rows // 2, rows, -rows)
    fore = [
        *turns(step[:, None] * split[None, :], second_len),
        *turns(STEP * split[None, :], second_len),
        *turns(near[:, None] * second[None, :], length),
        *turns(rows * devices[:, None, None] * second[None, None, :], length),
    ]
    forward, near_c, near_s = pl.pallas_call(
        forward_kernel,
        out_shape=[
            pltpu.VMEM((2, half_len, half_len), BF16),
            *[pltpu.VMEM((rows, second_len), F32)] * 2,
        ],
        in_specs=[whole()] * len(fore),
        out_specs=[whole()] * 3,
        compiler_params=params(16),
        cost_estimate=pl.CostEstimate(flops=10**7, bytes_accessed=2 * 10**7, transcendentals=0),
        name="forward_tables",
    )(*in_hbm(*fore))
    back = [
        *turns(2 * step[:, None] * half[None, :], second_len),
        *turns((2 * step[:, None] + 1) * half[None, :], second_len),
        *turns(2 * STEP * half[None, :], second_len),
        np.stack([lift_init[0][0], lift_init[1][0]]),
        np.stack([lift_init[0][1], lift_init[1][1]]),
        *turns(step_sign[:, None] * second[None, :], length),
        *turns(mid_rows[:, None] * second[None, :], length),
    ]
    columns = [
        *turns(step[:, None] * cols_rows[None, :], first_len),
        *turns(STEP * cols_rows[None, :], first_len),
    ]
    shapes = [
        ((half_len, second_len), BF16),
        ((half_len, second_len), BF16),
        ((first_len, second_len), F32),
        ((first_len, second_len), F32),
    ]
    column_shapes = [
        ((first_len, 2 * first_len), BF16),
        ((2, first_len // 2, first_len // 2), BF16),
        ((256, 256), BF16),
    ]
    inverse_tables = pl.pallas_call(
        inverse_tables_kernel,
        out_shape=[pltpu.VMEM(*shape) for shape in shapes],
        in_specs=[whole()] * len(back),
        out_specs=[whole()] * len(shapes),
        compiler_params=params(8),
        cost_estimate=pl.CostEstimate(flops=10**7, bytes_accessed=2 * 10**7, transcendentals=0),
        name="inverse_tables",
    )
    even_table, odd_table, lift_c, lift_s = inverse_tables(*in_hbm(*back))
    column_tables = pl.pallas_call(
        functools.partial(column_tables_kernel, rows),
        out_shape=[pltpu.VMEM(*shape) for shape in column_shapes],
        in_specs=[whole()] * len(columns),
        out_specs=[whole()] * len(column_shapes),
        compiler_params=params(8),
        cost_estimate=pl.CostEstimate(flops=10**7, bytes_accessed=10**7, transcendentals=0),
        name="column_tables",
    )
    cols_table, by_rows, by_bins = column_tables(*in_hbm(*columns))

    mid_c, mid_s = turns(first_len // 2 * second[None, :], length)
    all_rows = 2 * (segs + 2) * rows
    stage_two = pl.pallas_call(
        functools.partial(stage_two_kernel, segs, cols),
        out_shape=jax.ShapeDtypeStruct((2 * rows, 3 * half_len), BF16),
        in_specs=[whole()] * 3 + [outside()] * 2 + [whole()],
        out_specs=whole(),
        scratch_shapes=[
            *[vmem((1, second_len), F32)] * 2,
            vmem((2, all_rows, half_len)),
            vmem((rows, second_len), F32),
            vmem((all_rows, second_len), F32),
            pltpu.SemaphoreType.DMA((2,)),
        ],
        compiler_params=params(24),
        cost_estimate=pl.CostEstimate(flops=10**9, bytes_accessed=4 * 10**6, transcendentals=0),
        name="stage_two",
    )
    block = stage_two(moved, *in_vmem(near_c, near_s), *in_hbm(mid_c, mid_s), *in_vmem(forward))

    two = swap_with(block, 8)
    one = swap_with(block, 4)
    beside = swap_with(block, 2)
    far = swap_with(two, 4)
    ten = swap_with(two, 2)
    six = swap_with(one, 2)
    near = jnp.stack([block, beside, one, two])
    theirs = swap_with(near, 1)
    last_upper = swap_with(far[:rows], 2)
    last_lower = swap_with(ten[rows:], 4)
    last = jnp.concatenate([last_upper, last_lower], 0)
    more = swap_with(jnp.stack([six, ten, far]), 1)
    late = swap_with(last, 1)

    choose = pl.pallas_call(
        choose_kernel,
        grid_spec=pltpu.PrefetchScalarGridSpec(
            num_scalar_prefetch=2,
            grid=(),
            in_specs=[whole()] * 4,
            out_specs=whole(),
            scratch_shapes=[vmem((2, first_len // 2, 2 * half_len))],
        ),
        out_shape=jax.ShapeDtypeStruct((first_len, 2 * half_len), BF16),
        compiler_params=params(16),
        cost_estimate=pl.CostEstimate(flops=10**9, bytes_accessed=4 * 10**6, transcendentals=0),
        name="choose",
    )
    chosen = choose(order, cutoff, own, other, *in_vmem(by_rows, by_bins))

    spread = [(2 * first_len, second_len), BF16]
    tables = in_vmem(even_table, odd_table, lift_c, lift_s)
    early = pl.pallas_call(
        early_kernel,
        out_shape=[pltpu.VMEM(*spread), pltpu.VMEM((rows, half_len), F32)],
        in_specs=[whole()] * 7,
        out_specs=[whole()] * 2,
        scratch_shapes=[vmem((len(EARLY) * 2 * rows, 2 * half_len))],
        compiler_params=params(16),
        cost_estimate=pl.CostEstimate(flops=10**9, bytes_accessed=4 * 10**6, transcendentals=0),
        name="early",
    )
    lifted, norm = early(near, theirs, chosen, *tables)
    middle = pl.pallas_call(
        middle_kernel,
        out_shape=[pltpu.VMEM(*spread), pltpu.VMEM((rows, half_len), F32)],
        in_specs=[whole()] * 11,
        out_specs=[whole()] * 2,
        scratch_shapes=[vmem((len(MIDDLE) * 2 * rows, 2 * half_len))],
        input_output_aliases={4: 0},
        compiler_params=params(16),
        cost_estimate=pl.CostEstimate(flops=10**9, bytes_accessed=4 * 10**6, transcendentals=0),
        name="middle",
    )
    lifted, norm = middle(six, ten, far, more, *in_vmem(lifted, norm), chosen, *tables)
    result, _ = pl.pallas_call(
        late_kernel,
        out_shape=[pltpu.HBM((1, first_len, second_len), BF16), pltpu.VMEM(*spread)],
        in_specs=[whole()] * 10,
        out_specs=[outside(), whole()],
        scratch_shapes=[
            vmem((len(LATE) * 2 * rows, 2 * half_len)),
            vmem((first_len, second_len)),
            pltpu.SemaphoreType.DMA((second_len // 256,)),
        ],
        input_output_aliases={2: 1},
        compiler_params=params(16),
        name="late",
    )(last, late, *in_vmem(lifted, norm), chosen, *tables, *in_vmem(cols_table))
    return result


def angles(left_idx, right_idx, period):
    product = left_idx[:, None] * right_idx[None, :] % period
    phase_angle = product.astype(jnp.float32) * (2.0 * math.pi / period)
    return (jnp.cos(phase_angle), jnp.sin(phase_angle))


def filtered(white_pair, tmpl_pair, cut_bins, freq_bin):
    white_real = white_pair[0].astype(jnp.float32)
    white_imag = white_pair[1].astype(jnp.float32)
    tmpl_real = tmpl_pair[0].astype(jnp.float32)
    tmpl_imag = tmpl_pair[1].astype(jnp.float32)
    in_band = freq_bin[None] < cut_bins[:, None, None]
    filt_real = jnp.where(in_band, white_real * tmpl_real + white_imag * tmpl_imag, 0.0)
    filt_imag = jnp.where(in_band, white_imag * tmpl_real - white_real * tmpl_imag, 0.0)
    return jnp.concatenate([filt_real, filt_imag], -1).astype(jnp.bfloat16)


def inverse_rows(stacked, row_bins, second_len, length):
    half_len = second_len // 2
    cosine, sine = angles(
        jnp.arange(half_len, dtype=jnp.int32), jnp.arange(second_len, dtype=jnp.int32), second_len
    )
    dft_table = jnp.concatenate(
        [jnp.concatenate([cosine, sine], 1), jnp.concatenate([-sine, cosine], 1)], 0
    ).astype(jnp.bfloat16)
    spread = jnp.einsum("tkf,fg->tkg", stacked, dft_table, preferred_element_type=jnp.float32)
    spread_real = spread[..., :second_len]
    spread_imag = spread[..., second_len:]
    cos_twist, sin_twist = angles(row_bins, jnp.arange(second_len, dtype=jnp.int32), length)
    lift_real = spread_real * cos_twist - spread_imag * sin_twist
    lift_imag = spread_real * sin_twist + spread_imag * cos_twist
    return jnp.concatenate([lift_real, lift_imag], -1).astype(jnp.bfloat16)


def inverse_cols(lifted, first_len, second_len):
    row_idx = jnp.arange(first_len, dtype=jnp.int32)
    cosine, sine = angles(row_idx, row_idx, first_len)
    cosine = cosine.astype(jnp.bfloat16)
    sine = sine.astype(jnp.bfloat16)
    lift_real = lifted[..., :second_len]
    lift_imag = lifted[..., second_len:]
    field_real = jnp.einsum(
        "ak,tkb->tab", cosine, lift_real, preferred_element_type=jnp.float32
    ) - jnp.einsum("ak,tkb->tab", sine, lift_imag, preferred_element_type=jnp.float32)
    field_imag = jnp.einsum(
        "ak,tkb->tab", sine, lift_real, preferred_element_type=jnp.float32
    ) + jnp.einsum("ak,tkb->tab", cosine, lift_imag, preferred_element_type=jnp.float32)
    return (field_real, field_imag)


def plain_local(strain, analysis, bank, cutoff, order):
    highest = lax.Precision.HIGHEST
    dev_count = lax.axis_size("tmpl")
    my_index = lax.axis_index("tmpl")
    seg_count = strain.shape[0]
    first_len = strain.shape[1]
    col_count = strain.shape[2]
    second_len = col_count * dev_count
    length = first_len * second_len
    half_len = second_len // 2
    row_count = first_len // dev_count
    row_idx = jnp.arange(first_len, dtype=jnp.int32)
    col_index = my_index * col_count + jnp.arange(col_count, dtype=jnp.int32)
    sample_idx = row_idx[:, None] * second_len + col_index[None, :]
    window = (
        math.sqrt(8.0 / 3.0) * jnp.sin(sample_idx.astype(jnp.float32) * (math.pi / length)) ** 2
    )
    series = jnp.concatenate([strain * window, analysis[None]], 0)
    cos_one, sin_one = angles(row_idx, row_idx, first_len)
    part_real = jnp.einsum("ka,sab->skb", cos_one, series, precision=highest)
    part_imag = -jnp.einsum("ka,sab->skb", sin_one, series, precision=highest)
    cos_twist, sin_twist = angles(row_idx, col_index, length)
    twist_real = part_real * cos_twist + part_imag * sin_twist
    twist_imag = part_imag * cos_twist - part_real * sin_twist
    moved = lax.all_to_all(
        jnp.stack([twist_real, twist_imag]).astype(jnp.bfloat16),
        "tmpl",
        split_axis=2,
        concat_axis=3,
        tiled=True,
    ).astype(jnp.float32)
    cos_two, sin_two = angles(
        jnp.arange(second_len, dtype=jnp.int32), jnp.arange(half_len, dtype=jnp.int32), second_len
    )
    spec_real = jnp.einsum("skb,bf->skf", moved[0], cos_two, precision=highest) + jnp.einsum(
        "skb,bf->skf", moved[1], sin_two, precision=highest
    )
    spec_imag = jnp.einsum("skb,bf->skf", moved[1], cos_two, precision=highest) - jnp.einsum(
        "skb,bf->skf", moved[0], sin_two, precision=highest
    )
    power_spec = jnp.maximum(
        jnp.mean(spec_real[:seg_count] ** 2 + spec_imag[:seg_count] ** 2, axis=0), 0.2 * length
    )
    whitened = jnp.stack(
        [spec_real[seg_count] / power_spec, spec_imag[seg_count] / power_spec]
    ).astype(jnp.bfloat16)
    own_rows = my_index * row_count + jnp.arange(row_count, dtype=jnp.int32)
    half_idx = jnp.arange(half_len, dtype=jnp.int32)
    freq_local = own_rows[:, None] + first_len * half_idx[None, :]
    chosen = jnp.take(bank, order, axis=1)
    cuts = jnp.take(cutoff, order)
    bank_real = chosen[0].astype(jnp.float32)
    bank_imag = chosen[1].astype(jnp.float32)
    in_band = freq_local[None] < cuts[:, None, None]
    local_norm = jnp.sum(
        jnp.where(in_band, (bank_real**2 + bank_imag**2) / power_spec, 0.0), axis=(1, 2)
    )
    norm_sq = lax.psum(local_norm, "tmpl")
    per_device = cuts.shape[0] // dev_count
    own_norm = lax.dynamic_slice_in_dim(norm_sq, my_index * per_device, per_device)
    stacked = filtered(whitened, chosen, cuts, freq_local)
    lifted = lax.all_to_all(
        inverse_rows(stacked, own_rows, second_len, length),
        "tmpl",
        split_axis=0,
        concat_axis=1,
        tiled=True,
    )
    field_real, field_imag = inverse_cols(lifted, first_len, second_len)
    magnitude = jnp.sqrt(field_real**2 + field_imag**2)
    return (magnitude / jnp.sqrt(own_norm)[:, None, None]).astype(jnp.bfloat16)


def local(strain, analysis, bank, cutoff, order):
    dev_count, segs, cols = lax.axis_size("tmpl"), strain.shape[0], strain.shape[2]
    rows = strain.shape[1] // dev_count // 2
    fits = rows == STEP and cols == 64 and segs % 2 == 0 and dev_count == len(EARLY + MIDDLE + LATE)
    if fits and order.shape[0] == dev_count and lax.axis_size("grp") == 2:
        return tiled_local(strain, analysis, bank, cutoff, order)
    return plain_local(strain, analysis, bank, cutoff, order)


def solution(mesh):
    return jax.shard_map(
        local,
        mesh=mesh,
        in_specs=(P("grp", None, "tmpl"), P("grp", "tmpl"), P(None, None, "tmpl", None), P(), P()),
        out_specs=P(("grp", "tmpl"), None, None),
        check_vma=False,
    )
```

```python
import functools
import math

import jax
import jax.numpy as jnp
import numpy as np
from jax import lax
from jax.experimental import pallas as pl
from jax.experimental.pallas import tpu as pltpu
from jax.sharding import PartitionSpec as P

BF16 = jnp.bfloat16
F32 = jnp.float32
STEP = 16
PIECE = 128
EARLY = (0, 2, 4, 8, 1, 3, 5, 9)
MIDDLE = (6, 10, 12, 7, 11, 13)
LATE = (14, 15)


def turns(product, period):
    angle = (product % period) * (2.0 * math.pi / period)
    return np.cos(angle).astype(np.float32), np.sin(angle).astype(np.float32)


def matmul(left, right):
    return jnp.dot(left, right, preferred_element_type=F32)


def matmul_nt(left, right):
    return lax.dot_general(left, right, (((1,), (1,)), ((), ())), preferred_element_type=F32)


def vmem(shape, dtype=BF16):
    return pltpu.VMEM(shape, dtype)


def whole():
    return pl.BlockSpec(memory_space=pltpu.VMEM)


def outside():
    return pl.BlockSpec(memory_space=pltpu.HBM)


def in_hbm(*arrays):
    return [pltpu.with_memory_space_constraint(jnp.asarray(array), pltpu.HBM) for array in arrays]


def in_vmem(*arrays):
    return [pltpu.with_memory_space_constraint(array, pltpu.VMEM) for array in arrays]


def position():
    return lax.axis_index("tmpl"), lax.axis_index("grp")


def start_copies(pairs, sems):
    copies = [
        pltpu.make_async_copy(source, target, sems.at[at]) for at, (source, target) in enumerate(pairs)
    ]
    for copy in copies:
        copy.start()
    return copies


def params(mib):
    return pltpu.CompilerParams(vmem_limit_bytes=mib << 20)


def turn(cos, sin, by_cos, by_sin):
    return cos * by_cos - sin * by_sin, sin * by_cos + cos * by_sin


def halves(count):
    return np.concatenate([np.arange(0, count, 2), np.arange(1, count, 2)])


def aligned(start, size):
    return pl.ds(pl.multiple_of(start, size), size)


def stage_one_kernel(
    turns_of_eight, order_hbm, strain_hbm, analysis_hbm, spin_hbm, win_hbm, wave_hbm, bank, out,
    order, strain, analysis, spin, win, wave, packed, sems, bank_sem,
):
    segs, cols, first_len = strain.shape
    tail = segs * cols
    templates, half_len = bank.shape[1], bank.shape[3]
    rows = out.shape[0] // templates
    half = first_len // 2
    place, group = position()
    sources = [
        (order_hbm, order),
        (spin_hbm.at[place], spin),
        (win_hbm, win),
        *[(strain_hbm.at[seg], strain.at[seg]) for seg in range(segs)],
        (analysis_hbm, analysis),
        (wave_hbm, wave),
    ]
    copies = start_copies(sources, sems)
    lane = 2 * (tail + cols)
    copies[0].wait()
    bank_pairs = []
    for row in range(templates):
        for part in range(2):
            bank_pairs.append(
                (
                    bank.at[part, order[row], aligned(group * rows, rows), :],
                    out.at[
                        row * rows : (row + 1) * rows,
                        lane + part * half_len : lane + (part + 1) * half_len,
                    ],
                )
            )
    for source, target in bank_pairs:
        pltpu.make_async_copy(source, target, bank_sem).start()
    for copy in copies[1:3]:
        copy.wait()
    scale = 0.5 * math.sqrt(8.0 / 3.0)
    win_c, win_s = turn(win[0], win[1], spin[0:1, :], spin[1:2, :])
    window = jnp.concatenate(
        [scale - (win_c * (scale * by_cos) - win_s * (scale * by_sin)) for by_cos, by_sin in turns_of_eight], 0
    )

    def pack(at, values):
        packed[0, at : at + cols, :] = (values[:, :half] + values[:, half:]).astype(BF16)
        packed[1, at : at + cols, :] = (values[:, :half] - values[:, half:]).astype(BF16)

    for seg in range(segs):
        copies[3 + seg].wait()
        pack(seg * cols, strain[seg] * window)
    copies[3 + segs].wait()
    pack(tail, analysis[...])
    copies[4 + segs].wait()
    both = [matmul_nt(wave[odd], packed[odd]) for odd in range(2)]
    count = out.shape[0] // 2

    def woven(part):
        halves_of = [
            table[part * count : (part + 1) * count].reshape(templates, rows // 2, tail + cols) for table in both
        ]
        return jnp.concatenate(halves_of, 1).reshape(2 * count, tail + cols)

    real, imag = woven(0), woven(1)
    out[:, 0:tail] = real[:, :tail].astype(BF16)
    out[:, tail : 2 * tail] = imag[:, :tail].astype(BF16)
    joined = jnp.concatenate([real[:, tail:], imag[:, tail:]], 1)
    out[:, 2 * tail : lane] = joined.astype(BF16)
    whole_bank = out.at[:, lane:]
    pltpu.make_async_copy(whole_bank, whole_bank, bank_sem).wait()


def forward_kernel(
    fore_c, fore_s, fore_rc, fore_rs, near_c, near_s, base_c, base_s,
    forward, near_out_c, near_out_s,
):
    half_len = fore_c.shape[1]
    quarter = half_len // 2
    place, _ = position()
    first_lane = lax.broadcasted_iota(jnp.int32, fore_c.shape, 1) == 0
    sign = 1.0 - 2.0 * (lax.broadcasted_iota(jnp.int32, fore_c.shape, 0) % 2).astype(F32)

    def fore(step, carry):
        cos, sin = carry
        for part, table in enumerate((cos, jnp.where(first_lane, sign, sin))):
            for odd in range(2):
                lane = slice(odd * quarter, (odd + 1) * quarter)
                to = slice(part * quarter, (part + 1) * quarter)
                forward[odd, aligned(step * STEP, STEP), to] = table[:, lane].astype(BF16)
        return turn(cos, sin, fore_rc[...], fore_rs[...])

    lax.fori_loop(0, forward.shape[1] // STEP, fore, (fore_c[...], fore_s[...]))
    near_out_c[...], near_out_s[...] = turn(near_c[...], near_s[...], base_c[place], base_s[place])


def inverse_tables_kernel(
    even_c, even_s, odd_c, odd_s, rows_rc, rows_rs, even_out, odd_out
):
    half_len = even_c.shape[1]
    quarter = half_len // 2

    def spread(out, cos, sin):
        def body(step, carry):
            cos, sin = carry
            upper = aligned(step * STEP, STEP)
            lower = aligned(quarter + step * STEP, STEP)
            for lane in range(0, half_len, PIECE):
                real, imag = slice(2 * lane, 2 * lane + PIECE), slice(2 * lane + PIECE, 2 * (lane + PIECE))
                cos_at, sin_at = cos[:, lane : lane + PIECE], sin[:, lane : lane + PIECE]
                out[upper, real] = cos_at.astype(BF16)
                out[upper, imag] = sin_at.astype(BF16)
                out[lower, real] = (-sin_at).astype(BF16)
                out[lower, imag] = cos_at.astype(BF16)
            return turn(cos, sin, rows_rc[...], rows_rs[...])

        lax.fori_loop(0, quarter // STEP, body, (cos, sin))

    spread(even_out, even_c[...], even_s[...])
    spread(odd_out, odd_c[...], odd_s[...])


def lift_tables_kernel(
    lift_c, lift_s, lift_rc, lift_rs, mid_c, mid_s, lift_out_c, lift_out_s
):
    per = lift_out_c.shape[0] // 2
    for parity in range(2):

        def lifts(step, carry, parity=parity):
            cos, sin = carry
            at = aligned(parity * per + step * STEP, STEP)
            lift_out_c[at, :] = cos
            lift_out_s[at, :] = sin
            return turn(cos, sin, lift_rc[...], lift_rs[...])

        lax.fori_loop(0, per // STEP, lifts, (lift_c[parity], lift_s[parity]))
    lift_out_c[0:STEP, :] = mid_c[...]
    lift_out_s[0:STEP, :] = mid_s[...]


def column_tables_kernel(rows, cols_c, cols_s, cols_rc, cols_rs, cols_out, rows_out, bins_out):
    first_len = cols_c.shape[1]
    per = first_len // 2

    def columns(step, carry):
        cos, sin = carry
        upper = aligned(step * STEP, STEP)
        lower = aligned(per + step * STEP, STEP)
        for parity in range(2):
            at = slice(parity * per, (parity + 1) * per)
            left = slice(parity * first_len, parity * first_len + per)
            right = slice(parity * first_len + per, (parity + 1) * first_len)
            cols_out[upper, left] = cos[:, at].astype(BF16)
            cols_out[upper, right] = (-sin[:, at]).astype(BF16)
            cols_out[lower, left] = sin[:, at].astype(BF16)
            cols_out[lower, right] = cos[:, at].astype(BF16)
        return turn(cos, sin, cols_rc[...], cols_rs[...])

    lax.fori_loop(0, per // STEP, columns, (cols_c[...], cols_s[...]))
    sort_tables(rows, rows_out, bins_out)


def stage_two_kernel(
    segs, cols, moved, near_c, near_s, mid_c_hbm, mid_s_hbm, forward, out,
    mid_c, mid_s, stacked, middle, product, sems,
):
    place, _ = position()
    _, half_len, _ = forward.shape
    second_len = 2 * half_len
    quarter = half_len // 2
    copies = start_copies([(mid_c_hbm, mid_c), (mid_s_hbm, mid_s)], sems)
    sources, rows, _ = moved.shape
    tail = segs * cols
    all_rows = (segs + 1) * rows
    width = 2 * cols
    low = lax.broadcasted_iota(jnp.int32, (rows, width), 1) < cols
    own_first = place == 0
    packed_row = lax.broadcasted_iota(jnp.int32, (rows, width), 0) == 0
    drop = jnp.logical_and(packed_row, own_first)

    def pair(left, right):
        return (
            jnp.where(low, left, pltpu.roll(right, cols, 1)),
            jnp.where(low, pltpu.roll(left, cols, 1), right),
        )

    middle[...] = jnp.zeros_like(middle)
    tiles = sources // 2
    for tile in range(tiles // 2):
        lane = slice(tile * width, (tile + 1) * width)
        lanes = (lane, slice(half_len + tile * width, half_len + (tile + 1) * width))

        def piece(lo, tile=tile):
            hi = lo + width
            found = []
            for source in (2 * tile, 2 * tile + tiles):
                found.append(
                    pair(moved[source, :, lo:hi].astype(F32), moved[source + 1, :, lo:hi].astype(F32))
                )
            return [(found[0][at], found[1][at]) for at in range(2)]

        def put(seg, real, imag, lane=lane, lanes=lanes):
            turned_real, turned_imag = [], []
            for half in range(2):
                middle[seg : seg + 1, lanes[half]] = imag[half][0:1, :]
                kept = jnp.where(drop, 0.0, imag[half])
                cos, sin = near_c[:, lanes[half]], near_s[:, lanes[half]]
                turned_real.append(real[half] * cos + kept * sin)
                turned_imag.append(kept * cos - real[half] * sin)
            for at, (low_half, high_half) in ((seg * rows, turned_real), (all_rows + seg * rows, turned_imag)):
                stacked[0, at : at + rows, lane] = (low_half + high_half).astype(BF16)
                stacked[1, at : at + rows, lane] = (low_half - high_half).astype(BF16)

        for twin in range(segs // 2):
            real_one, real_two = piece(twin * width)
            imag_one, imag_two = piece(tail + twin * width)
            put(2 * twin, real_one, imag_one)
            put(2 * twin + 1, real_two, imag_two)
        real, imag = piece(2 * tail)
        put(segs, real, imag)
    for copy in copies:
        copy.wait()
    for part, turned in enumerate((middle[...] * mid_c[...], middle[...] * -mid_s[...])):
        at = slice(2 * all_rows + part * rows, 2 * all_rows + (part + 1) * rows)
        stacked[0, at, :] = (turned[:, :half_len] + turned[:, half_len:]).astype(BF16)
        stacked[1, at, :] = (turned[:, :half_len] - turned[:, half_len:]).astype(BF16)

    first_lane = lax.broadcasted_iota(jnp.int32, (rows, quarter), 1) == 0
    swap = jnp.logical_and(lax.broadcasted_iota(jnp.int32, (rows, quarter), 0) == 0, own_first)
    floor = 0.2 * (second_len * 2 * sources * rows)
    upper, lower = [], []
    for odd in range(2):
        cos_at = slice(odd * half_len, odd * half_len + quarter)
        sin_at = slice(odd * half_len + quarter, (odd + 1) * half_len)
        product[:, odd * half_len : (odd + 1) * half_len] = matmul(stacked[odd], forward[odd])

        def parts(at, lower_at, cos_at=cos_at, sin_at=sin_at):
            return (
                product[at : at + rows, cos_at],
                product[at : at + rows, sin_at],
                product[lower_at : lower_at + rows, cos_at],
                product[lower_at : lower_at + rows, sin_at],
            )

        def direct_of(rc, rs, ic, imag_s, odd=odd):
            if not odd:
                rs, imag_s = jnp.where(first_lane, 0.0, rs), jnp.where(first_lane, 0.0, imag_s)
            return rc + imag_s, ic - rs

        def mirror_of(rc, rs, ic, imag_s, odd=odd):
            real, imag = rc - imag_s, ic + rs
            if not odd:
                real, imag = jnp.where(first_lane, rs, real), jnp.where(first_lane, imag_s, imag)
            return real, imag

        level = jnp.zeros((rows, quarter), F32)
        mirror_level = level
        for seg in range(segs):
            four = parts(seg * rows, all_rows + seg * rows)
            real, imag = direct_of(*four)
            level = level + (real * real + imag * imag)
            real, imag = mirror_of(*four)
            mirror_level = mirror_level + (real * real + imag * imag)
        four = parts(segs * rows, all_rows + segs * rows)
        real, imag = direct_of(*four)
        mirror_real, mirror_imag = mirror_of(*four)
        mid_real, mid_imag = mirror_of(*parts(2 * all_rows, 2 * all_rows + rows))
        mid_level = jnp.sum((mid_real * mid_real + mid_imag * mid_imag)[:segs], 0, keepdims=True)
        mirror_level = jnp.where(swap, mid_level, mirror_level)
        mirror_real = jnp.where(swap, mid_real[segs : segs + 1], mirror_real)
        mirror_imag = jnp.where(swap, mid_imag[segs : segs + 1], mirror_imag)
        level = jnp.maximum(level * (1.0 / segs), floor)
        mirror_level = jnp.maximum(mirror_level * (1.0 / segs), floor)
        upper.append((real / level, imag / level, 1.0 / level))
        lower.append((mirror_real / mirror_level, -mirror_imag / mirror_level, 1.0 / mirror_level))
    eighth = rows // 2
    for part in range(3):
        mirrored = (lower[1][part], pltpu.roll(lower[0][part], quarter - 1, 1))
        for odd in range(2):
            lane = slice(part * half_len + odd * quarter, part * half_len + (odd + 1) * quarter)
            for parity in range(2):
                at = slice(parity * eighth, (parity + 1) * eighth)
                block = jnp.concatenate([upper[odd][part][at], mirrored[odd][at]], 0)
                out[parity * rows : (parity + 1) * rows, lane] = block.astype(BF16)


def sort_tables(rows, rows_out, bins_out):
    _, per, _ = rows_out.shape
    _, group = position()

    def one_hot(mask):
        return jnp.where(mask, 1.0, 0.0).astype(BF16)

    at = lax.broadcasted_iota(jnp.int32, (per, per), 0)
    lane = lax.broadcasted_iota(jnp.int32, (per, per), 1)
    for turned in range(2):
        row = packed_row_of(at, turned, 2 * per, rows)
        share = (row // rows) % 2
        source = row // (2 * rows) - turned * (per // (2 * rows))
        column = source * rows + row % rows + jnp.where(share == group, 0, per // 2)
        rows_out[turned] = one_hot(column == lane)
    wide = bins_out.shape[0]
    at = lax.broadcasted_iota(jnp.int32, (wide, wide), 0)
    lane = lax.broadcasted_iota(jnp.int32, (wide, wide), 1)
    bins_out[...] = one_hot(at == jnp.where(lane < wide // 2, 2 * lane, 2 * lane - wide + 1))


def packed_row_of(at, turned, first_len, rows):
    half = first_len // 4
    packed = at % half // (rows // 2) * rows + 2 * (at % (rows // 2)) + at // half
    if not turned:
        return packed
    return jnp.where(packed == 0, first_len // 2, first_len - packed)


def choose_kernel(order, cuts, own, other, by_rows, by_bins, out, held):
    place, _ = position()
    sources, rows, _ = own.shape
    per = sources * rows
    half_len = own.shape[2] // 2
    for source in range(sources):
        turned, at = source // (sources // 2), source % (sources // 2) * rows
        held[turned, at : at + rows, :] = own[source]
        held[turned, per // 2 + at : per // 2 + at + rows, :] = other[source]
    cut = cuts[order[place]]
    moved, room = [], []
    for turned in range(2):
        moved.append(matmul(by_rows[turned], held[turned]).reshape(per // (rows // 2), rows // 2, 2 * half_len))
        at = lax.broadcasted_iota(jnp.int32, (per, 128), 0)
        room.append((cut - packed_row_of(at, turned, 2 * per, rows)).reshape(per // (rows // 2), rows // 2, 128))
    picked = jnp.concatenate(moved, 1).reshape(2 * per, 2 * half_len).astype(BF16)
    room = jnp.concatenate(room, 1).reshape(2 * per, 128)
    wide = by_bins.shape[0]
    for part in range(2):
        for block in range(half_len // wide):
            lane = part * half_len + block * wide
            sorted_bins = matmul(picked[:, lane : lane + wide], by_bins[...])
            for odd in range(2):
                for at in range(0, wide // 2, 128):
                    first = block * (wide // 2) + at
                    bins = 2 * (first + lax.broadcasted_iota(jnp.int32, (1, 128), 1)) + odd
                    from_lane = odd * (wide // 2) + at
                    kept = jnp.where(
                        2 * per * bins < room, sorted_bins[:, from_lane : from_lane + 128], 0.0
                    )
                    to = part * half_len + odd * (half_len // 2) + first
                    out[:, to : to + 128] = kept.astype(BF16)


def filter_blocks(offsets, blocks, chosen, tables, norm, filtered, lifted):
    place, _ = position()
    even_table, odd_table, lift_c, lift_s = tables
    half_len = even_table.shape[0]
    quarter = half_len // 2
    first_len = chosen.shape[0]
    per = first_len // 2
    rows = blocks[0].shape[0] // 2
    groups = []
    for block, offset in zip(blocks, offsets):
        device = jnp.bitwise_xor(place, offset)
        for parity in range(2):
            row = slice(parity * rows, (parity + 1) * rows)
            at = aligned(parity * per + device * rows, rows)
            white_real = block[row, :half_len].astype(F32)
            white_imag = block[row, half_len : 2 * half_len].astype(F32)
            weight = block[row, 2 * half_len :].astype(F32)
            real = chosen[at, :half_len].astype(F32)
            imag = chosen[at, half_len:].astype(F32)
            norm = norm + (real * real + imag * imag) * weight
            filt_real = (white_real * real + white_imag * imag).astype(BF16)
            filt_imag = (white_imag * real - white_real * imag).astype(BF16)
            to = slice(len(groups) * rows, (len(groups) + 1) * rows)
            filtered[to, 0:quarter] = filt_real[:, :quarter]
            filtered[to, quarter:half_len] = filt_imag[:, :quarter]
            filtered[to, half_len : half_len + quarter] = filt_real[:, quarter:]
            filtered[to, half_len + quarter :] = filt_imag[:, quarter:]
            groups.append((to, at, parity * first_len + device * rows))
    for lane in range(0, half_len, PIECE):
        both = slice(2 * lane, 2 * (lane + PIECE))
        even = matmul(filtered[:, :half_len], even_table[:, both])
        odd = matmul(filtered[:, half_len:], odd_table[:, both])
        for upper in range(2):
            lanes = slice(upper * half_len + lane, upper * half_len + lane + PIECE)
            total = even - odd if upper else even + odd
            for row, at, target in groups:
                real, imag = total[row, :PIECE], total[row, PIECE:]
                cos, sin = lift_c[at, lanes], lift_s[at, lanes]
                lifted[aligned(target, rows), lanes] = (real * cos - imag * sin).astype(BF16)
                lifted[aligned(target + per, rows), lanes] = (real * sin + imag * cos).astype(BF16)
    return norm


def early_kernel(near, theirs, chosen, *refs):
    tables, (lifted, norm, filtered) = refs[:4], refs[4:]
    blocks = [*[near.at[at] for at in range(4)], *[theirs.at[at] for at in range(4)]]
    zero = jnp.zeros(norm.shape, F32)
    norm[...] = filter_blocks(EARLY, blocks, chosen, tables, zero, filtered, lifted)


def middle_kernel(six, ten, far, theirs, early, early_norm, chosen, *refs):
    tables, (lifted, norm, filtered) = refs[:4], refs[4:]
    blocks = [six, ten, far, *[theirs.at[at] for at in range(3)]]
    norm[...] = filter_blocks(MIDDLE, blocks, chosen, tables, early_norm[...], filtered, lifted)


def late_kernel(last, theirs, early, early_norm, chosen, *refs):
    tables, (cols_table, out, lifted, filtered, result, sems) = refs[:4], refs[4:]
    norm = filter_blocks(LATE, [last, theirs], chosen, tables, early_norm[...], filtered, lifted)
    scale = lax.rsqrt(jnp.sum(norm, keepdims=True))
    first_len = chosen.shape[0]
    per = first_len // 2
    wide = 256
    lanes = [slice(lane, lane + wide) for lane in range(0, lifted.shape[1], wide)]

    def products(at):
        return (
            matmul(cols_table[:, :first_len], lifted[:first_len, at]),
            matmul(cols_table[:, first_len:], lifted[first_len:, at]),
        )

    copies = []
    following = products(lanes[0])
    for block, at in enumerate(lanes):
        even, odd = following
        if block + 1 < len(lanes):
            following = products(lanes[block + 1])
        for upper in range(2):
            total = even - odd if upper else even + odd
            power = total[:per] * total[:per] + total[per:] * total[per:]
            size = power * lax.rsqrt(jnp.maximum(power, 1e-37))
            result[upper * per : (upper + 1) * per, at] = (size * scale).astype(BF16)
        copies.append(pltpu.make_async_copy(result.at[:, at], out.at[0, :, at], sems.at[block]))
        copies[-1].start()
    for copy in copies:
        copy.wait()


def swap_with(array, flip):
    pairs = [(at, at ^ flip) for at in range(lax.axis_size("tmpl"))]
    return lax.ppermute(array, "tmpl", pairs)


def tiled_local(strain, analysis, bank, cutoff, order):
    dev_count = lax.axis_size("tmpl")
    segs, first_len, cols = strain.shape
    second_len = cols * dev_count
    length = first_len * second_len
    half_len = second_len // 2
    rows = first_len // dev_count // 2
    templates = order.shape[0]
    lanes = 2 * (segs + 1) * cols

    first, second, half = np.arange(first_len), np.arange(second_len), np.arange(half_len)
    devices, step = np.arange(dev_count), np.arange(STEP)
    near = halves(rows)
    packed = (devices[:, None] * rows + near[None, :]).reshape(dev_count, 2, rows // 2)
    waves = []
    for odd in range(2):
        cos, sin = turns(packed[:, odd].reshape(-1, 1) * first[None, : first_len // 2], first_len)
        if not odd:
            sin[0] = 2 * (first[: first_len // 2] % 2) - 1.0
        waves.append(np.concatenate([cos, -sin]))
    win = np.stack(turns(np.arange(8)[:, None] + second_len * first[None, :], length))
    spin = np.stack(turns(cols * devices, length), 1)[:, :, None] * np.ones((1, 1, first_len), np.float32)
    turns_of_eight = [tuple(float(at) for at in turns(8 * block, length)) for block in range(cols // 8)]

    sent = pl.pallas_call(
        functools.partial(stage_one_kernel, turns_of_eight),
        in_specs=[outside()] * 7,
        out_specs=whole(),
        scratch_shapes=[
            pltpu.SMEM((templates,), jnp.int32),
            vmem((segs, cols, first_len), F32),
            vmem((cols, first_len), F32),
            vmem((2, first_len), F32),
            vmem((2, 8, first_len), F32),
            vmem((2, dev_count * rows, first_len // 2)),
            vmem((2, (segs + 1) * cols, first_len // 2)),
            pltpu.SemaphoreType.DMA((segs + 5,)),
            pltpu.SemaphoreType.DMA,
        ],
        out_shape=pltpu.VMEM((dev_count * rows, lanes + 2 * half_len), BF16),
        compiler_params=params(16),
        name="stage_one",
    )(
        *in_hbm(
            order, jnp.swapaxes(strain, 1, 2), jnp.swapaxes(analysis, 0, 1), spin, win,
            np.stack(waves).astype(BF16), bank,
        ),
    )
    moved = lax.all_to_all(
        sent.reshape(dev_count, rows, lanes + 2 * half_len), "tmpl", split_axis=0, concat_axis=0, tiled=True
    )
    own = moved[:, :, lanes:]
    other = lax.ppermute(own, "grp", [(0, 1), (1, 0)])

    split = halves(half_len)
    low = 2 * np.arange(rows // 2)
    lift_rows = [np.concatenate([low + odd, first_len - low - odd]) for odd in range(2)]
    lift_init = [turns(at[:, None] * second[None, :], length) for at in lift_rows]
    cols_parts = []
    for odd in range(2):
        straight = devices[:, None] * rows + low[None, :] + odd
        turned = np.where(straight == 0, first_len // 2, first_len - straight)
        cols_parts.append(np.concatenate([straight, turned], 1).reshape(-1))
    cols_rows = np.concatenate(cols_parts)
    mid_rows = lift_rows[0].copy()
    mid_rows[rows // 2] = first_len // 2
    step_sign = np.where(np.arange(rows) < rows // 2, rows, -rows)
    fore = [
        *turns(step[:, None] * split[None, :], second_len),
        *turns(STEP * split[None, :], second_len),
        *turns(near[:, None] * second[None, :], length),
        *turns(rows * devices[:, None, None] * second[None, None, :], length),
    ]
    forward, near_c, near_s = pl.pallas_call(
        forward_kernel,
        out_shape=[
            pltpu.VMEM((2, half_len, half_len), BF16),
            *[pltpu.VMEM((rows, second_len), F32)] * 2,
        ],
        in_specs=[whole()] * len(fore),
        out_specs=[whole()] * 3,
        compiler_params=params(16),
        cost_estimate=pl.CostEstimate(flops=10**7, bytes_accessed=2 * 10**7, transcendentals=0),
        name="forward_tables",
    )(*in_hbm(*fore))
    back = [
        *turns(2 * step[:, None] * half[None, :], second_len),
        *turns((2 * step[:, None] + 1) * half[None, :], second_len),
        *turns(2 * STEP * half[None, :], second_len),
    ]
    lifts = [
        np.stack([lift_init[0][0], lift_init[1][0]]),
        np.stack([lift_init[0][1], lift_init[1][1]]),
        *turns(step_sign[:, None] * second[None, :], length),
        *turns(mid_rows[:, None] * second[None, :], length),
    ]
    columns = [
        *turns(step[:, None] * cols_rows[None, :], first_len),
        *turns(STEP * cols_rows[None, :], first_len),
    ]
    shapes = [((half_len, second_len), BF16)] * 2
    lift_shapes = [((first_len, second_len), F32)] * 2
    column_shapes = [
        ((first_len, 2 * first_len), BF16),
        ((2, first_len // 2, first_len // 2), BF16),
        ((256, 256), BF16),
    ]
    inverse_tables = pl.pallas_call(
        inverse_tables_kernel,
        out_shape=[pltpu.VMEM(*shape) for shape in shapes],
        in_specs=[whole()] * len(back),
        out_specs=[whole()] * len(shapes),
        compiler_params=params(8),
        cost_estimate=pl.CostEstimate(flops=10**7, bytes_accessed=2 * 10**7, transcendentals=0),
        name="inverse_tables",
    )
    even_table, odd_table = inverse_tables(*in_hbm(*back))
    lift_tables = pl.pallas_call(
        lift_tables_kernel,
        out_shape=[pltpu.VMEM(*shape) for shape in lift_shapes],
        in_specs=[whole()] * len(lifts),
        out_specs=[whole()] * len(lift_shapes),
        compiler_params=params(8),
        cost_estimate=pl.CostEstimate(flops=10**7, bytes_accessed=10**7, transcendentals=0),
        name="lift_tables",
    )
    lift_c, lift_s = lift_tables(*in_hbm(*lifts))
    column_tables = pl.pallas_call(
        functools.partial(column_tables_kernel, rows),
        out_shape=[pltpu.VMEM(*shape) for shape in column_shapes],
        in_specs=[whole()] * len(columns),
        out_specs=[whole()] * len(column_shapes),
        compiler_params=params(8),
        cost_estimate=pl.CostEstimate(flops=10**7, bytes_accessed=10**7, transcendentals=0),
        name="column_tables",
    )
    cols_table, by_rows, by_bins = column_tables(*in_hbm(*columns))

    mid_c, mid_s = turns(first_len // 2 * second[None, :], length)
    all_rows = 2 * (segs + 2) * rows
    stage_two = pl.pallas_call(
        functools.partial(stage_two_kernel, segs, cols),
        out_shape=jax.ShapeDtypeStruct((2 * rows, 3 * half_len), BF16),
        in_specs=[whole()] * 3 + [outside()] * 2 + [whole()],
        out_specs=whole(),
        scratch_shapes=[
            *[vmem((1, second_len), F32)] * 2,
            vmem((2, all_rows, half_len)),
            vmem((rows, second_len), F32),
            vmem((all_rows, second_len), F32),
            pltpu.SemaphoreType.DMA((2,)),
        ],
        compiler_params=params(24),
        cost_estimate=pl.CostEstimate(flops=10**9, bytes_accessed=4 * 10**6, transcendentals=0),
        name="stage_two",
    )
    block = stage_two(moved, *in_vmem(near_c, near_s), *in_hbm(mid_c, mid_s), *in_vmem(forward))

    two = swap_with(block, 8)
    one = swap_with(block, 4)
    beside = swap_with(block, 2)
    far = swap_with(two, 4)
    ten = swap_with(two, 2)
    six = swap_with(one, 2)
    near = jnp.stack([block, beside, one, two])
    theirs = swap_with(near, 1)
    last_upper = swap_with(far[:rows], 2)
    last_lower = swap_with(ten[rows:], 4)
    last = jnp.concatenate([last_upper, last_lower], 0)
    more = swap_with(jnp.stack([six, ten, far]), 1)
    late = swap_with(last, 1)

    choose = pl.pallas_call(
        choose_kernel,
        grid_spec=pltpu.PrefetchScalarGridSpec(
            num_scalar_prefetch=2,
            grid=(),
            in_specs=[whole()] * 4,
            out_specs=whole(),
            scratch_shapes=[vmem((2, first_len // 2, 2 * half_len))],
        ),
        out_shape=jax.ShapeDtypeStruct((first_len, 2 * half_len), BF16),
        compiler_params=params(16),
        cost_estimate=pl.CostEstimate(flops=10**9, bytes_accessed=4 * 10**6, transcendentals=0),
        name="choose",
    )
    chosen = choose(order, cutoff, own, other, *in_vmem(by_rows, by_bins))

    spread = [(2 * first_len, second_len), BF16]
    tables = in_vmem(even_table, odd_table, lift_c, lift_s)
    early = pl.pallas_call(
        early_kernel,
        out_shape=[pltpu.VMEM(*spread), pltpu.VMEM((rows, half_len), F32)],
        in_specs=[whole()] * 7,
        out_specs=[whole()] * 2,
        scratch_shapes=[vmem((len(EARLY) * 2 * rows, 2 * half_len))],
        compiler_params=params(16),
        cost_estimate=pl.CostEstimate(flops=10**9, bytes_accessed=4 * 10**6, transcendentals=0),
        name="early",
    )
    lifted, norm = early(near, theirs, chosen, *tables)
    middle = pl.pallas_call(
        middle_kernel,
        out_shape=[pltpu.VMEM(*spread), pltpu.VMEM((rows, half_len), F32)],
        in_specs=[whole()] * 11,
        out_specs=[whole()] * 2,
        scratch_shapes=[vmem((len(MIDDLE) * 2 * rows, 2 * half_len))],
        input_output_aliases={4: 0},
        compiler_params=params(16),
        cost_estimate=pl.CostEstimate(flops=10**9, bytes_accessed=4 * 10**6, transcendentals=0),
        name="middle",
    )
    lifted, norm = middle(six, ten, far, more, *in_vmem(lifted, norm), chosen, *tables)
    result, _ = pl.pallas_call(
        late_kernel,
        out_shape=[pltpu.HBM((1, first_len, second_len), BF16), pltpu.VMEM(*spread)],
        in_specs=[whole()] * 10,
        out_specs=[outside(), whole()],
        scratch_shapes=[
            vmem((len(LATE) * 2 * rows, 2 * half_len)),
            vmem((first_len, second_len)),
            pltpu.SemaphoreType.DMA((second_len // 256,)),
        ],
        input_output_aliases={2: 1},
        compiler_params=params(16),
        name="late",
    )(last, late, *in_vmem(lifted, norm), chosen, *tables, *in_vmem(cols_table))
    return result


def angles(left_idx, right_idx, period):
    product = left_idx[:, None] * right_idx[None, :] % period
    phase_angle = product.astype(jnp.float32) * (2.0 * math.pi / period)
    return (jnp.cos(phase_angle), jnp.sin(phase_angle))


def filtered(white_pair, tmpl_pair, cut_bins, freq_bin):
    white_real = white_pair[0].astype(jnp.float32)
    white_imag = white_pair[1].astype(jnp.float32)
    tmpl_real = tmpl_pair[0].astype(jnp.float32)
    tmpl_imag = tmpl_pair[1].astype(jnp.float32)
    in_band = freq_bin[None] < cut_bins[:, None, None]
    filt_real = jnp.where(in_band, white_real * tmpl_real + white_imag * tmpl_imag, 0.0)
    filt_imag = jnp.where(in_band, white_imag * tmpl_real - white_real * tmpl_imag, 0.0)
    return jnp.concatenate([filt_real, filt_imag], -1).astype(jnp.bfloat16)


def inverse_rows(stacked, row_bins, second_len, length):
    half_len = second_len // 2
    cosine, sine = angles(
        jnp.arange(half_len, dtype=jnp.int32), jnp.arange(second_len, dtype=jnp.int32), second_len
    )
    dft_table = jnp.concatenate(
        [jnp.concatenate([cosine, sine], 1), jnp.concatenate([-sine, cosine], 1)], 0
    ).astype(jnp.bfloat16)
    spread = jnp.einsum("tkf,fg->tkg", stacked, dft_table, preferred_element_type=jnp.float32)
    spread_real = spread[..., :second_len]
    spread_imag = spread[..., second_len:]
    cos_twist, sin_twist = angles(row_bins, jnp.arange(second_len, dtype=jnp.int32), length)
    lift_real = spread_real * cos_twist - spread_imag * sin_twist
    lift_imag = spread_real * sin_twist + spread_imag * cos_twist
    return jnp.concatenate([lift_real, lift_imag], -1).astype(jnp.bfloat16)


def inverse_cols(lifted, first_len, second_len):
    row_idx = jnp.arange(first_len, dtype=jnp.int32)
    cosine, sine = angles(row_idx, row_idx, first_len)
    cosine = cosine.astype(jnp.bfloat16)
    sine = sine.astype(jnp.bfloat16)
    lift_real = lifted[..., :second_len]
    lift_imag = lifted[..., second_len:]
    field_real = jnp.einsum(
        "ak,tkb->tab", cosine, lift_real, preferred_element_type=jnp.float32
    ) - jnp.einsum("ak,tkb->tab", sine, lift_imag, preferred_element_type=jnp.float32)
    field_imag = jnp.einsum(
        "ak,tkb->tab", sine, lift_real, preferred_element_type=jnp.float32
    ) + jnp.einsum("ak,tkb->tab", cosine, lift_imag, preferred_element_type=jnp.float32)
    return (field_real, field_imag)


def plain_local(strain, analysis, bank, cutoff, order):
    highest = lax.Precision.HIGHEST
    dev_count = lax.axis_size("tmpl")
    my_index = lax.axis_index("tmpl")
    seg_count = strain.shape[0]
    first_len = strain.shape[1]
    col_count = strain.shape[2]
    second_len = col_count * dev_count
    length = first_len * second_len
    half_len = second_len // 2
    row_count = first_len // dev_count
    row_idx = jnp.arange(first_len, dtype=jnp.int32)
    col_index = my_index * col_count + jnp.arange(col_count, dtype=jnp.int32)
    sample_idx = row_idx[:, None] * second_len + col_index[None, :]
    window = (
        math.sqrt(8.0 / 3.0) * jnp.sin(sample_idx.astype(jnp.float32) * (math.pi / length)) ** 2
    )
    series = jnp.concatenate([strain * window, analysis[None]], 0)
    cos_one, sin_one = angles(row_idx, row_idx, first_len)
    part_real = jnp.einsum("ka,sab->skb", cos_one, series, precision=highest)
    part_imag = -jnp.einsum("ka,sab->skb", sin_one, series, precision=highest)
    cos_twist, sin_twist = angles(row_idx, col_index, length)
    twist_real = part_real * cos_twist + part_imag * sin_twist
    twist_imag = part_imag * cos_twist - part_real * sin_twist
    moved = lax.all_to_all(
        jnp.stack([twist_real, twist_imag]).astype(jnp.bfloat16),
        "tmpl",
        split_axis=2,
        concat_axis=3,
        tiled=True,
    ).astype(jnp.float32)
    cos_two, sin_two = angles(
        jnp.arange(second_len, dtype=jnp.int32), jnp.arange(half_len, dtype=jnp.int32), second_len
    )
    spec_real = jnp.einsum("skb,bf->skf", moved[0], cos_two, precision=highest) + jnp.einsum(
        "skb,bf->skf", moved[1], sin_two, precision=highest
    )
    spec_imag = jnp.einsum("skb,bf->skf", moved[1], cos_two, precision=highest) - jnp.einsum(
        "skb,bf->skf", moved[0], sin_two, precision=highest
    )
    power_spec = jnp.maximum(
        jnp.mean(spec_real[:seg_count] ** 2 + spec_imag[:seg_count] ** 2, axis=0), 0.2 * length
    )
    whitened = jnp.stack(
        [spec_real[seg_count] / power_spec, spec_imag[seg_count] / power_spec]
    ).astype(jnp.bfloat16)
    own_rows = my_index * row_count + jnp.arange(row_count, dtype=jnp.int32)
    half_idx = jnp.arange(half_len, dtype=jnp.int32)
    freq_local = own_rows[:, None] + first_len * half_idx[None, :]
    chosen = jnp.take(bank, order, axis=1)
    cuts = jnp.take(cutoff, order)
    bank_real = chosen[0].astype(jnp.float32)
    bank_imag = chosen[1].astype(jnp.float32)
    in_band = freq_local[None] < cuts[:, None, None]
    local_norm = jnp.sum(
        jnp.where(in_band, (bank_real**2 + bank_imag**2) / power_spec, 0.0), axis=(1, 2)
    )
    norm_sq = lax.psum(local_norm, "tmpl")
    per_device = cuts.shape[0] // dev_count
    own_norm = lax.dynamic_slice_in_dim(norm_sq, my_index * per_device, per_device)
    stacked = filtered(whitened, chosen, cuts, freq_local)
    lifted = lax.all_to_all(
        inverse_rows(stacked, own_rows, second_len, length),
        "tmpl",
        split_axis=0,
        concat_axis=1,
        tiled=True,
    )
    field_real, field_imag = inverse_cols(lifted, first_len, second_len)
    magnitude = jnp.sqrt(field_real**2 + field_imag**2)
    return (magnitude / jnp.sqrt(own_norm)[:, None, None]).astype(jnp.bfloat16)


def local(strain, analysis, bank, cutoff, order):
    dev_count, segs, cols = lax.axis_size("tmpl"), strain.shape[0], strain.shape[2]
    rows = strain.shape[1] // dev_count // 2
    fits = rows == STEP and cols == 64 and segs % 2 == 0 and dev_count == len(EARLY + MIDDLE + LATE)
    if fits and order.shape[0] == dev_count and lax.axis_size("grp") == 2:
        return tiled_local(strain, analysis, bank, cutoff, order)
    return plain_local(strain, analysis, bank, cutoff, order)


def solution(mesh):
    return jax.shard_map(
        local,
        mesh=mesh,
        in_specs=(P("grp", None, "tmpl"), P("grp", "tmpl"), P(None, None, "tmpl", None), P(), P()),
        out_specs=P(("grp", "tmpl"), None, None),
        check_vma=False,
    )
```

```python
import functools
import math

import jax
import jax.numpy as jnp
import numpy as np
from jax import lax
from jax.experimental import pallas as pl
from jax.experimental.pallas import tpu as pltpu
from jax.sharding import PartitionSpec as P

BF16 = jnp.bfloat16
F32 = jnp.float32
STEP = 16
PIECE = 128
EARLY = (0, 2, 4, 8, 1, 3, 5, 9)
MIDDLE = (6, 10, 12, 7, 11, 13)
LATE = (14, 15)


def turns(product, period):
    angle = (product % period) * (2.0 * math.pi / period)
    return np.cos(angle).astype(np.float32), np.sin(angle).astype(np.float32)


def matmul(left, right):
    return jnp.dot(left, right, preferred_element_type=F32)


def matmul_nt(left, right):
    return lax.dot_general(left, right, (((1,), (1,)), ((), ())), preferred_element_type=F32)


def vmem(shape, dtype=BF16):
    return pltpu.VMEM(shape, dtype)


def whole():
    return pl.BlockSpec(memory_space=pltpu.VMEM)


def outside():
    return pl.BlockSpec(memory_space=pltpu.HBM)


def in_hbm(*arrays):
    return [pltpu.with_memory_space_constraint(jnp.asarray(array), pltpu.HBM) for array in arrays]


def in_vmem(*arrays):
    return [pltpu.with_memory_space_constraint(array, pltpu.VMEM) for array in arrays]


def position():
    return lax.axis_index("tmpl"), lax.axis_index("grp")


def start_copies(pairs, sems):
    copies = [
        pltpu.make_async_copy(source, target, sems.at[at]) for at, (source, target) in enumerate(pairs)
    ]
    for copy in copies:
        copy.start()
    return copies


def params(mib):
    return pltpu.CompilerParams(vmem_limit_bytes=mib << 20)


def turn(cos, sin, by_cos, by_sin):
    return cos * by_cos - sin * by_sin, sin * by_cos + cos * by_sin


def halves(count):
    return np.concatenate([np.arange(0, count, 2), np.arange(1, count, 2)])


def aligned(start, size):
    return pl.ds(pl.multiple_of(start, size), size)


def stage_one_kernel(
    turns_of_eight, order_hbm, strain_hbm, analysis_hbm, spin_hbm, win_hbm, wave_hbm, bank, out,
    order, strain, analysis, spin, win, wave, packed, sems, bank_sem,
):
    segs, cols, first_len = strain.shape
    tail = segs * cols
    templates, half_len = bank.shape[1], bank.shape[3]
    rows = out.shape[0] // templates
    half = first_len // 2
    place, group = position()
    sources = [
        (order_hbm, order),
        (spin_hbm.at[place], spin),
        (win_hbm, win),
        *[(strain_hbm.at[seg], strain.at[seg]) for seg in range(segs)],
        (analysis_hbm, analysis),
        (wave_hbm, wave),
    ]
    copies = start_copies(sources, sems)
    lane = 2 * (tail + cols)
    copies[0].wait()
    bank_pairs = []
    for row in range(templates):
        for part in range(2):
            bank_pairs.append(
                (
                    bank.at[part, order[row], aligned(group * rows, rows), :],
                    out.at[
                        row * rows : (row + 1) * rows,
                        lane + part * half_len : lane + (part + 1) * half_len,
                    ],
                )
            )
    for source, target in bank_pairs:
        pltpu.make_async_copy(source, target, bank_sem).start()
    for copy in copies[1:3]:
        copy.wait()
    scale = 0.5 * math.sqrt(8.0 / 3.0)
    win_c, win_s = turn(win[0], win[1], spin[0:1, :], spin[1:2, :])
    window = jnp.concatenate(
        [scale - (win_c * (scale * by_cos) - win_s * (scale * by_sin)) for by_cos, by_sin in turns_of_eight], 0
    )

    def pack(at, values):
        packed[0, at : at + cols, :] = (values[:, :half] + values[:, half:]).astype(BF16)
        packed[1, at : at + cols, :] = (values[:, :half] - values[:, half:]).astype(BF16)

    for seg in range(segs):
        copies[3 + seg].wait()
        pack(seg * cols, strain[seg] * window)
    copies[3 + segs].wait()
    pack(tail, analysis[...])
    copies[4 + segs].wait()
    both = [matmul_nt(wave[odd], packed[odd]) for odd in range(2)]
    count = out.shape[0] // 2

    def woven(part):
        halves_of = [
            table[part * count : (part + 1) * count].reshape(templates, rows // 2, tail + cols) for table in both
        ]
        return jnp.concatenate(halves_of, 1).reshape(2 * count, tail + cols)

    real, imag = woven(0), woven(1)
    out[:, 0:tail] = real[:, :tail].astype(BF16)
    out[:, tail : 2 * tail] = imag[:, :tail].astype(BF16)
    joined = jnp.concatenate([real[:, tail:], imag[:, tail:]], 1)
    out[:, 2 * tail : lane] = joined.astype(BF16)
    whole_bank = out.at[:, lane:]
    pltpu.make_async_copy(whole_bank, whole_bank, bank_sem).wait()


def forward_kernel(
    fore_c, fore_s, fore_rc, fore_rs, near_c, near_s, base_c, base_s,
    forward, near_out_c, near_out_s,
):
    half_len = fore_c.shape[1]
    quarter = half_len // 2
    place, _ = position()
    first_lane = lax.broadcasted_iota(jnp.int32, fore_c.shape, 1) == 0
    sign = 1.0 - 2.0 * (lax.broadcasted_iota(jnp.int32, fore_c.shape, 0) % 2).astype(F32)

    def fore(step, carry):
        cos, sin = carry
        for part, table in enumerate((cos, jnp.where(first_lane, sign, sin))):
            for odd in range(2):
                lane = slice(odd * quarter, (odd + 1) * quarter)
                to = slice(part * quarter, (part + 1) * quarter)
                forward[odd, aligned(step * STEP, STEP), to] = table[:, lane].astype(BF16)
        return turn(cos, sin, fore_rc[...], fore_rs[...])

    lax.fori_loop(0, forward.shape[1] // STEP, fore, (fore_c[...], fore_s[...]))
    near_out_c[...], near_out_s[...] = turn(near_c[...], near_s[...], base_c[place], base_s[place])


def inverse_tables_kernel(
    even_c, even_s, odd_c, odd_s, rows_rc, rows_rs, even_out, odd_out
):
    half_len = even_c.shape[1]
    quarter = half_len // 2

    def spread(out, cos, sin):
        def body(step, carry):
            cos, sin = carry
            upper = aligned(step * STEP, STEP)
            lower = aligned(quarter + step * STEP, STEP)
            for lane in range(0, half_len, PIECE):
                real, imag = slice(2 * lane, 2 * lane + PIECE), slice(2 * lane + PIECE, 2 * (lane + PIECE))
                cos_at, sin_at = cos[:, lane : lane + PIECE], sin[:, lane : lane + PIECE]
                out[upper, real] = cos_at.astype(BF16)
                out[upper, imag] = sin_at.astype(BF16)
                out[lower, real] = (-sin_at).astype(BF16)
                out[lower, imag] = cos_at.astype(BF16)
            return turn(cos, sin, rows_rc[...], rows_rs[...])

        lax.fori_loop(0, quarter // STEP, body, (cos, sin))

    spread(even_out, even_c[...], even_s[...])
    spread(odd_out, odd_c[...], odd_s[...])


def lift_tables_kernel(
    lift_c, lift_s, lift_rc, lift_rs, mid_c, mid_s, lift_out_c, lift_out_s
):
    per = lift_out_c.shape[0] // 2
    for parity in range(2):

        def lifts(step, carry, parity=parity):
            cos, sin = carry
            at = aligned(parity * per + step * STEP, STEP)
            lift_out_c[at, :] = cos
            lift_out_s[at, :] = sin
            return turn(cos, sin, lift_rc[...], lift_rs[...])

        lax.fori_loop(0, per // STEP, lifts, (lift_c[parity], lift_s[parity]))
    lift_out_c[0:STEP, :] = mid_c[...]
    lift_out_s[0:STEP, :] = mid_s[...]


def column_tables_kernel(rows, cols_c, cols_s, cols_rc, cols_rs, cols_out, rows_out, bins_out):
    first_len = cols_c.shape[1]
    per = first_len // 2

    def columns(step, carry):
        cos, sin = carry
        upper = aligned(step * STEP, STEP)
        lower = aligned(per + step * STEP, STEP)
        for parity in range(2):
            at = slice(parity * per, (parity + 1) * per)
            left = slice(parity * first_len, parity * first_len + per)
            right = slice(parity * first_len + per, (parity + 1) * first_len)
            cols_out[upper, left] = cos[:, at].astype(BF16)
            cols_out[upper, right] = (-sin[:, at]).astype(BF16)
            cols_out[lower, left] = sin[:, at].astype(BF16)
            cols_out[lower, right] = cos[:, at].astype(BF16)
        return turn(cos, sin, cols_rc[...], cols_rs[...])

    lax.fori_loop(0, per // STEP, columns, (cols_c[...], cols_s[...]))
    sort_tables(rows, rows_out, bins_out)


def stage_two_kernel(
    segs, cols, moved, near_c, near_s, mid_c_hbm, mid_s_hbm, forward, out,
    mid_c, mid_s, stacked, middle, product, sems,
):
    place, _ = position()
    _, half_len, _ = forward.shape
    second_len = 2 * half_len
    quarter = half_len // 2
    copies = start_copies([(mid_c_hbm, mid_c), (mid_s_hbm, mid_s)], sems)
    sources, rows, _ = moved.shape
    tail = segs * cols
    all_rows = (segs + 1) * rows
    width = 2 * cols
    low = lax.broadcasted_iota(jnp.int32, (rows, width), 1) < cols
    own_first = place == 0
    packed_row = lax.broadcasted_iota(jnp.int32, (rows, width), 0) == 0
    drop = jnp.logical_and(packed_row, own_first)

    def pair(left, right):
        return (
            jnp.where(low, left, pltpu.roll(right, cols, 1)),
            jnp.where(low, pltpu.roll(left, cols, 1), right),
        )

    middle[...] = jnp.zeros_like(middle)
    tiles = sources // 2
    for tile in range(tiles // 2):
        lane = slice(tile * width, (tile + 1) * width)
        lanes = (lane, slice(half_len + tile * width, half_len + (tile + 1) * width))

        def piece(lo, tile=tile):
            hi = lo + width
            found = []
            for source in (2 * tile, 2 * tile + tiles):
                found.append(
                    pair(moved[source, :, lo:hi].astype(F32), moved[source + 1, :, lo:hi].astype(F32))
                )
            return [(found[0][at], found[1][at]) for at in range(2)]

        def put(seg, real, imag, lane=lane, lanes=lanes):
            turned_real, turned_imag = [], []
            for half in range(2):
                middle[seg : seg + 1, lanes[half]] = imag[half][0:1, :]
                kept = jnp.where(drop, 0.0, imag[half])
                cos, sin = near_c[:, lanes[half]], near_s[:, lanes[half]]
                turned_real.append(real[half] * cos + kept * sin)
                turned_imag.append(kept * cos - real[half] * sin)
            for at, (low_half, high_half) in ((seg * rows, turned_real), (all_rows + seg * rows, turned_imag)):
                stacked[0, at : at + rows, lane] = (low_half + high_half).astype(BF16)
                stacked[1, at : at + rows, lane] = (low_half - high_half).astype(BF16)

        for twin in range(segs // 2):
            real_one, real_two = piece(twin * width)
            imag_one, imag_two = piece(tail + twin * width)
            put(2 * twin, real_one, imag_one)
            put(2 * twin + 1, real_two, imag_two)
        real, imag = piece(2 * tail)
        put(segs, real, imag)
    for copy in copies:
        copy.wait()
    for part, turned in enumerate((middle[...] * mid_c[...], middle[...] * -mid_s[...])):
        at = slice(2 * all_rows + part * rows, 2 * all_rows + (part + 1) * rows)
        stacked[0, at, :] = (turned[:, :half_len] + turned[:, half_len:]).astype(BF16)
        stacked[1, at, :] = (turned[:, :half_len] - turned[:, half_len:]).astype(BF16)

    first_lane = lax.broadcasted_iota(jnp.int32, (rows, quarter), 1) == 0
    swap = jnp.logical_and(lax.broadcasted_iota(jnp.int32, (rows, quarter), 0) == 0, own_first)
    floor = 0.2 * (second_len * 2 * sources * rows)
    upper, lower = [], []
    for odd in range(2):
        cos_at = slice(odd * half_len, odd * half_len + quarter)
        sin_at = slice(odd * half_len + quarter, (odd + 1) * half_len)
        product[:, odd * half_len : (odd + 1) * half_len] = matmul(stacked[odd], forward[odd])

        def parts(at, lower_at, cos_at=cos_at, sin_at=sin_at):
            return (
                product[at : at + rows, cos_at],
                product[at : at + rows, sin_at],
                product[lower_at : lower_at + rows, cos_at],
                product[lower_at : lower_at + rows, sin_at],
            )

        def direct_of(rc, rs, ic, imag_s, odd=odd):
            if not odd:
                rs, imag_s = jnp.where(first_lane, 0.0, rs), jnp.where(first_lane, 0.0, imag_s)
            return rc + imag_s, ic - rs

        def mirror_of(rc, rs, ic, imag_s, odd=odd):
            real, imag = rc - imag_s, ic + rs
            if not odd:
                real, imag = jnp.where(first_lane, rs, real), jnp.where(first_lane, imag_s, imag)
            return real, imag

        level = jnp.zeros((rows, quarter), F32)
        mirror_level = level
        for seg in range(segs):
            four = parts(seg * rows, all_rows + seg * rows)
            real, imag = direct_of(*four)
            level = level + (real * real + imag * imag)
            real, imag = mirror_of(*four)
            mirror_level = mirror_level + (real * real + imag * imag)
        four = parts(segs * rows, all_rows + segs * rows)
        real, imag = direct_of(*four)
        mirror_real, mirror_imag = mirror_of(*four)
        mid_real, mid_imag = mirror_of(*parts(2 * all_rows, 2 * all_rows + rows))
        mid_level = jnp.sum((mid_real * mid_real + mid_imag * mid_imag)[:segs], 0, keepdims=True)
        mirror_level = jnp.where(swap, mid_level, mirror_level)
        mirror_real = jnp.where(swap, mid_real[segs : segs + 1], mirror_real)
        mirror_imag = jnp.where(swap, mid_imag[segs : segs + 1], mirror_imag)
        level = jnp.maximum(level * (1.0 / segs), floor)
        mirror_level = jnp.maximum(mirror_level * (1.0 / segs), floor)
        upper.append((real / level, imag / level, 1.0 / level))
        lower.append((mirror_real / mirror_level, -mirror_imag / mirror_level, 1.0 / mirror_level))
    eighth = rows // 2
    for part in range(3):
        mirrored = (lower[1][part], pltpu.roll(lower[0][part], quarter - 1, 1))
        for odd in range(2):
            lane = slice(part * half_len + odd * quarter, part * half_len + (odd + 1) * quarter)
            for parity in range(2):
                at = slice(parity * eighth, (parity + 1) * eighth)
                block = jnp.concatenate([upper[odd][part][at], mirrored[odd][at]], 0)
                out[parity * rows : (parity + 1) * rows, lane] = block.astype(BF16)


def sort_tables(rows, rows_out, bins_out):
    _, per, _ = rows_out.shape
    _, group = position()

    def one_hot(mask):
        return jnp.where(mask, 1.0, 0.0).astype(BF16)

    at = lax.broadcasted_iota(jnp.int32, (per, per), 0)
    lane = lax.broadcasted_iota(jnp.int32, (per, per), 1)
    for turned in range(2):
        row = packed_row_of(at, turned, 2 * per, rows)
        share = (row // rows) % 2
        source = row // (2 * rows) - turned * (per // (2 * rows))
        column = source * rows + row % rows + jnp.where(share == group, 0, per // 2)
        rows_out[turned] = one_hot(column == lane)
    wide = bins_out.shape[0]
    at = lax.broadcasted_iota(jnp.int32, (wide, wide), 0)
    lane = lax.broadcasted_iota(jnp.int32, (wide, wide), 1)
    bins_out[...] = one_hot(at == jnp.where(lane < wide // 2, 2 * lane, 2 * lane - wide + 1))


def packed_row_of(at, turned, first_len, rows):
    half = first_len // 4
    packed = at % half // (rows // 2) * rows + 2 * (at % (rows // 2)) + at // half
    if not turned:
        return packed
    return jnp.where(packed == 0, first_len // 2, first_len - packed)


def choose_kernel(order, cuts, own, other, by_rows, by_bins, out, held):
    place, _ = position()
    sources, rows, _ = own.shape
    per = sources * rows
    half_len = own.shape[2] // 2
    for source in range(sources):
        turned, at = source // (sources // 2), source % (sources // 2) * rows
        held[turned, at : at + rows, :] = own[source]
        held[turned, per // 2 + at : per // 2 + at + rows, :] = other[source]
    cut = cuts[order[place]]
    moved, room = [], []
    for turned in range(2):
        moved.append(matmul(by_rows[turned], held[turned]).reshape(per // (rows // 2), rows // 2, 2 * half_len))
        at = lax.broadcasted_iota(jnp.int32, (per, 128), 0)
        room.append((cut - packed_row_of(at, turned, 2 * per, rows)).reshape(per // (rows // 2), rows // 2, 128))
    picked = jnp.concatenate(moved, 1).reshape(2 * per, 2 * half_len).astype(BF16)
    room = jnp.concatenate(room, 1).reshape(2 * per, 128)
    wide = by_bins.shape[0]
    for part in range(2):
        for block in range(half_len // wide):
            lane = part * half_len + block * wide
            sorted_bins = matmul(picked[:, lane : lane + wide], by_bins[...])
            for odd in range(2):
                for at in range(0, wide // 2, 128):
                    first = block * (wide // 2) + at
                    bins = 2 * (first + lax.broadcasted_iota(jnp.int32, (1, 128), 1)) + odd
                    from_lane = odd * (wide // 2) + at
                    kept = jnp.where(
                        2 * per * bins < room, sorted_bins[:, from_lane : from_lane + 128], 0.0
                    )
                    to = part * half_len + odd * (half_len // 2) + first
                    out[:, to : to + 128] = kept.astype(BF16)


def filter_blocks(offsets, blocks, chosen, tables, norm, filtered, lifted):
    place, _ = position()
    even_table, odd_table, lift_c, lift_s = tables
    half_len = even_table.shape[0]
    quarter = half_len // 2
    first_len = chosen.shape[0]
    per = first_len // 2
    rows = blocks[0].shape[0] // 2
    groups = []
    for block, offset in zip(blocks, offsets):
        device = jnp.bitwise_xor(place, offset)
        for parity in range(2):
            row = slice(parity * rows, (parity + 1) * rows)
            at = aligned(parity * per + device * rows, rows)
            white_real = block[row, :half_len].astype(F32)
            white_imag = block[row, half_len : 2 * half_len].astype(F32)
            weight = block[row, 2 * half_len :].astype(F32)
            real = chosen[at, :half_len].astype(F32)
            imag = chosen[at, half_len:].astype(F32)
            norm = norm + (real * real + imag * imag) * weight
            filt_real = (white_real * real + white_imag * imag).astype(BF16)
            filt_imag = (white_imag * real - white_real * imag).astype(BF16)
            to = slice(len(groups) * rows, (len(groups) + 1) * rows)
            filtered[to, 0:quarter] = filt_real[:, :quarter]
            filtered[to, quarter:half_len] = filt_imag[:, :quarter]
            filtered[to, half_len : half_len + quarter] = filt_real[:, quarter:]
            filtered[to, half_len + quarter :] = filt_imag[:, quarter:]
            groups.append((to, at, parity * first_len + device * rows))
    for lane in range(0, half_len, PIECE):
        both = slice(2 * lane, 2 * (lane + PIECE))
        even = matmul(filtered[:, :half_len], even_table[:, both])
        odd = matmul(filtered[:, half_len:], odd_table[:, both])
        for upper in range(2):
            lanes = slice(upper * half_len + lane, upper * half_len + lane + PIECE)
            total = even - odd if upper else even + odd
            for row, at, target in groups:
                real, imag = total[row, :PIECE], total[row, PIECE:]
                cos, sin = lift_c[at, lanes], lift_s[at, lanes]
                lifted[aligned(target, rows), lanes] = (real * cos - imag * sin).astype(BF16)
                lifted[aligned(target + per, rows), lanes] = (real * sin + imag * cos).astype(BF16)
    return norm


def early_kernel(near, theirs, chosen, *refs):
    tables, (lifted, norm, filtered) = refs[:4], refs[4:]
    blocks = [*[near.at[at] for at in range(4)], *[theirs.at[at] for at in range(4)]]
    zero = jnp.zeros(norm.shape, F32)
    norm[...] = filter_blocks(EARLY, blocks, chosen, tables, zero, filtered, lifted)


def middle_kernel(six, ten, far, theirs, early, early_norm, chosen, *refs):
    tables, (lifted, norm, filtered) = refs[:4], refs[4:]
    blocks = [six, ten, far, *[theirs.at[at] for at in range(3)]]
    norm[...] = filter_blocks(MIDDLE, blocks, chosen, tables, early_norm[...], filtered, lifted)


def late_kernel(last, theirs, early, early_norm, chosen, *refs):
    tables, (cols_table, out, lifted, filtered, result, sems) = refs[:4], refs[4:]
    norm = filter_blocks(LATE, [last, theirs], chosen, tables, early_norm[...], filtered, lifted)
    scale = lax.rsqrt(jnp.sum(norm, keepdims=True))
    first_len = chosen.shape[0]
    per = first_len // 2
    wide = 256
    lanes = [slice(lane, lane + wide) for lane in range(0, lifted.shape[1], wide)]

    def products(at):
        return (
            matmul(cols_table[:, :first_len], lifted[:first_len, at]),
            matmul(cols_table[:, first_len:], lifted[first_len:, at]),
        )

    copies = []
    following = products(lanes[0])
    for block, at in enumerate(lanes):
        even, odd = following
        if block + 1 < len(lanes):
            following = products(lanes[block + 1])
        for upper in range(2):
            total = even - odd if upper else even + odd
            power = total[:per] * total[:per] + total[per:] * total[per:]
            size = power * lax.rsqrt(jnp.maximum(power, 1e-37))
            row = slice(upper * per, (upper + 1) * per)
            result[row, at] = (size * scale).astype(BF16)
            piece = sems.at[2 * block + upper]
            copies.append(pltpu.make_async_copy(result.at[row, at], out.at[0, row, at], piece))
            copies[-1].start()
    for copy in copies:
        copy.wait()


def swap_with(array, flip):
    pairs = [(at, at ^ flip) for at in range(lax.axis_size("tmpl"))]
    return lax.ppermute(array, "tmpl", pairs)


def tiled_local(strain, analysis, bank, cutoff, order):
    dev_count = lax.axis_size("tmpl")
    segs, first_len, cols = strain.shape
    second_len = cols * dev_count
    length = first_len * second_len
    half_len = second_len // 2
    rows = first_len // dev_count // 2
    templates = order.shape[0]
    lanes = 2 * (segs + 1) * cols

    first, second, half = np.arange(first_len), np.arange(second_len), np.arange(half_len)
    devices, step = np.arange(dev_count), np.arange(STEP)
    near = halves(rows)
    packed = (devices[:, None] * rows + near[None, :]).reshape(dev_count, 2, rows // 2)
    waves = []
    for odd in range(2):
        cos, sin = turns(packed[:, odd].reshape(-1, 1) * first[None, : first_len // 2], first_len)
        if not odd:
            sin[0] = 2 * (first[: first_len // 2] % 2) - 1.0
        waves.append(np.concatenate([cos, -sin]))
    win = np.stack(turns(np.arange(8)[:, None] + second_len * first[None, :], length))
    spin = np.stack(turns(cols * devices, length), 1)[:, :, None] * np.ones((1, 1, first_len), np.float32)
    turns_of_eight = [tuple(float(at) for at in turns(8 * block, length)) for block in range(cols // 8)]

    sent = pl.pallas_call(
        functools.partial(stage_one_kernel, turns_of_eight),
        in_specs=[outside()] * 7,
        out_specs=whole(),
        scratch_shapes=[
            pltpu.SMEM((templates,), jnp.int32),
            vmem((segs, cols, first_len), F32),
            vmem((cols, first_len), F32),
            vmem((2, first_len), F32),
            vmem((2, 8, first_len), F32),
            vmem((2, dev_count * rows, first_len // 2)),
            vmem((2, (segs + 1) * cols, first_len // 2)),
            pltpu.SemaphoreType.DMA((segs + 5,)),
            pltpu.SemaphoreType.DMA,
        ],
        out_shape=pltpu.VMEM((dev_count * rows, lanes + 2 * half_len), BF16),
        compiler_params=params(16),
        name="stage_one",
    )(
        *in_hbm(
            order, jnp.swapaxes(strain, 1, 2), jnp.swapaxes(analysis, 0, 1), spin, win,
            np.stack(waves).astype(BF16), bank,
        ),
    )
    moved = lax.all_to_all(
        sent.reshape(dev_count, rows, lanes + 2 * half_len), "tmpl", split_axis=0, concat_axis=0, tiled=True
    )
    own = moved[:, :, lanes:]
    other = lax.ppermute(own, "grp", [(0, 1), (1, 0)])

    split = halves(half_len)
    low = 2 * np.arange(rows // 2)
    lift_rows = [np.concatenate([low + odd, first_len - low - odd]) for odd in range(2)]
    lift_init = [turns(at[:, None] * second[None, :], length) for at in lift_rows]
    cols_parts = []
    for odd in range(2):
        straight = devices[:, None] * rows + low[None, :] + odd
        turned = np.where(straight == 0, first_len // 2, first_len - straight)
        cols_parts.append(np.concatenate([straight, turned], 1).reshape(-1))
    cols_rows = np.concatenate(cols_parts)
    mid_rows = lift_rows[0].copy()
    mid_rows[rows // 2] = first_len // 2
    step_sign = np.where(np.arange(rows) < rows // 2, rows, -rows)
    fore = [
        *turns(step[:, None] * split[None, :], second_len),
        *turns(STEP * split[None, :], second_len),
        *turns(near[:, None] * second[None, :], length),
        *turns(rows * devices[:, None, None] * second[None, None, :], length),
    ]
    forward, near_c, near_s = pl.pallas_call(
        forward_kernel,
        out_shape=[
            pltpu.VMEM((2, half_len, half_len), BF16),
            *[pltpu.VMEM((rows, second_len), F32)] * 2,
        ],
        in_specs=[whole()] * len(fore),
        out_specs=[whole()] * 3,
        compiler_params=params(16),
        cost_estimate=pl.CostEstimate(flops=10**7, bytes_accessed=2 * 10**7, transcendentals=0),
        name="forward_tables",
    )(*in_hbm(*fore))
    back = [
        *turns(2 * step[:, None] * half[None, :], second_len),
        *turns((2 * step[:, None] + 1) * half[None, :], second_len),
        *turns(2 * STEP * half[None, :], second_len),
    ]
    lifts = [
        np.stack([lift_init[0][0], lift_init[1][0]]),
        np.stack([lift_init[0][1], lift_init[1][1]]),
        *turns(step_sign[:, None] * second[None, :], length),
        *turns(mid_rows[:, None] * second[None, :], length),
    ]
    columns = [
        *turns(step[:, None] * cols_rows[None, :], first_len),
        *turns(STEP * cols_rows[None, :], first_len),
    ]
    shapes = [((half_len, second_len), BF16)] * 2
    lift_shapes = [((first_len, second_len), F32)] * 2
    column_shapes = [
        ((first_len, 2 * first_len), BF16),
        ((2, first_len // 2, first_len // 2), BF16),
        ((256, 256), BF16),
    ]
    inverse_tables = pl.pallas_call(
        inverse_tables_kernel,
        out_shape=[pltpu.VMEM(*shape) for shape in shapes],
        in_specs=[whole()] * len(back),
        out_specs=[whole()] * len(shapes),
        compiler_params=params(8),
        cost_estimate=pl.CostEstimate(flops=10**7, bytes_accessed=2 * 10**7, transcendentals=0),
        name="inverse_tables",
    )
    even_table, odd_table = inverse_tables(*in_hbm(*back))
    lift_tables = pl.pallas_call(
        lift_tables_kernel,
        out_shape=[pltpu.VMEM(*shape) for shape in lift_shapes],
        in_specs=[whole()] * len(lifts),
        out_specs=[whole()] * len(lift_shapes),
        compiler_params=params(8),
        cost_estimate=pl.CostEstimate(flops=10**7, bytes_accessed=10**7, transcendentals=0),
        name="lift_tables",
    )
    lift_c, lift_s = lift_tables(*in_hbm(*lifts))
    column_tables = pl.pallas_call(
        functools.partial(column_tables_kernel, rows),
        out_shape=[pltpu.VMEM(*shape) for shape in column_shapes],
        in_specs=[whole()] * len(columns),
        out_specs=[whole()] * len(column_shapes),
        compiler_params=params(8),
        cost_estimate=pl.CostEstimate(flops=10**7, bytes_accessed=10**7, transcendentals=0),
        name="column_tables",
    )
    cols_table, by_rows, by_bins = column_tables(*in_hbm(*columns))

    mid_c, mid_s = turns(first_len // 2 * second[None, :], length)
    all_rows = 2 * (segs + 2) * rows
    stage_two = pl.pallas_call(
        functools.partial(stage_two_kernel, segs, cols),
        out_shape=jax.ShapeDtypeStruct((2 * rows, 3 * half_len), BF16),
        in_specs=[whole()] * 3 + [outside()] * 2 + [whole()],
        out_specs=whole(),
        scratch_shapes=[
            *[vmem((1, second_len), F32)] * 2,
            vmem((2, all_rows, half_len)),
            vmem((rows, second_len), F32),
            vmem((all_rows, second_len), F32),
            pltpu.SemaphoreType.DMA((2,)),
        ],
        compiler_params=params(24),
        cost_estimate=pl.CostEstimate(flops=10**9, bytes_accessed=4 * 10**6, transcendentals=0),
        name="stage_two",
    )
    block = stage_two(moved, *in_vmem(near_c, near_s), *in_hbm(mid_c, mid_s), *in_vmem(forward))

    two = swap_with(block, 8)
    one = swap_with(block, 4)
    beside = swap_with(block, 2)
    far = swap_with(two, 4)
    ten = swap_with(two, 2)
    six = swap_with(one, 2)
    near = jnp.stack([block, beside, one, two])
    theirs = swap_with(near, 1)
    last_upper = swap_with(far[:rows], 2)
    last_lower = swap_with(ten[rows:], 4)
    last = jnp.concatenate([last_upper, last_lower], 0)
    more = swap_with(jnp.stack([six, ten, far]), 1)
    late_lower = swap_with(last_lower, 1)
    late_upper = swap_with(last_upper, 1)
    late = jnp.concatenate([late_upper, late_lower], 0)

    choose = pl.pallas_call(
        choose_kernel,
        grid_spec=pltpu.PrefetchScalarGridSpec(
            num_scalar_prefetch=2,
            grid=(),
            in_specs=[whole()] * 4,
            out_specs=whole(),
            scratch_shapes=[vmem((2, first_len // 2, 2 * half_len))],
        ),
        out_shape=jax.ShapeDtypeStruct((first_len, 2 * half_len), BF16),
        compiler_params=params(16),
        cost_estimate=pl.CostEstimate(flops=10**9, bytes_accessed=4 * 10**6, transcendentals=0),
        name="choose",
    )
    chosen = choose(order, cutoff, own, other, *in_vmem(by_rows, by_bins))

    spread = [(2 * first_len, second_len), BF16]
    tables = in_vmem(even_table, odd_table, lift_c, lift_s)
    early = pl.pallas_call(
        early_kernel,
        out_shape=[pltpu.VMEM(*spread), pltpu.VMEM((rows, half_len), F32)],
        in_specs=[whole()] * 7,
        out_specs=[whole()] * 2,
        scratch_shapes=[vmem((len(EARLY) * 2 * rows, 2 * half_len))],
        compiler_params=params(16),
        cost_estimate=pl.CostEstimate(flops=10**9, bytes_accessed=4 * 10**6, transcendentals=0),
        name="early",
    )
    lifted, norm = early(near, theirs, chosen, *tables)
    middle = pl.pallas_call(
        middle_kernel,
        out_shape=[pltpu.VMEM(*spread), pltpu.VMEM((rows, half_len), F32)],
        in_specs=[whole()] * 11,
        out_specs=[whole()] * 2,
        scratch_shapes=[vmem((len(MIDDLE) * 2 * rows, 2 * half_len))],
        input_output_aliases={4: 0},
        compiler_params=params(16),
        cost_estimate=pl.CostEstimate(flops=10**9, bytes_accessed=4 * 10**6, transcendentals=0),
        name="middle",
    )
    lifted, norm = middle(six, ten, far, more, *in_vmem(lifted, norm), chosen, *tables)
    result, _ = pl.pallas_call(
        late_kernel,
        out_shape=[pltpu.HBM((1, first_len, second_len), BF16), pltpu.VMEM(*spread)],
        in_specs=[whole()] * 10,
        out_specs=[outside(), whole()],
        scratch_shapes=[
            vmem((len(LATE) * 2 * rows, 2 * half_len)),
            vmem((first_len, second_len)),
            pltpu.SemaphoreType.DMA((second_len // 128,)),
        ],
        input_output_aliases={2: 1},
        compiler_params=params(16),
        name="late",
    )(last, late, *in_vmem(lifted, norm), chosen, *tables, *in_vmem(cols_table))
    return result


def angles(left_idx, right_idx, period):
    product = left_idx[:, None] * right_idx[None, :] % period
    phase_angle = product.astype(jnp.float32) * (2.0 * math.pi / period)
    return (jnp.cos(phase_angle), jnp.sin(phase_angle))


def filtered(white_pair, tmpl_pair, cut_bins, freq_bin):
    white_real = white_pair[0].astype(jnp.float32)
    white_imag = white_pair[1].astype(jnp.float32)
    tmpl_real = tmpl_pair[0].astype(jnp.float32)
    tmpl_imag = tmpl_pair[1].astype(jnp.float32)
    in_band = freq_bin[None] < cut_bins[:, None, None]
    filt_real = jnp.where(in_band, white_real * tmpl_real + white_imag * tmpl_imag, 0.0)
    filt_imag = jnp.where(in_band, white_imag * tmpl_real - white_real * tmpl_imag, 0.0)
    return jnp.concatenate([filt_real, filt_imag], -1).astype(jnp.bfloat16)


def inverse_rows(stacked, row_bins, second_len, length):
    half_len = second_len // 2
    cosine, sine = angles(
        jnp.arange(half_len, dtype=jnp.int32), jnp.arange(second_len, dtype=jnp.int32), second_len
    )
    dft_table = jnp.concatenate(
        [jnp.concatenate([cosine, sine], 1), jnp.concatenate([-sine, cosine], 1)], 0
    ).astype(jnp.bfloat16)
    spread = jnp.einsum("tkf,fg->tkg", stacked, dft_table, preferred_element_type=jnp.float32)
    spread_real = spread[..., :second_len]
    spread_imag = spread[..., second_len:]
    cos_twist, sin_twist = angles(row_bins, jnp.arange(second_len, dtype=jnp.int32), length)
    lift_real = spread_real * cos_twist - spread_imag * sin_twist
    lift_imag = spread_real * sin_twist + spread_imag * cos_twist
    return jnp.concatenate([lift_real, lift_imag], -1).astype(jnp.bfloat16)


def inverse_cols(lifted, first_len, second_len):
    row_idx = jnp.arange(first_len, dtype=jnp.int32)
    cosine, sine = angles(row_idx, row_idx, first_len)
    cosine = cosine.astype(jnp.bfloat16)
    sine = sine.astype(jnp.bfloat16)
    lift_real = lifted[..., :second_len]
    lift_imag = lifted[..., second_len:]
    field_real = jnp.einsum(
        "ak,tkb->tab", cosine, lift_real, preferred_element_type=jnp.float32
    ) - jnp.einsum("ak,tkb->tab", sine, lift_imag, preferred_element_type=jnp.float32)
    field_imag = jnp.einsum(
        "ak,tkb->tab", sine, lift_real, preferred_element_type=jnp.float32
    ) + jnp.einsum("ak,tkb->tab", cosine, lift_imag, preferred_element_type=jnp.float32)
    return (field_real, field_imag)


def plain_local(strain, analysis, bank, cutoff, order):
    highest = lax.Precision.HIGHEST
    dev_count = lax.axis_size("tmpl")
    my_index = lax.axis_index("tmpl")
    seg_count = strain.shape[0]
    first_len = strain.shape[1]
    col_count = strain.shape[2]
    second_len = col_count * dev_count
    length = first_len * second_len
    half_len = second_len // 2
    row_count = first_len // dev_count
    row_idx = jnp.arange(first_len, dtype=jnp.int32)
    col_index = my_index * col_count + jnp.arange(col_count, dtype=jnp.int32)
    sample_idx = row_idx[:, None] * second_len + col_index[None, :]
    window = (
        math.sqrt(8.0 / 3.0) * jnp.sin(sample_idx.astype(jnp.float32) * (math.pi / length)) ** 2
    )
    series = jnp.concatenate([strain * window, analysis[None]], 0)
    cos_one, sin_one = angles(row_idx, row_idx, first_len)
    part_real = jnp.einsum("ka,sab->skb", cos_one, series, precision=highest)
    part_imag = -jnp.einsum("ka,sab->skb", sin_one, series, precision=highest)
    cos_twist, sin_twist = angles(row_idx, col_index, length)
    twist_real = part_real * cos_twist + part_imag * sin_twist
    twist_imag = part_imag * cos_twist - part_real * sin_twist
    moved = lax.all_to_all(
        jnp.stack([twist_real, twist_imag]).astype(jnp.bfloat16),
        "tmpl",
        split_axis=2,
        concat_axis=3,
        tiled=True,
    ).astype(jnp.float32)
    cos_two, sin_two = angles(
        jnp.arange(second_len, dtype=jnp.int32), jnp.arange(half_len, dtype=jnp.int32), second_len
    )
    spec_real = jnp.einsum("skb,bf->skf", moved[0], cos_two, precision=highest) + jnp.einsum(
        "skb,bf->skf", moved[1], sin_two, precision=highest
    )
    spec_imag = jnp.einsum("skb,bf->skf", moved[1], cos_two, precision=highest) - jnp.einsum(
        "skb,bf->skf", moved[0], sin_two, precision=highest
    )
    power_spec = jnp.maximum(
        jnp.mean(spec_real[:seg_count] ** 2 + spec_imag[:seg_count] ** 2, axis=0), 0.2 * length
    )
    whitened = jnp.stack(
        [spec_real[seg_count] / power_spec, spec_imag[seg_count] / power_spec]
    ).astype(jnp.bfloat16)
    own_rows = my_index * row_count + jnp.arange(row_count, dtype=jnp.int32)
    half_idx = jnp.arange(half_len, dtype=jnp.int32)
    freq_local = own_rows[:, None] + first_len * half_idx[None, :]
    chosen = jnp.take(bank, order, axis=1)
    cuts = jnp.take(cutoff, order)
    bank_real = chosen[0].astype(jnp.float32)
    bank_imag = chosen[1].astype(jnp.float32)
    in_band = freq_local[None] < cuts[:, None, None]
    local_norm = jnp.sum(
        jnp.where(in_band, (bank_real**2 + bank_imag**2) / power_spec, 0.0), axis=(1, 2)
    )
    norm_sq = lax.psum(local_norm, "tmpl")
    per_device = cuts.shape[0] // dev_count
    own_norm = lax.dynamic_slice_in_dim(norm_sq, my_index * per_device, per_device)
    stacked = filtered(whitened, chosen, cuts, freq_local)
    lifted = lax.all_to_all(
        inverse_rows(stacked, own_rows, second_len, length),
        "tmpl",
        split_axis=0,
        concat_axis=1,
        tiled=True,
    )
    field_real, field_imag = inverse_cols(lifted, first_len, second_len)
    magnitude = jnp.sqrt(field_real**2 + field_imag**2)
    return (magnitude / jnp.sqrt(own_norm)[:, None, None]).astype(jnp.bfloat16)


def local(strain, analysis, bank, cutoff, order):
    dev_count, segs, cols = lax.axis_size("tmpl"), strain.shape[0], strain.shape[2]
    rows = strain.shape[1] // dev_count // 2
    fits = rows == STEP and cols == 64 and segs % 2 == 0 and dev_count == len(EARLY + MIDDLE + LATE)
    if fits and order.shape[0] == dev_count and lax.axis_size("grp") == 2:
        return tiled_local(strain, analysis, bank, cutoff, order)
    return plain_local(strain, analysis, bank, cutoff, order)


def solution(mesh):
    return jax.shard_map(
        local,
        mesh=mesh,
        in_specs=(P("grp", None, "tmpl"), P("grp", "tmpl"), P(None, None, "tmpl", None), P(), P()),
        out_specs=P(("grp", "tmpl"), None, None),
        check_vma=False,
    )
```
